32 devices in a mesh: dp: 8 (over y, x, core), mp: 4 (over z).
Axes of the slice: x: 2, y: 2, z: 4, core: 2. Of those that a mesh axis runs over, the one named last changes fastest.
Arguments:
- stream: float32 [768, 16384], P('mp', 'dp'), may hold values from -17 to 17
- segment_ids: int32 [8, 2048], P('dp'), may hold values from 0 to 3, as said below
- cotangent: float32 [768, 16384], P('mp', 'dp'), may hold values from -6 to 6
- ln1_gain: float32 [768], P('mp'), may hold values from 0.25 to 1.75
- qkv_weight: bfloat16 [3, 768, 768], P(None, 'mp'), may hold values from -0.21875 to 0.21875
- qv_bias: float32 [2, 768], P(None, 'mp'), may hold values from -3 to 3
- out_weight: bfloat16 [768, 768], P('mp'), may hold values from -1.75 to 1.75
- out_bias: float32 [768], replicated, may hold values from -3 to 3
- ln2_gain: float32 [768], P('mp'), may hold values from 0.25 to 1.75
- up_weight: bfloat16 [768, 3072], P(None, 'mp'), may hold values from -0.21875 to 0.21875
- up_bias: float32 [3072], P('mp'), may hold values from -3 to 3
- down_weight: bfloat16 [3072, 768], P('mp'), may hold values from -0.109375 to 0.109375
- down_bias: float32 [768], replicated, may hold values from -3 to 3
Outputs:
- mixed: float32 [768, 16384], P('mp', 'dp')
- stream_grad: float32 [768, 16384], P('mp', 'dp')
- ln1_grad: float32 [768], P('mp')
- qkv_grad: float32 [3, 768, 768], P(None, 'mp')
- qv_bias_grad: float32 [2, 768], P(None, 'mp')
- out_grad: float32 [768, 768], P('mp')
- out_bias_grad: float32 [768], replicated
- ln2_grad: float32 [768], P('mp')
- up_grad: float32 [768, 3072], P(None, 'mp')
- up_bias_grad: float32 [3072], P('mp')
- down_grad: float32 [3072, 768], P('mp')
- down_bias_grad: float32 [768], replicated
The draws below stay inside these ranges and needn't reach their ends.
Inputs may be any that keep to these rules, and one draw needn't show every extreme that they name: `segment_ids`: half of the dp rows, which ones drawn from the seed, hold one sequence of 16384 // 8 tokens (all ids 0); the others hold 4 sequences of 512 tokens each, numbered in order.
All inputs are finite; a program needn't handle non-finite values.
Results may differ from the reference program's by a relative error of at most 0.012.
Values may be sent and summed in bfloat16 or wider, within the bound.
A program may use at most 192 MiB of HBM per device.

```python
import jax
import jax.numpy as jnp
from jax import lax

D = 768
H = 12
HD = 64
FF = 3072
TOK_DEV = 2048
QB = 512
SEGS = 4
TOKENS = 16384
N_DP = 8


def draw_stream(key, part):
    first_key, second_key = jax.random.split(jax.random.fold_in(key, 11), 2)
    columns = jnp.arange(D, dtype=jnp.float32) / D
    column_scale = 0.5 * jnp.exp(jnp.log(4.0) * columns)
    row_scale = jnp.exp(jax.random.uniform(second_key, (TOKENS, 1), minval=-0.7, maxval=0.7))
    base = jax.random.normal(first_key, (TOKENS, D))
    base = jnp.clip(base, -4.0, 4.0)
    return (base * column_scale[None, :] * row_scale).T.astype(jnp.float32)


def draw_segment_ids(key, part):
    order = jax.random.permutation(jax.random.fold_in(key, 23), N_DP)
    long_rows = order < N_DP // 2
    short_ids = jnp.arange(TOK_DEV, dtype=jnp.int32) // (TOK_DEV // SEGS)
    zero_ids = jnp.zeros((TOK_DEV,), jnp.int32)
    return jnp.where(long_rows[:, None], zero_ids[None, :], short_ids[None, :]).astype(jnp.int32)


def block_scale(own_key, extent, cuts, smallest, largest):
    level = 1.0
    for axis_at, blocks in cuts:
        draws = jax.random.uniform(jax.random.fold_in(jax.random.fold_in(own_key, 6), axis_at), (blocks,), jnp.float32, smallest / len(cuts), largest / len(cuts))
        level = level * jnp.repeat(jnp.exp(draws), extent[axis_at] // blocks).reshape((-1,) + (1,) * (len(extent) - 1 - axis_at))
    return level


def gaussian(own_key, dims, scale, most, shards=(), held_as=jnp.bfloat16):
    drawn = jax.random.normal(own_key, dims, jnp.float32) * scale
    if len(shards) > 0:
        drawn = block_scale(own_key, dims, shards, -0.22, 0.18) * drawn
    return jnp.clip(drawn, min=-most, max=most).astype(held_as)


def setup_inputs(seed: int = 0) -> dict:
    splits = jax.random.split(jax.random.key(seed), 14)
    return {
        "stream": draw_stream(jax.random.fold_in(splits[13], 71), 0),
        "segment_ids": draw_segment_ids(jax.random.fold_in(splits[13], 71), 0),
        "cotangent": gaussian(splits[2], (D, TOKENS), 1.0, 6.0, ((0, 4), (1, 8)), jnp.float32),
        "ln1_gain": jnp.clip(1.0 + 0.15 * jax.random.normal(splits[3], (D,), jnp.float32), 0.25, 1.75),
        "qkv_weight": gaussian(splits[4], (3, D, D), D ** -0.5, 0.21875, ((1, 4),)),
        "qv_bias": gaussian(splits[5], (2, D), 0.5, 3.0, ((1, 4),), jnp.float32),
        "out_weight": gaussian(splits[6], (D, D), (D // 64) ** -0.5, 1.75, ((0, 4),)),
        "out_bias": gaussian(splits[7], (D,), 0.5, 3.0, (), jnp.float32),
        "ln2_gain": jnp.clip(1.0 + 0.15 * jax.random.normal(splits[8], (D,), jnp.float32), 0.25, 1.75),
        "up_weight": gaussian(splits[9], (D, FF), D ** -0.5, 0.21875, ((1, 4),)),
        "up_bias": gaussian(splits[10], (FF,), 0.5, 3.0, ((0, 4),), jnp.float32),
        "down_weight": gaussian(splits[11], (FF, D), FF ** -0.5, 0.109375, ((0, 4),)),
        "down_bias": gaussian(splits[12], (D,), 0.5, 3.0, (), jnp.float32),
    }


EPS = 1e-05
NEG = -1e+30
HIGH = lax.Precision.HIGHEST

@jax.custom_vjp
def low(v):
    return lax.optimization_barrier(v.astype(jnp.bfloat16)).astype(jnp.float32)

@jax.custom_vjp
def low_back(v):
    return v

def low_keep(v):
    return (low(v), None)

def low_pass(kept, grad):
    return (grad,)

def back_keep(v):
    return (v, None)

def back_low(kept, grad):
    return (low(grad),)
low.defvjp(low_keep, low_pass)
low_back.defvjp(back_keep, back_low)

def crms(values_in, gain):
    stream_width = values_in.shape[1]
    row_sum = lax.optimization_barrier(jnp.sum(values_in, axis=1, keepdims=True))
    square_sum = lax.optimization_barrier(jnp.sum(values_in * values_in, axis=1, keepdims=True))
    inverse = lax.rsqrt((square_sum + row_sum * row_sum) / stream_width + EPS)
    final = (jnp.arange(stream_width) == stream_width - 1)[None, :]
    recovered = jnp.where(final, -row_sum, values_in)
    return recovered * inverse * gain

def attend(queries, keys_in, values_in, segments):
    token_count = queries.shape[0]
    query_blocks = queries.reshape(token_count // QB, QB, H, HD)
    key_heads = keys_in.reshape(token_count, H, HD)
    value_heads = values_in.reshape(token_count, H, HD)
    positions = jnp.arange(token_count, dtype=jnp.int32)

    def one_block(packed):
        query_rows, segment_rows, position_rows = packed
        scores = jnp.einsum('qhe,khe->hqk', query_rows, key_heads, precision=HIGH) * HD ** (-0.5)
        allowed = (segment_rows[:, None] == segments[None, :]) & (positions[None, :] <= position_rows[:, None])
        scores = low_back(jnp.where(allowed[None], scores, NEG))
        row_max = lax.optimization_barrier(jnp.max(scores, axis=-1, keepdims=True))
        expo = jnp.exp(scores - row_max)
        probs = expo / lax.optimization_barrier(jnp.sum(expo, axis=-1, keepdims=True))
        return jnp.einsum('hqk,khe->qhe', low(probs), value_heads, precision=HIGH).reshape(QB, H * HD)
    context = lax.map(jax.checkpoint(one_block), (query_blocks, segments.reshape(-1, QB), positions.reshape(-1, QB)))
    return context.reshape(token_count, H * HD)

def branch_tail(projected, keep_mask):
    projected = low_back(projected)
    centred = low_back(projected - lax.optimization_barrier(jnp.mean(projected, axis=1, keepdims=True)))
    return jnp.where(keep_mask, centred, 0.0)

def forward(stream_in, segments, weights):
    ln_one, joined_w, qv_b, out_w, out_b, ln_two, up_w, up_b, down_w, down_b = weights
    stream_width = stream_in.shape[1]
    keep_mask = (jnp.arange(stream_width) != stream_width - 1)[None, :]
    masked = jnp.where(keep_mask, stream_in, 0.0)
    normed_one = low(crms(masked, ln_one))
    joined = jnp.einsum('td,kcd->tkc', normed_one, joined_w, precision=HIGH)
    queries = low(low_back(joined[:, 0] + qv_b[0]))
    keys_in = low(low_back(joined[:, 1]))
    values_in = low(low_back(joined[:, 2] + qv_b[1]))
    context = low(low_back(attend(queries, keys_in, values_in, segments)))
    middle = masked + branch_tail(jnp.dot(context, out_w, precision=HIGH) + out_b, keep_mask)
    normed_two = low(crms(middle, ln_two))
    pre_act = low_back(jnp.dot(normed_two, up_w, precision=HIGH) + up_b)
    hidden = low(jax.nn.gelu(pre_act, approximate=True))
    return middle + branch_tail(jnp.dot(hidden, down_w, precision=HIGH) + down_b, keep_mask)

def reference(stream, segment_ids, cotangent, ln1_gain, qkv_weight, qv_bias, out_weight, out_bias, ln2_gain, up_weight, up_bias, down_weight, down_bias):
    params = tuple((weight_arr.astype(jnp.float32) for weight_arr in (ln1_gain, qkv_weight, qv_bias, out_weight, out_bias, ln2_gain, up_weight, up_bias, down_weight, down_bias)))
    stream_rows = stream.T.reshape(N_DP, TOK_DEV, D)
    cot_rows = cotangent.T.reshape(N_DP, TOK_DEV, D)

    def one_row(totals, packed):
        row_stream, row_segments, row_cot = packed

        def local(row_in, *weights):
            return forward(row_in, row_segments, weights)
        result, pullback = jax.vjp(local, row_stream, *params)
        grads = pullback(row_cot)
        totals = tuple((older + newer for older, newer in zip(totals, grads[1:])))
        return (totals, (result, grads[0]))
    zeros = tuple((jnp.zeros_like(weight_arr) for weight_arr in params))
    totals, (mixed, stream_grad) = lax.scan(one_row, zeros, (stream_rows, segment_ids, cot_rows))
    return (mixed.reshape(TOKENS, D).T, stream_grad.reshape(TOKENS, D).T, totals[0], totals[1], totals[2], totals[3], totals[4], totals[5], totals[6], totals[7], totals[8], totals[9])
```

```python
import functools

import jax
import jax.numpy as jnp
from jax import lax
from jax.experimental import pallas as pl
from jax.experimental.pallas import tpu as pltpu
from jax.sharding import Mesh, PartitionSpec as P

HD = 64
QB = 512
GROUP = 4
EPS = 1e-05
NEG = -1e30
MESH = pl.DeviceIdType.MESH
BF = jnp.bfloat16
F32 = jnp.float32
ALL = ("blk", "do", "di", "mp")
ROWS = ("blk", "do", "di")


def places():
    return lax.axis_index("do"), lax.axis_index("di"), lax.axis_index("mp")


def holder(row, quarter):
    return lax.rem(quarter, 2), 2 * row + quarter // 2


def dev(do, di, mp):
    return (lax.axis_index("blk"), do, di, mp)


def flip(index, bit):
    return index + bit * (1 - 2 * lax.rem(index // bit, 2))


def remote(source, target, send, recv, device):
    return pltpu.make_async_remote_copy(
        source, target, send, recv, device_id=device, device_id_type=MESH
    )


def greet(others):
    barrier = pltpu.get_barrier_semaphore()
    for other in others:
        pl.semaphore_signal(barrier, inc=1, device_id=other, device_id_type=MESH)
    pl.semaphore_wait(barrier, len(others))


def neighbours(do, di, mp):
    column = [
        dev(do, lax.rem(di + a, 2), lax.rem(mp + b, GROUP))
        for a in range(2)
        for b in range(GROUP)
        if a or b
    ]
    return column + [dev(flip(do, 1), di, mp), dev(flip(do, 2), di, mp)]


def send_block(source, target, send, recv, place, target_place, do):
    (di, mp), (tdi, tmp) = place, target_place
    other = jnp.logical_or(tdi != di, tmp != mp)

    @pl.when(other)
    def _():
        remote(source, target, send, recv, dev(do, tdi, tmp)).start()

    @pl.when(jnp.logical_not(other))
    def _():
        pltpu.make_async_copy(source, target, recv).start()


def sent_block(source, target, send, recv, place, target_place, do):
    (di, mp), (tdi, tmp) = place, target_place
    other = jnp.logical_or(tdi != di, tmp != mp)

    @pl.when(other)
    def _():
        remote(source, target, send, recv, dev(do, tdi, tmp)).wait_send()


def piece_of(ref, do, di):
    rows, lanes = ref.shape[0] // GROUP, ref.shape[1] // 2
    return ref.at[
        pl.ds(pl.multiple_of(do * rows, rows), rows), pl.ds(pl.multiple_of(di * lanes, lanes), lanes)
    ]


def pieces_of(weight):
    return weight.reshape(GROUP, 2, weight.shape[0] // (2 * GROUP), weight.shape[1])


def dot_nt(left, right):
    return lax.dot_general(left, right, (((1,), (1,)), ((), ())), preferred_element_type=F32)


def dot_tn(left, right):
    return lax.dot_general(left, right, (((0,), (0,)), ((), ())), preferred_element_type=F32)


def add_pairs(count, target, first, second):
    def step(i, carry):
        ref = target(i)
        ref[...] = (first(i)[...].astype(F32) + second(i)[...].astype(F32)).astype(ref.dtype)
        return carry

    lax.fori_loop(0, count, step, 0)


def backward_kernel(
    gctx_ref, delta_ref, x_ref, gn2_ref, heads_ref, rest_ref, qkv_ref, lse_ref, normed_ref,
    smalls_ref, headw_ref, segs_ref, stat_ref, sums_ref, dup_ref, oup_ref, ddown_ref, odown_ref, dout_ref,
    m_ref, s_ref, qkvg_ref, small_out, up_out, down_out, out_out,
    gall, k_tok, v_tok, causal, acc_k, acc_v, gj, acc_w, acc_b, gain_wide, acc_gain,
    part, near, total, far_buf, s_blocks,
    core_out, mine_up, mine_down, mine_out,
    one_up, one_down, one_out, two_up, two_down, two_out, z_up, z_down, z_out,
    fin_up, fin_down, fin_out, gq, q_one, q_two, q_z, q_fin, small_a, small_b, small_z,
    own_sem, b_send, b_recv, r_send, r_recv, send, recv,
):
    do, di, mp = places()
    width, tokens = x_ref.shape
    columns = heads_ref.shape[1]
    heads = columns // HD
    row, quarter, half = mp // 2, own_quarter(di, mp), lax.rem(mp, 2)
    place = (di, mp)
    sibling, across = dev(do, 1 - di, mp), dev(do, di, flip(mp, 1))
    posted, pending = [], []

    def prepare(source, target, device):
        n = len(posted)
        copy = remote(source, target, send.at[n], recv.at[n], device)
        posted.append(copy)
        pending.append(copy)
        return copy

    def post(source, target, device):
        copy = prepare(source, target, device)
        copy.start()
        return copy

    def finish(copy):
        copy.wait()
        pending[:] = [other for other in pending if other is not copy]

    def arrived(copies):
        for copy in copies:
            copy.wait_recv()

    def column(bit):
        return dev(flip(do, bit), di, mp)

    grads = (
        (dup_ref, mine_up, oup_ref, one_up, two_up, z_up, fin_up, up_out, 1, 2),
        (ddown_ref, mine_down, odown_ref, one_down, two_down, z_down, fin_down, down_out, 2, 1),
        (dout_ref, mine_out, core_out, one_out, two_out, z_out, fin_out, out_out, 1, 2),
    )
    own = []
    for i, g in enumerate(grads[:2]):
        for n, piece in enumerate((do, flip(do, g[9]))):
            own.append(pltpu.make_async_copy(g[0].at[piece], g[1].at[piece], own_sem.at[4 + 2 * i + n]))
        own.append(pltpu.make_async_copy(g[2], g[3], own_sem.at[8 + i]))
    own.append(pltpu.make_async_copy(dout_ref.at[:, di], mine_out, own_sem.at[2]))
    for copy in own:
        copy.start()
    greet(neighbours(do, di, mp))

    swaps = []
    for k in range(GROUP):
        swaps.append(
            (
                gctx_ref.at[k], gall.at[quarter], b_send.at[k], b_recv.at[quarter], place,
                holder(row, k), do,
            )
        )
        send_block(*swaps[k])
    stage_core = [post(dout_ref.at[:, 1 - di], core_out, sibling)]

    def turn(step, carry):
        h, kb = step // GROUP, lax.rem(step, GROUP)
        rows = pl.ds(pl.multiple_of(columns + h * HD, HD), HD)
        k_tok[h, kb] = qkv_ref[kb, rows].T
        rows = pl.ds(pl.multiple_of(2 * columns + h * HD, HD), HD)
        v_tok[h, kb] = qkv_ref[kb, rows].T
        return carry

    lax.fori_loop(0, heads * GROUP, turn, 0)
    causal[...] = jnp.where(
        lax.broadcasted_iota(jnp.int32, causal.shape, 0)
        <= lax.broadcasted_iota(jnp.int32, causal.shape, 1),
        0.0, NEG,
    )
    for j in range(GROUP):
        turned = smalls_ref[j].T[:columns, 0:1]
        gain_wide[j * columns : (j + 1) * columns] = jnp.broadcast_to(turned, (columns, 128))
    acc_b[...] = jnp.zeros_like(acc_b)
    acc_w[...] = jnp.zeros_like(acc_w)
    segments = segs_ref[row]
    head_weight = headw_ref[...].reshape(3 * columns, width)
    def back_block(block):
        seg_q = segments[:, block * tokens : (block + 1) * tokens]
        masks = [
            jnp.where(segments[:, kb * tokens : kb * tokens + 1] == seg_q, 0.0, NEG)
            for kb in range(block)
        ]

        def one_head(h, carry):
            rows = pl.ds(pl.multiple_of(h * HD, HD), HD)
            k_rows = pl.ds(pl.multiple_of(columns + h * HD, HD), HD)
            query = qkv_ref[block, rows] * HD ** (-0.5)
            grad = gall[block, rows]
            mixed = heads_ref[block, rows].astype(F32) + rest_ref[block, rows].astype(F32)
            weighted = jnp.sum(grad.astype(F32) * mixed, axis=0, keepdims=True)
            lse = lse_ref[h, block, 0:1]
            grad_query = jnp.zeros((HD, tokens), F32)
            for kb in range(block + 1):
                raw = jnp.dot(k_tok[h, kb], query, preferred_element_type=F32)
                raw = raw + (causal[...] if kb == block else masks[kb])
                probs = jnp.exp(raw - lse)
                grad_probs = jnp.dot(v_tok[h, kb], grad, preferred_element_type=F32)
                grad_scores = (probs * (grad_probs - weighted)).astype(BF)
                grad_query += jnp.dot(qkv_ref[kb, k_rows], grad_scores, preferred_element_type=F32)
                key_term = dot_nt(query, grad_scores)
                value_term = dot_nt(grad, probs.astype(BF))
                if block == GROUP - 1:
                    acc_k[kb, rows] = key_term
                    acc_v[kb, rows] = value_term
                else:
                    acc_k[kb, rows] += key_term
                    acc_v[kb, rows] += value_term
            gj[rows] = (grad_query * HD ** (-0.5)).astype(BF)
            return carry

        lax.fori_loop(0, heads, one_head, 0)
        gj[columns : 2 * columns] = acc_k[block].astype(BF)
        gj[2 * columns :] = acc_v[block].astype(BF)
        part[block] = dot_tn(head_weight, gj[...])

    def near_args(i):
        return part.at[i], near.at[i // 2], r_send.at[i], r_recv.at[i], sibling

    def far_args(i):
        return total, far_buf, r_send.at[GROUP + i], r_recv.at[GROUP + i], across

    def to_sibling(i):
        @pl.when(di != i % 2)
        def _():
            remote(*near_args(i)).start()

    def across_row(i):
        @pl.when(di == i % 2)
        def _():
            remote(*near_args(i)).wait_recv()
            at = lambda k: pl.ds(pl.multiple_of(k * columns, columns), columns)
            add_pairs(
                GROUP,
                lambda k: near.at[i // 2, at(k)],
                lambda k: near.at[i // 2, at(k)],
                lambda k: part.at[i, at(k)],
            )

            @pl.when(half != i // 2)
            def _():
                total[...] = near[i // 2].astype(BF)
                remote(*far_args(i)).start()

    def weight_terms(block):
        acc_w[...] += dot_nt(gj[...], normed_ref[block])
        terms = gj[...].astype(F32)
        for k in range(tokens // 128):
            acc_b[: 3 * columns] += terms[:, k * 128 : (k + 1) * 128]

    def stage_one():
        arrived(stage_core)
        own[-1].wait()
        g = grads[2]
        add_pairs(
            GROUP * GROUP,
            lambda n: mine_out.at[n // GROUP, lax.rem(n, GROUP)],
            lambda n: mine_out.at[n // GROUP, lax.rem(n, GROUP)],
            lambda n: core_out.at[n // GROUP, lax.rem(n, GROUP)],
        )
        pieces = (flip(do, g[8]), flip(flip(do, g[8]), g[9]))
        return [post(mine_out.at[p], one_out.at[n], column(g[8])) for n, p in enumerate(pieces)]

    def stage_two(chosen):
        later = []
        for g in chosen:
            mine, one, first, second = g[1], g[3], g[8], g[9]
            for n, piece in ((1, flip(do, second)), (0, do)):
                add_pairs(
                    mine.shape[1], lambda k: mine.at[piece, k], lambda k: mine.at[piece, k],
                    lambda k: one.at[n, k],
                )
                if n == 1:
                    later.append(post(mine.at[piece], g[4], column(second)))
        return later

    def stage_three(copies, chosen):
        arrived(copies)
        later = []
        for g in chosen:
            mine, two, z_buf = g[1], g[4], g[5]
            add_pairs(
                mine.shape[1], lambda k: mine.at[do, k], lambda k: mine.at[do, k],
                lambda k: two.at[k],
            )
            for r in range(1, GROUP):
                later.append(
                    post(mine.at[do, r], z_buf.at[r - 1], dev(do, di, lax.rem(mp + r, GROUP)))
                )
        return later

    def stage_four(copies):
        arrived(copies)
        later = []
        for i, g in enumerate(grads):
            mine, z_buf, fin = g[1], g[5], g[6]
            fin[...] = (
                mine[do, 0].astype(F32) + z_buf[0].astype(F32)
                + z_buf[1].astype(F32) + z_buf[2].astype(F32)
            )
            pltpu.make_async_copy(fin, g[7].at[do, di], own_sem.at[i]).start()
            later.append(post(fin, g[7].at[do, di], column(g[8])))
        return later

    def stage_five(copies):
        arrived(copies)
        later = []
        for i, g in enumerate(grads):
            pltpu.make_async_copy(g[6], g[7].at[do, di], own_sem.at[i]).wait()
            for piece in (do, flip(do, g[8])):
                later.append(post(g[7].at[piece, di], g[7].at[piece, di], column(g[9])))
        return later

    def stage_six(copies):
        arrived(copies)
        return [post(g[7].at[:, di], g[7].at[:, di], sibling) for g in grads]

    for copy in own[:-1]:
        copy.wait()
    copies = stage_two(grads[:2])
    for k in range(GROUP):
        pltpu.make_async_copy(gctx_ref.at[k], gall.at[k], b_recv.at[k]).wait()
    for k in range(GROUP):
        swaps.append(
            (
                delta_ref.at[k], m_ref.at[quarter], b_send.at[GROUP + k],
                b_recv.at[GROUP + quarter], place, (row, k), do,
            )
        )
        send_block(*swaps[GROUP + k])
    back_block(3)
    to_sibling(3)
    weight_terms(3)
    out_copies = stage_one()
    copies = stage_three(copies, grads[:2])
    back_block(2)
    to_sibling(2)
    across_row(3)
    weight_terms(2)
    arrived(out_copies)
    out_copies = stage_two(grads[2:])
    back_block(1)
    to_sibling(1)
    across_row(2)
    weight_terms(1)
    copies += stage_three(out_copies, grads[2:])
    back_block(0)
    to_sibling(0)
    across_row(1)
    weight_terms(0)
    across_row(0)

    wide = width // 2
    sides = (pl.ds(0, wide), pl.ds(wide, wide))
    bits = ((1, 2), (2, 1))
    gq[...] = acc_w[...].astype(BF).reshape(gq.shape)
    q_copies = []
    for side, (first, second) in enumerate(bits):
        for n, piece in enumerate((flip(do, first), flip(flip(do, first), second))):
            q_copies.append(post(gq.at[piece, :, sides[side]], q_one.at[side, n], column(first)))
    copies = stage_four(copies)

    @pl.when(half == 0)
    def _():
        for i in (0, 1):
            @pl.when(di == i)
            def _():
                remote(*far_args(i)).wait_recv()

    @pl.when(half == 1)
    def _():
        for i in (2, 3):
            @pl.when(di == i - 2)
            def _():
                remote(*far_args(i)).wait_recv()

    acc_gain[...] = jnp.zeros_like(acc_gain)

    def norm_step(lane, carry):
        lanes = pl.ds(pl.multiple_of(lane * 128, 128), 128)
        values = x_ref[:, lanes]
        grad = near[half, :, lanes] + far_buf[:, lanes].astype(F32)
        row_sum, inverse = stat_ref[0:1, lanes], stat_ref[1:2, lanes]
        final = lax.broadcasted_iota(jnp.int32, (width, 128), 0) == width - 1
        recovered = jnp.where(final, -row_sum, values)
        scaled = grad * gain_wide[...]
        acc_gain[...] += grad * recovered * inverse
        dot_sum = jnp.sum(scaled * recovered, axis=0, keepdims=True)
        tail = scaled[width - 1 :]
        factor = dot_sum * (inverse * inverse * inverse) / width
        grad_in = inverse * (scaled - tail) - factor * (values + row_sum)
        grad_in = jnp.where(final, 0.0, grad_in) + gn2_ref[:, lanes].astype(F32)
        for j in range(GROUP):
            s_blocks[j, :, lanes] = grad_in[j * columns : (j + 1) * columns].astype(BF)
        return carry

    lax.fori_loop(0, tokens // 128, norm_step, 0)
    for k in range(GROUP):
        swaps.append(
            (
                s_blocks.at[k], s_ref.at[quarter], b_send.at[2 * GROUP + k],
                b_recv.at[2 * GROUP + quarter], place, (row, k), do,
            )
        )
        send_block(*swaps[2 * GROUP + k])

    small_a[...] = jnp.zeros_like(small_a)
    small_a[0] = jnp.sum(acc_gain[...].T, axis=0, keepdims=True)
    bias_row = jnp.sum(acc_b[...].T, axis=0, keepdims=True)
    for r in range(3):
        small_a[1 + r] = sums_ref[r]
    for r in range(GROUP):
        small_a[4 + lax.rem(mp + r, GROUP)] = sums_ref[3 + r]
    small_a[8 + 2 * quarter, :, :columns] = bias_row[:, :columns]
    small_a[9 + 2 * quarter, :, :columns] = bias_row[:, 2 * columns : 3 * columns]
    small_one = post(small_a, small_b.at[0], sibling)

    arrived(q_copies)
    q_copies = []
    for side, (first, second) in enumerate(bits):
        for n, piece in ((1, flip(do, second)), (0, do)):
            gq[piece, :, sides[side]] = (
                gq[piece, :, sides[side]].astype(F32) + q_one[side, n].astype(F32)
            ).astype(BF)
            if n == 1:
                q_copies.append(post(gq.at[piece, :, sides[side]], q_two.at[side], column(second)))
    finish(small_one)
    small_a[...] += small_b[0]
    small_one = post(small_a, small_b.at[1], column(1))
    copies = stage_five(copies)
    arrived(q_copies)
    z_args = []
    for side in range(2):
        gq[do, :, sides[side]] = (
            gq[do, :, sides[side]].astype(F32) + q_two[side].astype(F32)
        ).astype(BF)
        z_args.append(
            (
                gq.at[do, :, sides[side]], q_z.at[row], b_send.at[3 * GROUP + side],
                b_recv.at[3 * GROUP + row], place, (side, quarter), do,
            )
        )
        send_block(*z_args[side])
    finish(small_one)
    small_a[...] += small_b[1]
    small_one = post(small_a, small_b.at[2], column(2))

    for r in range(2):
        pltpu.make_async_copy(q_z.at[r], q_z.at[r], b_recv.at[3 * GROUP + r]).wait()
    q_fin[...] = q_z[0].astype(F32) + q_z[1].astype(F32)

    def q_ref(piece, core):
        return qkvg_ref.at[piece, core]

    q_own = pltpu.make_async_copy(q_fin, q_ref(do, di), own_sem.at[3])
    q_own.start()
    q_copies = [post(q_fin, q_ref(do, di), column(bit)) for bit in (1, 2)]
    finish(small_one)
    small_z[mp] = small_a[...] + small_b[2]
    small_copies = [
        post(small_z.at[mp], small_z.at[mp], dev(do, di, lax.rem(mp + r, GROUP)))
        for r in range(1, GROUP)
    ]
    copies = stage_six(copies)
    arrived(q_copies)

    q_last = prepare(q_ref(do, di), q_ref(do, di), sibling)
    n = len(posted) - 1

    @pl.when(di == 0)
    def _():
        piece = q_ref(flip(do, 1), di)
        remote(piece, piece, send.at[n], recv.at[n], column(2)).start()

    @pl.when(di == 1)
    def _():
        piece = q_ref(flip(do, 2), di)
        remote(piece, piece, send.at[n], recv.at[n], column(1)).start()

    q_own.wait()
    q_last.wait_recv()
    q_copies = [post(qkvg_ref.at[:, di], qkvg_ref.at[:, di], sibling)]
    arrived(small_copies)
    small_out[...] = small_z[0] + small_z[1] + small_z[2] + small_z[3]
    arrived(q_copies)

    for k in range(GROUP):
        pltpu.make_async_copy(delta_ref.at[k], m_ref.at[k], b_recv.at[GROUP + k]).wait()
        pltpu.make_async_copy(s_blocks.at[k], s_ref.at[k], b_recv.at[2 * GROUP + k]).wait()
    for args in swaps + z_args:
        sent_block(*args)
    for i in range(GROUP):
        @pl.when(di != i % 2)
        def _():
            remote(*near_args(i)).wait_send()

        @pl.when(jnp.logical_and(di == i % 2, half != i // 2))
        def _():
            remote(*far_args(i)).wait_send()

    arrived(copies)
    for copy in pending:
        copy.wait_send()


def backward_part(values):
    (
        grad_context, delta, x_mine, grad_norm, heads_out, _, qkv, lse, normed, smalls,
        head_weight, segs, _, sums, up_grad, _, down_grad, _, out_grad,
    ) = values
    columns, tokens = heads_out.shape[1:]
    width = x_mine.shape[0]
    heads = columns // HD
    shape = jax.ShapeDtypeStruct
    vmem, anywhere = pl.BlockSpec(memory_space=pltpu.VMEM), pl.BlockSpec(memory_space=pl.ANY)
    dma = pltpu.SemaphoreType.DMA
    slabs = (GROUP, columns, tokens)
    pieces = head_weight.shape[1]
    weight_grads = (up_grad, down_grad, out_grad)
    rows = [w.shape[-2:] for w in weight_grads]
    halves = [(GROUP, GROUP) + r for r in rows]
    buffers = (
        halves[2:]
        + halves
        + [(2, GROUP) + r for r in rows]
        + [(GROUP,) + r for r in rows]
        + [(GROUP - 1,) + r for r in rows]
    )
    return pl.pallas_call(
        backward_kernel,
        out_shape=[
            shape(slabs, BF),
            shape(slabs, BF),
            shape((GROUP, 2, pieces, width // 2), F32),
            shape((16, 1, width), F32),
        ]
        + [shape((GROUP, 2) + r, F32) for r in rows],
        in_specs=[vmem] * 14 + [anywhere] * 5,
        out_specs=[vmem] * 4 + [anywhere] * 3,
        scratch_shapes=[
            pltpu.VMEM(slabs, BF),
            pltpu.VMEM((heads, GROUP, tokens, HD), BF),
            pltpu.VMEM((heads, GROUP, tokens, HD), BF),
            pltpu.VMEM((tokens, tokens), F32),
            pltpu.VMEM(slabs, F32),
            pltpu.VMEM(slabs, F32),
            pltpu.VMEM((3 * columns, tokens), BF),
            pltpu.VMEM((3 * columns, width), F32),
            pltpu.VMEM((640, 128), F32),
            pltpu.VMEM((width, 128), F32),
            pltpu.VMEM((width, 128), F32),
            pltpu.VMEM((GROUP, width, tokens), F32),
            pltpu.VMEM((2, width, tokens), F32),
            pltpu.VMEM((width, tokens), BF),
            pltpu.VMEM((width, tokens), BF),
            pltpu.VMEM(slabs, BF),
        ]
        + [pltpu.VMEM(b, BF) for b in buffers]
        + [pltpu.VMEM(r, F32) for r in rows]
        + [
            pltpu.VMEM((GROUP, pieces, width), BF),
            pltpu.VMEM((2, 2, pieces, width // 2), BF),
            pltpu.VMEM((2, pieces, width // 2), BF),
            pltpu.VMEM((2, pieces, width // 2), BF),
            pltpu.VMEM((pieces, width // 2), F32),
            pltpu.VMEM((16, 1, width), F32),
            pltpu.VMEM((3, 16, 1, width), F32),
            pltpu.VMEM((GROUP, 16, 1, width), F32),
            dma((10,)),
            dma((14,)),
            dma((14,)),
            dma((2 * GROUP,)),
            dma((2 * GROUP,)),
            dma((56,)),
            dma((56,)),
        ],
        compiler_params=pltpu.CompilerParams(
            collective_id=7, has_side_effects=True, vmem_limit_bytes=60 * 2**20
        ),
    )(*values)


def own_quarter(di, mp):
    return 2 * lax.rem(mp, 2) + di


def lane_chunks(count, step):
    lax.fori_loop(
        0, count, lambda i, c: (step(pl.ds(pl.multiple_of(i * 128, 128), 128)), c)[1], 0
    )


def xor(index, mask):
    for bit in (1, 2):
        if mask & bit:
            index = flip(index, bit)
    return index


def first_kernel(
    stream_ref, cot_ref, seg_ref, small_ref, bias_ref, qkvw_ref, up_own, down_own, out_own,
    mine_ref, heads_ref, rest_ref, qkv_ref, lse_ref, normed_ref, smalls_ref, headw_ref, segs_ref,
    stat_ref, delta_ref, gctx_ref, gnorm_ref, sums_ref, mine_up, one_up, mine_down, one_down, dout_ref,
    up_all, down_all, out_all,
    grad_ref, context_ref, k_tokens, big, causal, wide_gain, back_gain, n2t, gyt,
    stats, x_more, g_more,
    w_up, w_down, w_out, d_up, d_down, n2, gy, pre, ghid, hidden, gpre, mlp, gn2, acc_gain,
    core_up, core_down,
    own_sem, in_sem, w_sem, x_send, x_recv, g_send, g_recv, c_send, c_recv, s_send, s_recv,
    st_send, st_recv, r_send, r_recv, h_send, h_recv, a_send, a_recv, t_send, t_recv, k_send, k_recv, o_send, o_recv,
):
    do, di, mp = places()
    width, tokens = normed_ref.shape[1], normed_ref.shape[2]
    columns = stream_ref.shape[0]
    heads_here = columns // HD
    lanes_count = tokens // 128
    row, quarter = mp // 2, own_quarter(di, mp)
    place = (di, mp)
    sibling, across = dev(do, 1 - di, mp), dev(do, di, flip(mp, 1))
    far = 2 * (1 - lax.rem(mp, 2)) + di
    weights = ((up_own, up_all), (down_own, down_all), (out_own, out_all))
    final = lax.broadcasted_iota(jnp.int32, (width, 128), 0) == width - 1

    def column(bit):
        return dev(flip(do, bit), di, mp)

    loads = []
    for i, ref in enumerate((stream_ref, cot_ref)):
        for k in range(GROUP):
            loads.append(
                pltpu.make_async_copy(
                    ref.at[:, pl.ds(k * tokens, tokens)],
                    big.at[pl.ds(i * width + k * columns, columns)],
                    own_sem.at[2 + GROUP * i + k],
                )
            )
    own = [
        pltpu.make_async_copy(small_ref, smalls_ref.at[mp], own_sem.at[0]),
        pltpu.make_async_copy(seg_ref, segs_ref.at[di], own_sem.at[1]),
    ]
    for copy in loads + own:
        copy.start()
    greet(neighbours(do, di, mp))
    is_last = jnp.logical_and(
        mp == GROUP - 1, lax.broadcasted_iota(jnp.int32, (columns, tokens), 0) == columns - 1
    )

    def target_of(k):
        return lax.rem(k, 2), 2 * di + k // 2

    def rows_at(j):
        return pl.ds(pl.multiple_of(j * columns, 64), columns)

    def others():
        return [dev(do, di, lax.rem(mp + r, GROUP)) for r in range(1, GROUP)]

    x_rest = [n2t.at[pl.ds(k * columns, columns)] for k in range(GROUP)]
    g_rest = [gnorm_ref.at[pl.ds(k * columns, columns)] for k in range(GROUP)]

    for k in range(GROUP):
        loads[k].wait()
        rows_k = pl.ds(k * columns, columns)
        part = jnp.where(is_last, 0.0, big[rows_k])
        big[rows_k] = part
        stats[mp, k, 0:1] = jnp.sum(part, axis=0, keepdims=True)
        stats[mp, k, 1:2] = jnp.sum(part * part, axis=0, keepdims=True)
    sums_over = [
        remote(stats.at[mp], stats.at[mp], st_send.at[r], st_recv.at[GROUP - r - 1], other)
        for r, other in zip(range(GROUP - 1), others())
    ]
    for copy in sums_over:
        copy.start()
    smalls = []
    for r in range(1, GROUP):
        target = dev(do, di, lax.rem(mp + r, GROUP))
        smalls.append(
            remote(small_ref, smalls_ref.at[mp], s_send.at[r], s_recv.at[GROUP - r], target)
        )
    smalls.append(remote(seg_ref, segs_ref.at[di], s_send.at[0], s_recv.at[0], sibling))
    for copy in smalls:
        copy.start()
    own_turned = small_ref[...].T
    own_gain = own_turned[:columns, 0:1]
    for copy in sums_over:
        copy.wait_recv()
    x_args, stat_args, x_rest_args = [], [], []
    for k in range(GROUP):
        row_sum = stats[0, k, 0:1] + stats[1, k, 0:1] + stats[2, k, 0:1] + stats[3, k, 0:1]
        squares = stats[0, k, 1:2] + stats[1, k, 1:2] + stats[2, k, 1:2] + stats[3, k, 1:2]
        mean = (squares + row_sum * row_sum) / width + EPS
        inverse = lax.rsqrt(mean)
        stats[GROUP, k, 0:1] = row_sum
        stats[GROUP, k, 1:2] = inverse
        stats[GROUP, k, 2:3] = 1.0 / inverse
        values = big[k * columns : (k + 1) * columns]
        recovered = jnp.where(is_last, -row_sum, values)
        normed = (recovered * inverse * own_gain).astype(BF)
        delta_ref[k] = normed
        x_args.append(
            (
                delta_ref.at[k], normed_ref.at[k, rows_at(mp)], x_send.at[k], x_recv.at[mp],
                place, target_of(k), do,
            )
        )
        send_block(*x_args[k])
        near = (normed.astype(F32) * (1.0 / own_gain)) * stats[GROUP, k, 2:3]
        x_rest[k][...] = jnp.where(is_last, 0.0, values - near).astype(BF)
        stat_args.append(
            (stats.at[GROUP, k], stat_ref, r_send.at[k], r_recv.at[0], place, target_of(k), do)
        )
        x_rest_args.append(
            (
                x_rest[k], x_more.at[mp], r_send.at[GROUP + k], r_recv.at[1 + mp],
                place, target_of(k), do,
            )
        )

    @pl.when(mp == 0)
    def _():
        for args in stat_args:
            send_block(*args)

    head_target = (lax.rem(mp, 2), mp // 2 + 2 * di)
    head_args = (
        qkvw_ref.at[do], headw_ref.at[do], h_send.at[0], h_recv.at[0], place, head_target, do,
    )
    send_block(*head_args)

    gathers = []
    for k in range(GROUP):
        j = xor(mp, k)
        part = normed_ref.at[quarter, rows_at(j)]
        pltpu.make_async_copy(part, part, x_recv.at[j]).wait()
        for lane, other in enumerate((across, sibling)):
            copy = remote(part, part, g_send.at[lane, k], g_recv.at[lane, k], other)
            copy.start()
            gathers.append(copy)

    def over_mp(i, r):
        ref, all_ref = weights[i]
        return remote(
            ref.at[do, di] if i < 2 else piece_of(ref, do, di), all_ref.at[do, di, r],
            a_send.at[i, r], a_recv.at[i, r], dev(do, di, lax.rem(mp + GROUP - r, GROUP)),
        )

    for r in range(1, GROUP):
        over_mp(2, r).start()
    for i in range(2):
        over_mp(i, 1).start()

    orders = ((1, 2), (2, 1))

    def hop(i, r, stage):
        all_ref = weights[i][1]
        first, second = orders[i]
        if stage == 3:
            ref = all_ref.at[:, di, r]
            return [remote(ref, ref, t_send.at[i, r, 3], t_recv.at[i, r, 3], sibling)]
        pieces = (do,) if stage == 1 else (do, flip(do, first))
        bit = first if stage == 1 else second
        copies = []
        for n, piece in enumerate(pieces):
            ref = all_ref.at[piece, di, r]
            at = stage - 1 + n
            copies.append(remote(ref, ref, t_send.at[i, r, at], t_recv.at[i, r, at], column(bit)))
        return copies

    def out_hop(stage):
        if stage == 3:
            ref = out_all.at[:, di, pl.ds(1, GROUP - 1)]
            return [remote(ref, ref, t_send.at[0, 0, 3], t_recv.at[0, 0, 3], sibling)]
        pieces = (do,) if stage == 1 else (do, flip(do, 1))
        copies = []
        for n, piece in enumerate(pieces):
            ref = out_all.at[piece, di, pl.ds(1, GROUP - 1)]
            at = stage - 1 + n
            copies.append(
                remote(ref, ref, t_send.at[0, 0, at], t_recv.at[0, 0, at], column(stage))
            )
        return copies

    def start(copies):
        for copy in copies:
            copy.start()

    def arrived(copies):
        for copy in copies:
            copy.wait_recv()

    def both(r, stage):
        return hop(0, r, stage) + hop(1, r, stage)

    pltpu.make_async_copy(qkvw_ref.at[do], headw_ref.at[do], h_recv.at[0]).wait()
    cut = 80
    part_a, part_b = pl.ds(0, cut), pl.ds(cut, headw_ref.shape[1] - cut)
    heads = []

    def head_copy(piece, part, bit):
        ref = headw_ref.at[piece, part]
        n = len(heads) + 1
        copy = remote(ref, ref, h_send.at[n], h_recv.at[n], column(bit))
        copy.start()
        heads.append(copy)

    head_copy(do, part_a, 1)
    head_copy(do, part_b, 2)

    arrived(smalls)
    for copy in own:
        copy.wait()
    for j in range(GROUP):
        turned = smalls_ref[j].T
        at = slice(j * columns, (j + 1) * columns)
        back_gain[at] = jnp.broadcast_to(1.0 / turned[:columns, 0:1], (columns, 128))
        wide_gain[at] = jnp.broadcast_to(turned[columns : 2 * columns, 0:1], (columns, 128))
    biases = smalls_ref[quarter].T
    query_bias = biases[2 * columns : 3 * columns, 0:1]
    value_bias = biases[3 * columns :, 0:1]
    causal[...] = jnp.where(
        lax.broadcasted_iota(jnp.int32, causal.shape, 0)
        <= lax.broadcasted_iota(jnp.int32, causal.shape, 1),
        0.0, NEG,
    )
    for k in range(GROUP):
        loads[GROUP + k].wait()
        part = jnp.where(is_last, 0.0, big[width + k * columns : width + (k + 1) * columns])
        gctx_ref[k] = part.astype(BF)
        g_rest[k][...] = (part - gctx_ref[k].astype(F32)).astype(BF)
    arrived(heads[:2])
    head_copy(do, part_a, 2)
    head_copy(flip(do, 1), part_a, 2)
    head_copy(do, part_b, 1)
    head_copy(flip(do, 2), part_b, 1)
    for k in range(GROUP):
        gathers[2 * k].wait_recv()
        part = normed_ref.at[far, rows_at(xor(mp, 1 ^ k))]
        copy = remote(part, part, g_send.at[2, k], g_recv.at[2, k], sibling)
        copy.start()
        gathers.append(copy)
    for k in range(GROUP):
        gathers[2 * k + 1].wait_recv()
        gathers[2 * GROUP + k].wait_recv()
    arrived(heads[2:])
    cot_args = [
        (gctx_ref.at[k], grad_ref.at[mp], c_send.at[k], c_recv.at[mp], place, target_of(k), do)
        for k in range(GROUP)
    ]
    for args in cot_args:
        send_block(*args)
    g_rest_args = [
        (
            g_rest[k], g_more.at[mp], r_send.at[2 * GROUP + k], r_recv.at[1 + GROUP + mp],
            place, target_of(k), do,
        )
        for k in range(GROUP)
    ]
    head_weight = headw_ref[...].reshape(3 * columns, width)

    def project(block, carry):
        joined = jnp.dot(head_weight, normed_ref[block], preferred_element_type=F32)
        qkv_ref[block, :columns] = (joined[:columns] + query_bias).astype(BF)
        keys = joined[columns : 2 * columns].astype(BF)
        qkv_ref[block, columns : 2 * columns] = keys
        qkv_ref[block, 2 * columns :] = (joined[2 * columns :] + value_bias).astype(BF)
        for h in range(heads_here):
            k_tokens[h, block] = keys[h * HD : (h + 1) * HD].T
        return carry

    lax.fori_loop(0, GROUP, project, 0)
    segments = segs_ref[row]

    def attend(block):
        seg_q = segments[:, block * tokens : (block + 1) * tokens]
        masks = [
            jnp.where(segments[:, kb * tokens : kb * tokens + 1] == seg_q, 0.0, NEG)
            for kb in range(block)
        ]

        def one_head(h, carry):
            rows = pl.ds(pl.multiple_of(h * HD, HD), HD)
            v_rows = pl.ds(pl.multiple_of(2 * columns + h * HD, HD), HD)
            query = qkv_ref[block, rows] * HD ** (-0.5)
            top = None
            for kb in range(block + 1):
                raw = jnp.dot(k_tokens[h, kb], query, preferred_element_type=F32)
                raw = raw + (causal[...] if kb == block else masks[kb])
                big[kb * tokens : (kb + 1) * tokens] = raw
                high = jnp.max(raw, axis=0, keepdims=True)
                top = high if top is None else jnp.maximum(top, high)
            total = jnp.zeros((1, tokens), F32)
            for kb in range(block + 1):
                expo = jnp.exp(big[kb * tokens : (kb + 1) * tokens] - top)
                big[kb * tokens : (kb + 1) * tokens] = expo
                total += jnp.sum(expo, axis=0, keepdims=True)
            portion = 1.0 / total
            mixed = jnp.zeros((HD, tokens), F32)
            for kb in range(block + 1):
                probs = (big[kb * tokens : (kb + 1) * tokens] * portion).astype(BF)
                mixed += jnp.dot(qkv_ref[kb, v_rows], probs, preferred_element_type=F32)
            rounded = mixed.astype(BF)
            heads_ref[block, rows] = rounded
            rest_ref[block, rows] = (mixed - rounded.astype(F32)).astype(BF)
            lse_ref[h, block] = jnp.broadcast_to(top + jnp.log(total), (8, tokens))
            return carry

        lax.fori_loop(0, heads_here, one_head, 0)

    context_args = [
        (
            heads_ref.at[block], context_ref.at[quarter], c_send.at[GROUP + block],
            c_recv.at[GROUP + quarter], place, holder(row, block), do,
        )
        for block in range(GROUP)
    ]

    def arrived_mp(r):
        arrived([over_mp(0, r), over_mp(1, r)])

    arrived([over_mp(2, r) for r in range(1, GROUP)])
    start(out_hop(1))
    arrived_mp(1)
    start(both(1, 1))
    for args in x_rest_args:
        send_block(*args)
    attend(0)
    send_block(*context_args[0])
    arrived(out_hop(1))
    start(out_hop(2))
    start([over_mp(i, 2) for i in range(2)])
    attend(1)
    send_block(*context_args[1])
    arrived(both(1, 1))
    start(both(1, 2))
    start([over_mp(i, 3) for i in range(2)])
    attend(2)
    send_block(*context_args[2])
    arrived(out_hop(2))
    start(out_hop(3))
    arrived_mp(2)
    start(both(2, 1))
    attend(3)
    send_block(*context_args[3])
    arrived(both(1, 2))
    start(both(1, 3))
    arrived(both(2, 1))
    start(both(2, 2))
    arrived_mp(3)
    start(both(3, 1))
    for args in g_rest_args:
        send_block(*args)

    attn, middle = big.at[pl.ds(0, width)], big.at[pl.ds(width, width)]
    own_weights = [
        pltpu.make_async_copy(ref, buf.at[0], in_sem.at[i, 0])
        for i, (ref, buf) in enumerate(((up_own, w_up), (down_own, w_down)))
    ]

    def fetch(r, slot):
        return [
            pltpu.make_async_copy(ref.at[:, :, r], buf.at[slot], in_sem.at[i, slot])
            for i, (ref, buf) in enumerate(((up_all, w_up), (down_all, w_down)))
        ]

    start(own_weights)
    rows, lanes = columns // GROUP, width // 2
    arrived(out_hop(3))
    out_loads = [pltpu.make_async_copy(out_own, w_out.at[mp], w_sem.at[0])]
    for r in range(1, GROUP):
        shard = lax.rem(mp + r, GROUP)
        for piece in range(GROUP):
            for side in range(2):
                out_loads.append(
                    pltpu.make_async_copy(
                        out_all.at[piece, side, r],
                        w_out.at[shard, pl.ds(piece * rows, rows), pl.ds(side * lanes, lanes)],
                        w_sem.at[(r * GROUP + piece) * 2 + side],
                    )
                )
    start(out_loads)
    bias_cols = bias_ref[...].T
    for k in range(GROUP):
        pltpu.make_async_copy(grad_ref.at[k], grad_ref.at[k], c_recv.at[k]).wait()

    def cotangent_at(at):
        return grad_ref[:, :, at].reshape(width, 128).astype(F32)

    def centre_grad(at):
        grad = cotangent_at(at)
        gyt[:, at] = (grad - jnp.sum(grad, axis=0, keepdims=True) / width).astype(BF)

    lane_chunks(lanes_count, centre_grad)
    gy[...] = gyt[...].T
    sums_ref[2] = jnp.sum(gy[...].astype(F32), axis=0, keepdims=True)
    for copy in out_loads:
        copy.wait()
    for k in range(GROUP):
        pltpu.make_async_copy(heads_ref.at[k], context_ref.at[k], c_recv.at[GROUP + k]).wait()
    pltpu.make_async_copy(stat_ref, stat_ref, r_recv.at[0]).wait()
    for k in range(GROUP):
        pltpu.make_async_copy(x_more.at[k], x_more.at[k], r_recv.at[1 + k]).wait()
    projected = dot_tn(w_out[0], context_ref[0])
    for s in range(1, GROUP):
        projected += dot_tn(w_out[s], context_ref[s])
    attn[...] = projected + bias_cols[:, 0:1]

    def norm(at):
        values = attn[:, at]
        values = values - jnp.sum(values, axis=0, keepdims=True) / width
        values = jnp.where(final, 0.0, values)
        attn[:, at] = values
        mine = (normed_ref[quarter, :, at].astype(F32) * back_gain[...]) * stat_ref[2:3, at]
        mine = mine + x_more[:, :, at].reshape(width, 128).astype(F32)
        mine = jnp.where(final, 0.0, mine)
        mine_ref[:, at] = mine
        values = values + mine
        middle[:, at] = values
        row_sum = jnp.sum(values, axis=0, keepdims=True)
        square_sum = jnp.sum(values * values, axis=0, keepdims=True)
        inverse = lax.rsqrt((square_sum + row_sum * row_sum) / width + EPS)
        recovered = jnp.where(final, -row_sum, values)
        n2t[:, at] = (recovered * inverse * wide_gain[...]).astype(BF)

    for args in x_rest_args:
        sent_block(*args)
    lane_chunks(lanes_count, norm)
    n2[...] = n2t[...].T
    arrived(both(2, 2))
    start(both(2, 3))
    arrived(both(GROUP - 1, 1))
    start(both(GROUP - 1, 2))
    grads = (
        (d_up, core_up, mine_up, one_up, 1, 2),
        (d_down, core_down, mine_down, one_down, 2, 1),
    )

    def to_sibling(r, slot):
        return [
            remote(g[0].at[slot, :, 1 - di], g[1].at[r], k_send.at[i, slot], k_recv.at[i, r], sibling)
            for i, g in enumerate(grads)
        ]

    def to_column(r):
        copies = []
        for i, g in enumerate(grads):
            first, second = g[4], g[5]
            for n, piece in enumerate((flip(do, first), flip(flip(do, first), second))):
                copies.append(
                    remote(
                        g[2].at[piece, r], g[3].at[n, r], o_send.at[i, n, r], o_recv.at[i, n, r],
                        column(first),
                    )
                )
        return copies

    def combine(r, slot):
        for copy in to_sibling(r, slot):
            copy.wait()
        for g in grads:
            add_pairs(
                GROUP, lambda k: g[2].at[k, r], lambda k: g[0].at[slot, k, di], lambda k: g[1].at[r, k]
            )
        start(to_column(r))

    chunk = 64
    root = 0.7978845608028654

    def shard_step(r, carry):
        slot = lax.rem(r, 2)
        for copy in fetch(r, slot):
            copy.wait()

        @pl.when(r < GROUP - 1)
        def _():
            arrived(both(r + 1, 3))
            start(fetch(r + 1, 1 - slot))

        @pl.when(r == 0)
        def _():
            arrived(both(GROUP - 1, 2))
            start(both(GROUP - 1, 3))

        up = w_up[slot].reshape(width, width)
        down = w_down[slot].reshape(width, width)
        bias = smalls_ref[lax.rem(mp + r, GROUP), 1:2]
        pre[...] = jnp.dot(n2[...], up, preferred_element_type=F32) + bias
        ghid[...] = dot_nt(gy[...], down)

        def gelu(i, carry):
            at = pl.ds(pl.multiple_of(i * chunk, chunk), chunk)
            p = pre[at]
            square = p * p
            t = jnp.tanh(root * (p + 0.044715 * (p * square)))
            half = 0.5 * (1.0 + t)
            hidden[at] = (p * half).astype(BF)
            slope = half + 0.5 * p * (1.0 - t * t) * (root * (1.0 + 3 * 0.044715 * square))
            gpre[at] = (ghid[at] * slope).astype(BF)
            return carry

        lax.fori_loop(0, tokens // chunk, gelu, 0)

        @pl.when(r >= 1)
        def _():
            combine(r - 1, 1 - slot)

        d_down[slot] = dot_tn(hidden[...], gy[...]).astype(BF).reshape(d_down.shape[1:])
        d_up[slot] = (
            jnp.dot(n2t[...], gpre[...], preferred_element_type=F32)
            .astype(BF)
            .reshape(d_up.shape[1:])
        )
        start(to_sibling(r, slot))
        sums_ref[3 + r] = jnp.sum(gpre[...].astype(F32), axis=0, keepdims=True)
        more_mlp = jnp.dot(hidden[...], down, preferred_element_type=F32)
        more_grad = dot_nt(gpre[...], up)

        @pl.when(r == 0)
        def _():
            mlp[...] = more_mlp
            gn2[...] = more_grad

        @pl.when(r > 0)
        def _():
            mlp[...] += more_mlp
            gn2[...] += more_grad

        return carry

    lax.fori_loop(0, GROUP, shard_step, 0)
    combine(GROUP - 1, (GROUP - 1) % 2)
    mlp_y = mlp[...] + bias_ref[1:2]
    pre[...] = mlp_y - jnp.sum(mlp_y, axis=1, keepdims=True) / width
    acc_gain[...] = jnp.zeros_like(acc_gain)
    gat = gyt
    for args in x_args + cot_args + g_rest_args:
        sent_block(*args)
    for k in range(GROUP):
        pltpu.make_async_copy(g_more.at[k], g_more.at[k], r_recv.at[1 + GROUP + k]).wait()

    def back(at):
        mlp_z = jnp.where(final, 0.0, pre[at].T)
        delta = attn[:, at] + mlp_z
        grad = gn2[at].T
        values = middle[:, at]
        row_sum = jnp.sum(values, axis=0, keepdims=True)
        square_sum = jnp.sum(values * values, axis=0, keepdims=True)
        inverse = lax.rsqrt((square_sum + row_sum * row_sum) / width + EPS)
        recovered = jnp.where(final, -row_sum, values)
        acc_gain[...] += grad * recovered * inverse
        scaled = grad * wide_gain[...]
        dot_sum = jnp.sum(scaled * recovered, axis=0, keepdims=True)
        tail = scaled[width - 1 :]
        factor = dot_sum * (inverse * inverse * inverse) / width
        grad_in = inverse * (scaled - tail) - factor * (values + row_sum)
        grad_in = jnp.where(final, 0.0, grad_in)
        gnorm_ref[:, at] = grad_in.astype(BF)
        more = g_more[:, :, at].reshape(width, 128).astype(F32)
        grad_z = jnp.where(final, 0.0, (cotangent_at(at) + more) + grad_in)
        grad_z = grad_z.astype(BF).astype(F32)
        gat[:, at] = (grad_z - jnp.sum(grad_z, axis=0, keepdims=True) / width).astype(BF)
        for j in range(GROUP):
            delta_ref[j, :, at] = delta[j * columns : (j + 1) * columns].astype(BF)

    lane_chunks(lanes_count, back)
    sums_ref[0] = jnp.sum(acc_gain[...].T, axis=0, keepdims=True)
    sums_ref[1] = dot_nt(jnp.ones((8, tokens), BF), gat[...])[:1]
    sums_ref[7] = jnp.zeros_like(sums_ref[7])
    for s in range(GROUP):
        gctx_ref[s] = jnp.dot(w_out[s], gat[...], preferred_element_type=F32).astype(BF)
        terms = dot_nt(context_ref[s], gat[...]).astype(BF)
        for side in range(2):
            dout_ref[:, side, lax.rem(s + GROUP - mp, GROUP)] = terms[
                :, side * lanes : (side + 1) * lanes
            ].reshape(GROUP, rows, lanes)
    sent_block(*head_args)
    for args in context_args:
        sent_block(*args)

    @pl.when(mp == 0)
    def _():
        for args in stat_args:
            sent_block(*args)

    sent = gathers + smalls + heads + sums_over
    for r in range(1, GROUP):
        sent += [over_mp(i, r) for i in range(3)]
        for stage in (1, 2, 3):
            sent += both(r, stage)
    for stage in (1, 2, 3):
        sent += out_hop(stage)
    for copy in sent:
        copy.wait_send()
    for r in range(GROUP):
        for copy in to_column(r):
            copy.wait()


def first_part(stream, cotangent, segment_ids, small, biases, qkv_weight, up, down, out):
    columns, token_count = stream.shape
    width, tokens = columns * GROUP, token_count // GROUP
    heads = columns // HD
    shape = jax.ShapeDtypeStruct
    vmem, anywhere = pl.BlockSpec(memory_space=pltpu.VMEM), pl.BlockSpec(memory_space=pl.ANY)
    dma = pltpu.SemaphoreType.DMA
    up, down = pieces_of(up), pieces_of(down)
    head_pieces = qkv_weight.reshape(GROUP, 3 * columns // GROUP, width)
    slabs = (GROUP, columns, tokens)
    rows = up.shape[2:]
    out_rows = (columns // GROUP, width // 2)
    part, half = (2,) + up.shape, (GROUP, GROUP) + rows
    bf = lambda *dims: pltpu.VMEM(dims, BF)
    fl = lambda *dims: pltpu.VMEM(dims, F32)
    return pl.pallas_call(
        first_kernel,
        out_shape=[
            shape((width, tokens), F32),
            shape(slabs, BF),
            shape(slabs, BF),
            shape((GROUP, 3 * columns, tokens), BF),
            shape((heads, GROUP, 8, tokens), F32),
            shape((GROUP, width, tokens), BF),
            shape((GROUP,) + small.shape, F32),
            shape(head_pieces.shape, BF),
            shape((2, 1, token_count), jnp.int32),
            shape((8, tokens), F32),
            shape(slabs, BF),
            shape(slabs, BF),
            shape((width, tokens), BF),
            shape((8, 1, width), F32),
        ]
        + [shape(half, BF), shape((2,) + half[1:], BF)] * 2
        + [shape((GROUP, 2, GROUP) + out_rows, BF)]
        + [shape((GROUP, 2, GROUP) + p, BF) for p in (rows, rows, out_rows)],
        in_specs=[anywhere] * 2 + [vmem] * 3 + [anywhere] * 4,
        out_specs=[vmem] * 19 + [anywhere] * 3,
        scratch_shapes=[
            bf(*slabs), bf(*slabs), bf(heads, GROUP, tokens, HD),
            fl(token_count, tokens), fl(tokens, tokens), fl(width, 128), fl(width, 128),
            bf(width, tokens), bf(width, tokens), fl(GROUP + 1, GROUP, 8, tokens),
            bf(*slabs), bf(*slabs),
            bf(*part), bf(*part), bf(GROUP, columns, width), bf(*part), bf(*part),
            bf(tokens, width), bf(tokens, width), fl(tokens, width), fl(tokens, width),
            bf(tokens, width), bf(tokens, width), fl(tokens, width), fl(tokens, width),
            fl(width, 128), bf(*half), bf(*half),
            dma((10,)), dma((2, 2)), dma((2 * GROUP * GROUP,)),
            dma((GROUP,)), dma((GROUP,)), dma((3, GROUP)), dma((3, GROUP)),
            dma((2 * GROUP,)), dma((2 * GROUP,)), dma((GROUP,)), dma((GROUP,)),
            dma((GROUP,)), dma((GROUP,)), dma((3 * GROUP,)), dma((1 + 2 * GROUP,)),
            dma((7,)), dma((7,)), dma((3, GROUP)), dma((3, GROUP)),
            dma((2, GROUP, GROUP)), dma((2, GROUP, GROUP)), dma((2, 2)), dma((2, GROUP)),
            dma((2, 2, GROUP)), dma((2, 2, GROUP)),
        ],
        compiler_params=pltpu.CompilerParams(
            collective_id=6, has_side_effects=True, vmem_limit_bytes=62 * 2**20
        ),
    )(stream, cotangent, segment_ids, small, biases, head_pieces, up, down, out)


def local(
    stream, segment_ids, cotangent, ln1_gain, qkv_weight, qv_bias, out_weight, out_bias,
    ln2_gain, up_weight, up_bias, down_weight, down_bias,
):
    columns, token_count = stream.shape
    mp_count = lax.axis_size("mp")
    width = columns * mp_count
    do, di, mp = places()
    row, quarter = mp // 2, own_quarter(di, mp)
    heads_here = columns // HD
    scale = HD ** (-0.5)
    tokens = token_count // GROUP
    keep_local = ((mp * columns + lax.iota(jnp.int32, columns)) != width - 1)[:, None]
    last = (lax.iota(jnp.int32, width) == width - 1)[:, None]

    small = jnp.stack([jnp.concatenate([ln1_gain, ln2_gain, qv_bias[0], qv_bias[1]]), up_bias])
    small = jnp.pad(small, ((0, 6), (0, 0)))
    biases = jnp.pad(jnp.stack([out_bias, down_bias]), ((0, 6), (0, 0)))
    (
        mine, heads_out, heads_rest, qkv, lse, normed_one, smalls, head_weight, segs, stat, delta,
        grad_context, grad_norm_two, sums, *rest,
    ) = first_part(
        stream, cotangent, segment_ids, small, biases, qkv_weight, up_weight, down_weight,
        out_weight,
    )
    weight_grads = rest[:5]
    masked = jnp.where(keep_local, stream, 0.0)
    mixed_in, grad_in_local, qkv_grad, small, up_grad, down_grad, out_grad = backward_part(
        (
            grad_context, delta, mine, grad_norm_two, heads_out, heads_rest, qkv, lse, normed_one,
            smalls, head_weight, segs, stat, sums, *weight_grads,
        )
    )
    local_of = lambda blocks: blocks.transpose(1, 0, 2).reshape(columns, token_count).astype(F32)
    mixed = masked + local_of(mixed_in)
    stream_grad = jnp.where(keep_local, cotangent + local_of(grad_in_local), 0.0)
    qkv_grad = qkv_grad.transpose(0, 2, 1, 3).reshape(3, columns, width)
    up_grad, down_grad = [g.reshape(-1, width) for g in (up_grad, down_grad)]
    out_grad = out_grad.transpose(0, 2, 1, 3).reshape(columns, width)
    if lax.axis_size("blk") > 1:
        small, qkv_grad, up_grad, down_grad, out_grad = lax.psum(
            (small, qkv_grad, up_grad, down_grad, out_grad), "blk"
        )
    small = small[:, 0]
    shard = lambda values: lax.dynamic_slice_in_dim(values, mp * columns, columns, 0)
    at = lambda start, count: lax.dynamic_slice_in_dim(small, start, count, 0)
    return (
        mixed,
        stream_grad,
        shard(small[0]),
        qkv_grad,
        at(8 + 2 * mp, 2)[:, :columns],
        out_grad,
        small[2],
        shard(small[1]),
        up_grad,
        at(4 + mp, 1)[0],
        down_grad,
        small[3],
    )


def solution(mesh):
    rows, mp_count = mesh.shape["dp"], mesh.shape["mp"]
    pairs = Mesh(mesh.devices.reshape(rows // 8, 4, 2, mp_count), ALL)
    return jax.shard_map(
        local,
        mesh=pairs,
        in_specs=(
            P("mp", ROWS),
            P(ROWS, None),
            P("mp", ROWS),
            P("mp"),
            P(None, "mp", None),
            P(None, "mp"),
            P("mp", None),
            P(),
            P("mp"),
            P(None, "mp"),
            P("mp"),
            P("mp", None),
            P(),
        ),
        out_specs=(
            P("mp", ROWS),
            P("mp", ROWS),
            P("mp"),
            P(None, "mp", None),
            P(None, "mp"),
            P("mp", None),
            P(),
            P("mp"),
            P(None, "mp"),
            P("mp"),
            P("mp", None),
            P(),
        ),
        check_vma=False,
    )
```

```python
import functools

import jax
import jax.numpy as jnp
from jax import lax
from jax.experimental import pallas as pl
from jax.experimental.pallas import tpu as pltpu
from jax.sharding import Mesh, PartitionSpec as P

HD = 64
QB = 512
GROUP = 4
EPS = 1e-05
NEG = -1e30
MESH = pl.DeviceIdType.MESH
BF = jnp.bfloat16
F32 = jnp.float32
ALL = ("blk", "do", "di", "mp")
ROWS = ("blk", "do", "di")


def places():
    return lax.axis_index("do"), lax.axis_index("di"), lax.axis_index("mp")


def holder(row, quarter):
    return quarter // 2, 2 * row + lax.rem(quarter, 2)


def dev(do, di, mp):
    return (lax.axis_index("blk"), do, di, mp)


def flip(index, bit):
    return index + bit * (1 - 2 * lax.rem(index // bit, 2))


def remote(source, target, send, recv, device):
    return pltpu.make_async_remote_copy(
        source, target, send, recv, device_id=device, device_id_type=MESH
    )


def greet(others):
    barrier = pltpu.get_barrier_semaphore()
    for other in others:
        pl.semaphore_signal(barrier, inc=1, device_id=other, device_id_type=MESH)
    pl.semaphore_wait(barrier, len(others))


def neighbours(do, di, mp):
    column = [
        dev(do, lax.rem(di + a, 2), lax.rem(mp + b, GROUP))
        for a in range(2)
        for b in range(GROUP)
        if a or b
    ]
    return column + [dev(flip(do, 1), di, mp), dev(flip(do, 2), di, mp)]


def send_block(source, target, send, recv, place, target_place, do):
    (di, mp), (tdi, tmp) = place, target_place
    other = jnp.logical_or(tdi != di, tmp != mp)

    @pl.when(other)
    def _():
        remote(source, target, send, recv, dev(do, tdi, tmp)).start()

    @pl.when(jnp.logical_not(other))
    def _():
        pltpu.make_async_copy(source, target, recv).start()


def sent_block(source, target, send, recv, place, target_place, do):
    (di, mp), (tdi, tmp) = place, target_place
    other = jnp.logical_or(tdi != di, tmp != mp)

    @pl.when(other)
    def _():
        remote(source, target, send, recv, dev(do, tdi, tmp)).wait_send()


def piece_of(ref, do, di):
    rows, lanes = ref.shape[0] // GROUP, ref.shape[1] // 2
    return ref.at[
        pl.ds(pl.multiple_of(do * rows, rows), rows), pl.ds(pl.multiple_of(di * lanes, lanes), lanes)
    ]


def pieces_of(weight):
    return weight.reshape(GROUP, 2, weight.shape[0] // (2 * GROUP), weight.shape[1])


def dot_nt(left, right):
    return lax.dot_general(left, right, (((1,), (1,)), ((), ())), preferred_element_type=F32)


def dot_tn(left, right):
    return lax.dot_general(left, right, (((0,), (0,)), ((), ())), preferred_element_type=F32)


def add_pairs(count, target, first, second):
    def step(i, carry):
        ref = target(i)
        ref[...] = (first(i)[...].astype(F32) + second(i)[...].astype(F32)).astype(ref.dtype)
        return carry

    lax.fori_loop(0, count, step, 0)


def backward_kernel(
    gctx_ref, delta_ref, x_ref, gn2_ref, heads_ref, rest_ref, qkv_ref, lse_ref, normed_ref,
    smalls_ref, headw_ref, segs_ref, stat_ref, sums_ref, dup_ref, oup_ref, ddown_ref, odown_ref,
    dout_ref, stream_ref, cot_ref,
    small_out, mixed_ref, back_ref, qkvg_ref, up_out, down_out, out_out,
    s_ref, local_in, m_in, gall, k_tok, v_tok, causal, acc_k, acc_v, gj, acc_w, acc_b, gain_wide, acc_gain,
    part, near, total, far_buf, s_blocks,
    core_out, mine_up, mine_down, mine_out,
    one_up, one_down, one_out, two_up, two_down, two_out, z_up, z_down, z_out,
    fin_up, fin_down, fin_out, gq, q_one, q_two, q_z, q_fin, small_a, small_b, small_z,
    own_sem, b_send, b_recv, r_send, r_recv, send, recv,
):
    do, di, mp = places()
    width, tokens = x_ref.shape
    columns = heads_ref.shape[1]
    heads = columns // HD
    row, quarter, half = mp // 2, own_quarter(di, mp), lax.rem(mp, 2)
    place = (di, mp)
    sibling, across = dev(do, 1 - di, mp), dev(do, di, flip(mp, 1))
    posted, pending = [], []

    def prepare(source, target, device):
        n = len(posted)
        copy = remote(source, target, send.at[n], recv.at[n], device)
        posted.append(copy)
        pending.append(copy)
        return copy

    def post(source, target, device):
        copy = prepare(source, target, device)
        copy.start()
        return copy

    def finish(copy):
        copy.wait()
        pending[:] = [other for other in pending if other is not copy]

    def arrived(copies):
        for copy in copies:
            copy.wait_recv()

    def column(bit):
        return dev(flip(do, bit), di, mp)

    grads = (
        (dup_ref, mine_up, oup_ref, one_up, two_up, z_up, fin_up, up_out, 1, 2),
        (ddown_ref, mine_down, odown_ref, one_down, two_down, z_down, fin_down, down_out, 2, 1),
        (dout_ref, mine_out, core_out, one_out, two_out, z_out, fin_out, out_out, 1, 2),
    )
    own = []
    for i, g in enumerate(grads[:2]):
        for n, piece in enumerate((do, flip(do, g[9]))):
            own.append(pltpu.make_async_copy(g[0].at[piece], g[1].at[piece], own_sem.at[4 + 2 * i + n]))
        own.append(pltpu.make_async_copy(g[2], g[3], own_sem.at[8 + i]))
    own.append(pltpu.make_async_copy(dout_ref.at[:, di], mine_out, own_sem.at[2]))
    mixed_load = pltpu.make_async_copy(stream_ref, local_in, own_sem.at[10])
    mixed_load.start()
    for copy in own:
        copy.start()
    greet(neighbours(do, di, mp))

    swaps = []
    for k in range(GROUP):
        swaps.append(
            (
                gctx_ref.at[k], gall.at[quarter], b_send.at[k], b_recv.at[quarter], place,
                holder(row, k), do,
            )
        )
        send_block(*swaps[k])
    stage_core = [post(dout_ref.at[:, 1 - di], core_out, sibling)]

    def turn(step, carry):
        h, kb = step // GROUP, lax.rem(step, GROUP)
        rows = pl.ds(pl.multiple_of(columns + h * HD, HD), HD)
        k_tok[h, kb] = qkv_ref[kb, rows].T
        rows = pl.ds(pl.multiple_of(2 * columns + h * HD, HD), HD)
        v_tok[h, kb] = qkv_ref[kb, rows].T
        return carry

    lax.fori_loop(0, heads * GROUP, turn, 0)
    causal[...] = jnp.where(
        lax.broadcasted_iota(jnp.int32, causal.shape, 0)
        <= lax.broadcasted_iota(jnp.int32, causal.shape, 1),
        0.0, NEG,
    )
    for j in range(GROUP):
        turned = smalls_ref[j].T[:columns, 0:1]
        gain_wide[j * columns : (j + 1) * columns] = jnp.broadcast_to(turned, (columns, 128))
    acc_b[...] = jnp.zeros_like(acc_b)
    acc_w[...] = jnp.zeros_like(acc_w)
    segments = segs_ref[row]
    head_weight = headw_ref[...].reshape(3 * columns, width)
    def back_block(block):
        seg_q = segments[:, block * tokens : (block + 1) * tokens]
        masks = [
            jnp.where(segments[:, kb * tokens : kb * tokens + 1] == seg_q, 0.0, NEG)
            for kb in range(block)
        ]

        def one_head(h, carry):
            rows = pl.ds(pl.multiple_of(h * HD, HD), HD)
            k_rows = pl.ds(pl.multiple_of(columns + h * HD, HD), HD)
            query = qkv_ref[block, rows] * HD ** (-0.5)
            grad = gall[block, rows]
            mixed = heads_ref[block, rows].astype(F32) + rest_ref[block, rows].astype(F32)
            weighted = jnp.sum(grad.astype(F32) * mixed, axis=0, keepdims=True)
            lse = lse_ref[h, block, 0:1]
            grad_query = jnp.zeros((HD, tokens), F32)
            for kb in range(block + 1):
                raw = jnp.dot(k_tok[h, kb], query, preferred_element_type=F32)
                raw = raw + (causal[...] if kb == block else masks[kb])
                probs = jnp.exp(raw - lse)
                grad_probs = jnp.dot(v_tok[h, kb], grad, preferred_element_type=F32)
                grad_scores = (probs * (grad_probs - weighted)).astype(BF)
                grad_query += jnp.dot(qkv_ref[kb, k_rows], grad_scores, preferred_element_type=F32)
                key_term = dot_nt(query, grad_scores)
                value_term = dot_nt(grad, probs.astype(BF))
                if block == GROUP - 1:
                    acc_k[kb, rows] = key_term
                    acc_v[kb, rows] = value_term
                else:
                    acc_k[kb, rows] += key_term
                    acc_v[kb, rows] += value_term
            gj[rows] = (grad_query * HD ** (-0.5)).astype(BF)
            return carry

        lax.fori_loop(0, heads, one_head, 0)
        gj[columns : 2 * columns] = acc_k[block].astype(BF)
        gj[2 * columns :] = acc_v[block].astype(BF)
        part[block] = dot_tn(head_weight, gj[...])

    def near_args(i):
        return part.at[i], near.at[i % 2], r_send.at[i], r_recv.at[i], sibling

    def far_args(i):
        return total, far_buf, r_send.at[GROUP + i], r_recv.at[GROUP + i], across

    def to_sibling(i):
        @pl.when(di != i // 2)
        def _():
            remote(*near_args(i)).start()

    def across_row(i):
        @pl.when(di == i // 2)
        def _():
            remote(*near_args(i)).wait_recv()
            at = lambda k: pl.ds(pl.multiple_of(k * columns, columns), columns)
            add_pairs(
                GROUP,
                lambda k: near.at[i % 2, at(k)],
                lambda k: near.at[i % 2, at(k)],
                lambda k: part.at[i, at(k)],
            )

            @pl.when(half != i % 2)
            def _():
                total[...] = near[i % 2].astype(BF)
                remote(*far_args(i)).start()

    def weight_terms(block):
        acc_w[...] += dot_nt(gj[...], normed_ref[block])
        terms = gj[...].astype(F32)
        for k in range(tokens // 128):
            acc_b[: 3 * columns] += terms[:, k * 128 : (k + 1) * 128]

    def stage_one():
        arrived(stage_core)
        own[-1].wait()
        g = grads[2]
        add_pairs(
            GROUP * GROUP,
            lambda n: mine_out.at[n // GROUP, lax.rem(n, GROUP)],
            lambda n: mine_out.at[n // GROUP, lax.rem(n, GROUP)],
            lambda n: core_out.at[n // GROUP, lax.rem(n, GROUP)],
        )
        pieces = (flip(do, g[8]), flip(flip(do, g[8]), g[9]))
        return [post(mine_out.at[p], one_out.at[n], column(g[8])) for n, p in enumerate(pieces)]

    def stage_two(chosen):
        later = []
        for g in chosen:
            mine, one, first, second = g[1], g[3], g[8], g[9]
            for n, piece in ((1, flip(do, second)), (0, do)):
                add_pairs(
                    mine.shape[1], lambda k: mine.at[piece, k], lambda k: mine.at[piece, k],
                    lambda k: one.at[n, k],
                )
                if n == 1:
                    later.append(post(mine.at[piece], g[4], column(second)))
        return later

    def stage_three(copies, chosen):
        arrived(copies)
        later = []
        for g in chosen:
            mine, two, z_buf = g[1], g[4], g[5]
            add_pairs(
                mine.shape[1], lambda k: mine.at[do, k], lambda k: mine.at[do, k],
                lambda k: two.at[k],
            )
            for r in range(1, GROUP):
                later.append(
                    post(mine.at[do, r], z_buf.at[r - 1], dev(do, di, lax.rem(mp + r, GROUP)))
                )
        return later

    def result_of(i, piece):
        return grads[i][7].at[piece, di] if i < 2 else piece_of(out_out, piece, di)

    def stage_four(copies):
        arrived(copies)
        later = []
        for i, g in enumerate(grads):
            mine, z_buf, fin = g[1], g[5], g[6]
            fin[...] = (
                mine[do, 0].astype(F32) + z_buf[0].astype(F32)
                + z_buf[1].astype(F32) + z_buf[2].astype(F32)
            )
            target = result_of(i, do)
            pltpu.make_async_copy(fin, target, own_sem.at[i]).start()
            later.append(post(fin, target, column(g[8])))
        return later

    def stage_five(copies):
        arrived(copies)
        later = []
        for i, g in enumerate(grads):
            pltpu.make_async_copy(g[6], result_of(i, do), own_sem.at[i]).wait()
            for piece in (do, flip(do, g[8])):
                later.append(post(result_of(i, piece), result_of(i, piece), column(g[9])))
        return later

    def stage_six(copies):
        arrived(copies)
        halves = [g[7].at[:, di] for g in grads[:2]]
        lanes = out_out.shape[1] // 2
        halves.append(out_out.at[:, pl.ds(pl.multiple_of(di * lanes, lanes), lanes)])
        return [post(h, h, sibling) for h in halves]

    for copy in own[:-1]:
        copy.wait()
    copies = stage_two(grads[:2])
    not_last = jnp.logical_or(
        mp < GROUP - 1, lax.broadcasted_iota(jnp.int32, (columns, 128), 0) < columns - 1
    )

    def add_local(blocks):
        def step(n, carry):
            k, lane = n // (tokens // 128), lax.rem(n, tokens // 128)
            at = pl.ds(pl.multiple_of(n * 128, 128), 128)
            inner = pl.ds(pl.multiple_of(lane * 128, 128), 128)
            value = local_in[:, at] + blocks[k, :, inner].astype(F32)
            local_in[:, at] = jnp.where(not_last, value, 0.0)
            return carry

        lax.fori_loop(0, GROUP * (tokens // 128), step, 0)

    for k in range(GROUP):
        pltpu.make_async_copy(gctx_ref.at[k], gall.at[k], b_recv.at[k]).wait()
    for k in range(GROUP):
        swaps.append(
            (
                delta_ref.at[k], m_in.at[quarter], b_send.at[GROUP + k],
                b_recv.at[GROUP + quarter], place, (row, k), do,
            )
        )
        send_block(*swaps[GROUP + k])
    back_block(3)
    to_sibling(3)
    weight_terms(3)
    out_copies = stage_one()
    copies = stage_three(copies, grads[:2])
    back_block(2)
    to_sibling(2)
    across_row(3)
    weight_terms(2)
    arrived(out_copies)
    out_copies = stage_two(grads[2:])
    back_block(1)
    to_sibling(1)
    across_row(2)
    weight_terms(1)
    copies += stage_three(out_copies, grads[2:])
    for k in range(GROUP):
        pltpu.make_async_copy(delta_ref.at[k], m_in.at[k], b_recv.at[GROUP + k]).wait()
    mixed_load.wait()
    add_local(m_in)
    mixed_out = pltpu.make_async_copy(local_in, mixed_ref, own_sem.at[10])
    mixed_out.start()
    back_block(0)
    to_sibling(0)
    across_row(1)
    weight_terms(0)
    across_row(0)

    wide = width // 2
    sides = (pl.ds(0, wide), pl.ds(wide, wide))
    bits = ((1, 2), (2, 1))
    gq[...] = acc_w[...].astype(BF).reshape(gq.shape)
    q_copies = []
    for side, (first, second) in enumerate(bits):
        for n, piece in enumerate((flip(do, first), flip(flip(do, first), second))):
            q_copies.append(post(gq.at[piece, :, sides[side]], q_one.at[side, n], column(first)))

    @pl.when(half == 0)
    def _():
        for i in (0, 2):
            @pl.when(di == i // 2)
            def _():
                remote(*far_args(i)).wait_recv()

    @pl.when(half == 1)
    def _():
        for i in (1, 3):
            @pl.when(di == i // 2)
            def _():
                remote(*far_args(i)).wait_recv()

    acc_gain[...] = jnp.zeros_like(acc_gain)

    def norm_step(lane, carry):
        lanes = pl.ds(pl.multiple_of(lane * 128, 128), 128)
        values = x_ref[:, lanes]
        grad = near[half, :, lanes] + far_buf[:, lanes].astype(F32)
        row_sum, inverse = stat_ref[0:1, lanes], stat_ref[1:2, lanes]
        final = lax.broadcasted_iota(jnp.int32, (width, 128), 0) == width - 1
        recovered = jnp.where(final, -row_sum, values)
        scaled = grad * gain_wide[...]
        acc_gain[...] += grad * recovered * inverse
        dot_sum = jnp.sum(scaled * recovered, axis=0, keepdims=True)
        tail = scaled[width - 1 :]
        factor = dot_sum * (inverse * inverse * inverse) / width
        grad_in = inverse * (scaled - tail) - factor * (values + row_sum)
        grad_in = jnp.where(final, 0.0, grad_in) + gn2_ref[:, lanes].astype(F32)
        for j in range(GROUP):
            s_blocks[j, :, lanes] = grad_in[j * columns : (j + 1) * columns].astype(BF)
        return carry

    lax.fori_loop(0, tokens // 128, norm_step, 0)
    for k in range(GROUP):
        swaps.append(
            (
                s_blocks.at[k], s_ref.at[quarter], b_send.at[2 * GROUP + k],
                b_recv.at[2 * GROUP + quarter], place, (row, k), do,
            )
        )
        send_block(*swaps[2 * GROUP + k])
    mixed_out.wait()
    cot_load = pltpu.make_async_copy(cot_ref, local_in, own_sem.at[11])
    cot_load.start()

    small_a[...] = jnp.zeros_like(small_a)
    small_a[0] = jnp.sum(acc_gain[...].T, axis=0, keepdims=True)
    bias_row = jnp.sum(acc_b[...].T, axis=0, keepdims=True)
    for r in range(3):
        small_a[1 + r] = sums_ref[r]
    for r in range(GROUP):
        small_a[4 + lax.rem(mp + r, GROUP)] = sums_ref[3 + r]
    small_a[8 + 2 * quarter, :, :columns] = bias_row[:, :columns]
    small_a[9 + 2 * quarter, :, :columns] = bias_row[:, 2 * columns : 3 * columns]
    small_one = post(small_a, small_b.at[0], sibling)

    arrived(q_copies)
    copies = stage_four(copies)
    q_copies = []
    for side, (first, second) in enumerate(bits):
        for n, piece in ((1, flip(do, second)), (0, do)):
            gq[piece, :, sides[side]] = (
                gq[piece, :, sides[side]].astype(F32) + q_one[side, n].astype(F32)
            ).astype(BF)
            if n == 1:
                q_copies.append(post(gq.at[piece, :, sides[side]], q_two.at[side], column(second)))
    finish(small_one)
    small_a[...] += small_b[0]
    small_one = post(small_a, small_b.at[1], column(1))
    copies = stage_five(copies)
    arrived(q_copies)
    z_args = []
    for side in range(2):
        gq[do, :, sides[side]] = (
            gq[do, :, sides[side]].astype(F32) + q_two[side].astype(F32)
        ).astype(BF)
        z_args.append(
            (
                gq.at[do, :, sides[side]], q_z.at[row], b_send.at[3 * GROUP + side],
                b_recv.at[3 * GROUP + row], place, (side, quarter), do,
            )
        )
        send_block(*z_args[side])
    finish(small_one)
    small_a[...] += small_b[1]
    small_one = post(small_a, small_b.at[2], column(2))

    for r in range(2):
        pltpu.make_async_copy(q_z.at[r], q_z.at[r], b_recv.at[3 * GROUP + r]).wait()
    q_fin[...] = q_z[0].astype(F32) + q_z[1].astype(F32)

    def q_ref(piece, core):
        count = gq.shape[1]
        return qkvg_ref.at[
            pl.ds(pl.multiple_of(piece * count, count), count),
            pl.ds(pl.multiple_of(core * wide, wide), wide),
        ]

    q_own = pltpu.make_async_copy(q_fin, q_ref(do, di), own_sem.at[3])
    q_own.start()
    q_copies = [post(q_fin, q_ref(do, di), column(bit)) for bit in (1, 2)]
    finish(small_one)
    small_z[mp] = small_a[...] + small_b[2]
    small_copies = [
        post(small_z.at[mp], small_z.at[mp], dev(do, di, lax.rem(mp + r, GROUP)))
        for r in range(1, GROUP)
    ]
    copies = stage_six(copies)
    arrived(q_copies)

    q_last = prepare(q_ref(do, di), q_ref(do, di), sibling)
    n = len(posted) - 1

    @pl.when(di == 0)
    def _():
        piece = q_ref(flip(do, 1), di)
        remote(piece, piece, send.at[n], recv.at[n], column(2)).start()

    @pl.when(di == 1)
    def _():
        piece = q_ref(flip(do, 2), di)
        remote(piece, piece, send.at[n], recv.at[n], column(1)).start()

    q_own.wait()
    q_last.wait_recv()
    q_half = qkvg_ref.at[:, pl.ds(pl.multiple_of(di * wide, wide), wide)]
    q_copies = [post(q_half, q_half, sibling)]
    arrived(small_copies)
    small_out[...] = small_z[0] + small_z[1] + small_z[2] + small_z[3]
    arrived(q_copies)

    for k in range(GROUP):
        pltpu.make_async_copy(s_blocks.at[k], s_ref.at[k], b_recv.at[2 * GROUP + k]).wait()
    cot_load.wait()
    add_local(s_ref)
    back_out = pltpu.make_async_copy(local_in, back_ref, own_sem.at[11])
    back_out.start()
    for args in swaps + z_args:
        sent_block(*args)
    for i in range(GROUP):
        @pl.when(di != i // 2)
        def _():
            remote(*near_args(i)).wait_send()

        @pl.when(jnp.logical_and(di == i // 2, half != i % 2))
        def _():
            remote(*far_args(i)).wait_send()

    arrived(copies)
    for copy in pending:
        copy.wait_send()
    back_out.wait()


def backward_part(values):
    (
        grad_context, _, x_mine, grad_norm, heads_out, _, qkv, lse, normed, smalls,
        head_weight, segs, _, sums, up_grad, _, down_grad, _, out_grad, stream, _,
    ) = values
    columns, tokens = heads_out.shape[1:]
    width = x_mine.shape[0]
    heads = columns // HD
    shape = jax.ShapeDtypeStruct
    vmem, anywhere = pl.BlockSpec(memory_space=pltpu.VMEM), pl.BlockSpec(memory_space=pl.ANY)
    dma = pltpu.SemaphoreType.DMA
    slabs = (GROUP, columns, tokens)
    pieces = head_weight.shape[1]
    weight_grads = (up_grad, down_grad, out_grad)
    rows = [w.shape[-2:] for w in weight_grads]
    halves = [(GROUP, GROUP) + r for r in rows]
    buffers = (
        halves[2:]
        + halves
        + [(2, GROUP) + r for r in rows]
        + [(GROUP,) + r for r in rows]
        + [(GROUP - 1,) + r for r in rows]
    )
    return pl.pallas_call(
        backward_kernel,
        out_shape=[
            shape((16, 1, width), F32),
            shape(stream.shape, F32),
            shape(stream.shape, F32),
            shape((GROUP * pieces, width), F32),
        ]
        + [shape((GROUP, 2) + r, F32) for r in rows[:2]]
        + [shape((columns, width), F32)],
        in_specs=[vmem] * 14 + [anywhere] * 7,
        out_specs=[vmem] + [anywhere] * 6,
        scratch_shapes=[
            pltpu.VMEM(slabs, BF),
            pltpu.VMEM(stream.shape, F32),
            pltpu.VMEM(slabs, BF),
            pltpu.VMEM(slabs, BF),
            pltpu.VMEM((heads, GROUP, tokens, HD), BF),
            pltpu.VMEM((heads, GROUP, tokens, HD), BF),
            pltpu.VMEM((tokens, tokens), F32),
            pltpu.VMEM(slabs, F32),
            pltpu.VMEM(slabs, F32),
            pltpu.VMEM((3 * columns, tokens), BF),
            pltpu.VMEM((3 * columns, width), F32),
            pltpu.VMEM((640, 128), F32),
            pltpu.VMEM((width, 128), F32),
            pltpu.VMEM((width, 128), F32),
            pltpu.VMEM((GROUP, width, tokens), F32),
            pltpu.VMEM((2, width, tokens), F32),
            pltpu.VMEM((width, tokens), BF),
            pltpu.VMEM((width, tokens), BF),
            pltpu.VMEM(slabs, BF),
        ]
        + [pltpu.VMEM(b, BF) for b in buffers]
        + [pltpu.VMEM(r, F32) for r in rows]
        + [
            pltpu.VMEM((GROUP, pieces, width), BF),
            pltpu.VMEM((2, 2, pieces, width // 2), BF),
            pltpu.VMEM((2, pieces, width // 2), BF),
            pltpu.VMEM((2, pieces, width // 2), BF),
            pltpu.VMEM((pieces, width // 2), F32),
            pltpu.VMEM((16, 1, width), F32),
            pltpu.VMEM((3, 16, 1, width), F32),
            pltpu.VMEM((GROUP, 16, 1, width), F32),
            dma((12,)),
            dma((14,)),
            dma((14,)),
            dma((2 * GROUP,)),
            dma((2 * GROUP,)),
            dma((56,)),
            dma((56,)),
        ],
        compiler_params=pltpu.CompilerParams(
            collective_id=7, has_side_effects=True, vmem_limit_bytes=60 * 2**20
        ),
    )(*values)


def own_quarter(di, mp):
    return 2 * di + lax.rem(mp, 2)


def lane_chunks(count, step):
    lax.fori_loop(
        0, count, lambda i, c: (step(pl.ds(pl.multiple_of(i * 128, 128), 128)), c)[1], 0
    )


def xor(index, mask):
    for bit in (1, 2):
        if mask & bit:
            index = flip(index, bit)
    return index


def first_kernel(
    stream_ref, cot_ref, seg_ref, gain1_ref, gain2_ref, qv_ref, upb_ref, outb_ref, downb_ref,
    qkvw_ref, up_own, down_own, out_own,
    mine_ref, heads_ref, rest_ref, qkv_ref, lse_ref, normed_ref, smalls_ref, headw_ref, segs_ref,
    stat_ref, delta_ref, gctx_ref, gnorm_ref, sums_ref, mine_up, one_up, mine_down, one_down, dout_ref,
    up_all, down_all, out_all,
    grad_ref, context_ref, k_tokens, big, causal, wide_gain, back_gain, n2t, gyt,
    stats, x_more, g_more,
    w_up, w_down, w_out, d_up, d_down, n2, gy, pre, ghid, hidden, gpre, mlp, gn2, acc_gain,
    core_up, core_down,
    own_sem, in_sem, w_sem, x_send, x_recv, g_send, g_recv, c_send, c_recv, s_send, s_recv,
    st_send, st_recv, r_send, r_recv, h_send, h_recv, a_send, a_recv, t_send, t_recv, k_send, k_recv, o_send, o_recv,
):
    do, di, mp = places()
    width, tokens = normed_ref.shape[1], normed_ref.shape[2]
    columns = stream_ref.shape[0]
    heads_here = columns // HD
    lanes_count = tokens // 128
    row, quarter = mp // 2, own_quarter(di, mp)
    place = (di, mp)
    sibling, across = dev(do, 1 - di, mp), dev(do, di, flip(mp, 1))
    far = 2 * di + 1 - lax.rem(mp, 2)
    weights = ((up_own, up_all), (down_own, down_all), (out_own, out_all))
    final = lax.broadcasted_iota(jnp.int32, (width, 128), 0) == width - 1

    def column(bit):
        return dev(flip(do, bit), di, mp)

    loads = []
    for i, ref in enumerate((stream_ref, cot_ref)):
        for k in range(GROUP):
            loads.append(
                pltpu.make_async_copy(
                    ref.at[:, pl.ds(k * tokens, tokens)],
                    big.at[pl.ds(i * width + k * columns, columns)],
                    own_sem.at[2 + GROUP * i + k],
                )
            )
    own = [pltpu.make_async_copy(seg_ref, segs_ref.at[di], own_sem.at[1])]
    for copy in loads + own:
        copy.start()
    smalls_ref[mp] = jnp.zeros(smalls_ref.shape[1:], F32)
    smalls_ref[mp, 0:1, :columns] = gain1_ref[...]
    smalls_ref[mp, 1:2, :columns] = gain2_ref[...]
    smalls_ref[mp, 2:4, :columns] = qv_ref[...]
    smalls_ref[mp, 4:5] = upb_ref[...]
    greet(neighbours(do, di, mp))
    is_last = jnp.logical_and(
        mp == GROUP - 1, lax.broadcasted_iota(jnp.int32, (columns, tokens), 0) == columns - 1
    )

    def target_of(k):
        return k // 2, 2 * di + k % 2

    def rows_at(j):
        return pl.ds(pl.multiple_of(j * columns, 64), columns)

    def others():
        return [dev(do, di, lax.rem(mp + r, GROUP)) for r in range(1, GROUP)]

    def over_mp(i, r):
        ref, all_ref = weights[i]
        return remote(
            ref.at[do, di] if i < 2 else piece_of(ref, do, di), all_ref.at[do, di, r],
            a_send.at[i, r], a_recv.at[i, r], dev(do, di, lax.rem(mp + GROUP - r, GROUP)),
        )

    orders = ((1, 2), (2, 1))

    def hop(i, r, stage):
        all_ref = weights[i][1]
        first, second = orders[i]
        if stage == 3:
            ref = all_ref.at[:, di, r]
            return [remote(ref, ref, t_send.at[i, r, 3], t_recv.at[i, r, 3], sibling)]
        pieces = (do,) if stage == 1 else (do, flip(do, first))
        bit = first if stage == 1 else second
        copies = []
        for n, piece in enumerate(pieces):
            ref = all_ref.at[piece, di, r]
            at = stage - 1 + n
            copies.append(remote(ref, ref, t_send.at[i, r, at], t_recv.at[i, r, at], column(bit)))
        return copies

    def out_hop(stage):
        if stage == 3:
            ref = out_all.at[:, di, pl.ds(1, GROUP - 1)]
            return [remote(ref, ref, t_send.at[0, 0, 3], t_recv.at[0, 0, 3], sibling)]
        pieces = (do,) if stage == 1 else (do, flip(do, 1))
        copies = []
        for n, piece in enumerate(pieces):
            ref = out_all.at[piece, di, pl.ds(1, GROUP - 1)]
            at = stage - 1 + n
            copies.append(
                remote(ref, ref, t_send.at[0, 0, at], t_recv.at[0, 0, at], column(stage))
            )
        return copies

    def start(copies):
        for copy in copies:
            copy.start()

    def arrived(copies):
        for copy in copies:
            copy.wait_recv()

    def arrived_mp(r):
        arrived([over_mp(0, r), over_mp(1, r)])

    def both(r, stage):
        return hop(0, r, stage) + hop(1, r, stage)

    x_rest = [n2t.at[pl.ds(k * columns, columns)] for k in range(GROUP)]
    g_rest = [gnorm_ref.at[pl.ds(k * columns, columns)] for k in range(GROUP)]

    for k in range(GROUP):
        loads[k].wait()
        rows_k = pl.ds(k * columns, columns)
        part = jnp.where(is_last, 0.0, big[rows_k])
        big[rows_k] = part
        stats[mp, k, 0:1] = jnp.sum(part, axis=0, keepdims=True)
        stats[mp, k, 1:2] = jnp.sum(part * part, axis=0, keepdims=True)
    sums_over = [
        remote(stats.at[mp], stats.at[mp], st_send.at[r], st_recv.at[GROUP - r - 1], other)
        for r, other in zip(range(GROUP - 1), others())
    ]
    for copy in sums_over:
        copy.start()
    smalls = []
    for r in range(1, GROUP):
        target = dev(do, di, lax.rem(mp + r, GROUP))
        smalls.append(
            remote(smalls_ref.at[mp], smalls_ref.at[mp], s_send.at[r], s_recv.at[GROUP - r], target)
        )
    smalls.append(remote(seg_ref, segs_ref.at[di], s_send.at[0], s_recv.at[0], sibling))
    for copy in smalls:
        copy.start()
    own_gain = smalls_ref[mp].T[:columns, 0:1]
    for copy in sums_over:
        copy.wait_recv()
    x_args, stat_args, x_rest_args = [], [], []
    for k in range(GROUP):
        row_sum = stats[0, k, 0:1] + stats[1, k, 0:1] + stats[2, k, 0:1] + stats[3, k, 0:1]
        squares = stats[0, k, 1:2] + stats[1, k, 1:2] + stats[2, k, 1:2] + stats[3, k, 1:2]
        mean = (squares + row_sum * row_sum) / width + EPS
        inverse = lax.rsqrt(mean)
        stats[GROUP, k, 0:1] = row_sum
        stats[GROUP, k, 1:2] = inverse
        stats[GROUP, k, 2:3] = 1.0 / inverse
        values = big[k * columns : (k + 1) * columns]
        recovered = jnp.where(is_last, -row_sum, values)
        normed = (recovered * inverse * own_gain).astype(BF)
        delta_ref[k] = normed
        x_args.append(
            (
                delta_ref.at[k], normed_ref.at[k, rows_at(mp)], x_send.at[k], x_recv.at[mp],
                place, target_of(k), do,
            )
        )
        send_block(*x_args[k])
        near = (normed.astype(F32) * (1.0 / own_gain)) * stats[GROUP, k, 2:3]
        x_rest[k][...] = jnp.where(is_last, 0.0, values - near).astype(BF)
        stat_args.append(
            (stats.at[GROUP, k], stat_ref, r_send.at[k], r_recv.at[0], place, target_of(k), do)
        )
        x_rest_args.append(
            (
                x_rest[k], x_more.at[mp], r_send.at[GROUP + k], r_recv.at[1 + mp],
                place, target_of(k), do,
            )
        )

    @pl.when(mp == 0)
    def _():
        for args in stat_args:
            send_block(*args)

    head_target = (mp // 2, lax.rem(mp, 2) + 2 * di)
    head_args = (
        qkvw_ref.at[do], headw_ref.at[do], h_send.at[0], h_recv.at[0], place, head_target, do,
    )
    send_block(*head_args)

    gathers = []
    for k in range(GROUP):
        j = xor(mp, k)
        part = normed_ref.at[quarter, rows_at(j)]
        pltpu.make_async_copy(part, part, x_recv.at[j]).wait()
        for lane, other in enumerate((across, sibling)):
            copy = remote(part, part, g_send.at[lane, k], g_recv.at[lane, k], other)
            copy.start()
            gathers.append(copy)

    start([over_mp(2, r) for r in range(1, GROUP)])
    start([over_mp(i, r) for r in (1, 2) for i in range(2)])

    pltpu.make_async_copy(qkvw_ref.at[do], headw_ref.at[do], h_recv.at[0]).wait()
    cut = 80
    part_a, part_b = pl.ds(0, cut), pl.ds(cut, headw_ref.shape[1] - cut)
    heads = []

    def head_copy(piece, part, bit):
        ref = headw_ref.at[piece, part]
        n = len(heads) + 1
        copy = remote(ref, ref, h_send.at[n], h_recv.at[n], column(bit))
        copy.start()
        heads.append(copy)

    head_copy(do, part_a, 1)
    head_copy(do, part_b, 2)

    arrived(smalls)
    for copy in own:
        copy.wait()
    for j in range(GROUP):
        turned = smalls_ref[j].T
        at = slice(j * columns, (j + 1) * columns)
        back_gain[at] = jnp.broadcast_to(1.0 / turned[:columns, 0:1], (columns, 128))
        wide_gain[at] = jnp.broadcast_to(turned[:columns, 1:2], (columns, 128))
    biases = smalls_ref[quarter].T
    query_bias, value_bias = biases[:columns, 2:3], biases[:columns, 3:4]
    causal[...] = jnp.where(
        lax.broadcasted_iota(jnp.int32, causal.shape, 0)
        <= lax.broadcasted_iota(jnp.int32, causal.shape, 1),
        0.0, NEG,
    )
    for k in range(GROUP):
        loads[GROUP + k].wait()
        part = jnp.where(is_last, 0.0, big[width + k * columns : width + (k + 1) * columns])
        gctx_ref[k] = part.astype(BF)
        g_rest[k][...] = (part - gctx_ref[k].astype(F32)).astype(BF)
    arrived(heads[:2])
    head_copy(do, part_a, 2)
    head_copy(flip(do, 1), part_a, 2)
    head_copy(do, part_b, 1)
    head_copy(flip(do, 2), part_b, 1)
    for k in range(GROUP):
        gathers[2 * k].wait_recv()
        part = normed_ref.at[far, rows_at(xor(mp, 1 ^ k))]
        copy = remote(part, part, g_send.at[2, k], g_recv.at[2, k], sibling)
        copy.start()
        gathers.append(copy)
    for k in range(GROUP):
        gathers[2 * k + 1].wait_recv()
        gathers[2 * GROUP + k].wait_recv()
    arrived(heads[2:])
    cot_args = [
        (gctx_ref.at[k], grad_ref.at[mp], c_send.at[k], c_recv.at[mp], place, target_of(k), do)
        for k in range(GROUP)
    ]
    for args in x_rest_args:
        send_block(*args)
    arrived([over_mp(2, r) for r in range(1, GROUP)])
    start(out_hop(1))
    arrived_mp(1)
    start(both(1, 1))
    g_rest_args = [
        (
            g_rest[k], g_more.at[mp], r_send.at[2 * GROUP + k], r_recv.at[1 + GROUP + mp],
            place, target_of(k), do,
        )
        for k in range(GROUP)
    ]
    head_weight = headw_ref[...].reshape(3 * columns, width)

    def project(block, carry):
        joined = jnp.dot(head_weight, normed_ref[block], preferred_element_type=F32)
        qkv_ref[block, :columns] = (joined[:columns] + query_bias).astype(BF)
        keys = joined[columns : 2 * columns].astype(BF)
        qkv_ref[block, columns : 2 * columns] = keys
        qkv_ref[block, 2 * columns :] = (joined[2 * columns :] + value_bias).astype(BF)
        for h in range(heads_here):
            k_tokens[h, block] = keys[h * HD : (h + 1) * HD].T
        return carry

    lax.fori_loop(0, GROUP, project, 0)
    segments = segs_ref[row]

    def attend(block):
        seg_q = segments[:, block * tokens : (block + 1) * tokens]
        masks = [
            jnp.where(segments[:, kb * tokens : kb * tokens + 1] == seg_q, 0.0, NEG)
            for kb in range(block)
        ]

        def one_head(h, carry):
            rows = pl.ds(pl.multiple_of(h * HD, HD), HD)
            v_rows = pl.ds(pl.multiple_of(2 * columns + h * HD, HD), HD)
            query = qkv_ref[block, rows] * HD ** (-0.5)
            top = None
            for kb in range(block + 1):
                raw = jnp.dot(k_tokens[h, kb], query, preferred_element_type=F32)
                raw = raw + (causal[...] if kb == block else masks[kb])
                big[kb * tokens : (kb + 1) * tokens] = raw
                high = jnp.max(raw, axis=0, keepdims=True)
                top = high if top is None else jnp.maximum(top, high)
            total = jnp.zeros((1, tokens), F32)
            for kb in range(block + 1):
                expo = jnp.exp(big[kb * tokens : (kb + 1) * tokens] - top)
                big[kb * tokens : (kb + 1) * tokens] = expo
                total += jnp.sum(expo, axis=0, keepdims=True)
            portion = 1.0 / total
            mixed = jnp.zeros((HD, tokens), F32)
            for kb in range(block + 1):
                probs = (big[kb * tokens : (kb + 1) * tokens] * portion).astype(BF)
                mixed += jnp.dot(qkv_ref[kb, v_rows], probs, preferred_element_type=F32)
            rounded = mixed.astype(BF)
            heads_ref[block, rows] = rounded
            rest_ref[block, rows] = (mixed - rounded.astype(F32)).astype(BF)
            lse_ref[h, block] = jnp.broadcast_to(top + jnp.log(total), (8, tokens))
            return carry

        lax.fori_loop(0, heads_here, one_head, 0)

    context_args = [
        (
            heads_ref.at[block], context_ref.at[quarter], c_send.at[GROUP + block],
            c_recv.at[GROUP + quarter], place, holder(row, block), do,
        )
        for block in range(GROUP)
    ]

    attend(0)
    send_block(*context_args[0])
    for args in cot_args:
        send_block(*args)
    arrived(out_hop(1))
    start(out_hop(2))
    arrived_mp(2)
    start(both(2, 1))
    arrived(both(1, 1))
    start(both(1, 2))
    attend(1)
    send_block(*context_args[1])
    start([over_mp(i, 3) for i in range(2)])
    attend(2)
    send_block(*context_args[2])
    arrived(out_hop(2))
    start(out_hop(3))
    arrived(both(1, 2))
    start(both(1, 3))
    arrived(both(2, 1))
    start(both(2, 2))
    attend(3)
    send_block(*context_args[3])
    arrived(both(2, 2))
    start(both(2, 3))
    for args in g_rest_args:
        send_block(*args)

    attn, middle = big.at[pl.ds(0, width)], big.at[pl.ds(width, width)]
    own_weights = [
        pltpu.make_async_copy(ref, buf.at[0], in_sem.at[i, 0])
        for i, (ref, buf) in enumerate(((up_own, w_up), (down_own, w_down)))
    ]

    def fetch(r, slot):
        return [
            pltpu.make_async_copy(ref.at[:, :, r], buf.at[slot], in_sem.at[i, slot])
            for i, (ref, buf) in enumerate(((up_all, w_up), (down_all, w_down)))
        ]

    start(own_weights)
    rows, lanes = columns // GROUP, width // 2
    arrived(out_hop(3))
    out_loads = [pltpu.make_async_copy(out_own, w_out.at[mp], w_sem.at[0])]
    for r in range(1, GROUP):
        shard = lax.rem(mp + r, GROUP)
        for piece in range(GROUP):
            for side in range(2):
                out_loads.append(
                    pltpu.make_async_copy(
                        out_all.at[piece, side, r],
                        w_out.at[shard, pl.ds(piece * rows, rows), pl.ds(side * lanes, lanes)],
                        w_sem.at[(r * GROUP + piece) * 2 + side],
                    )
                )
    start(out_loads)
    out_bias = jnp.broadcast_to(outb_ref[...], (8, width)).T[:, 0:1]
    def cotangent_at(at):
        return grad_ref[:, :, at].reshape(width, 128).astype(F32)

    def centre_grad(at):
        grad = cotangent_at(at)
        gyt[:, at] = (grad - jnp.sum(grad, axis=0, keepdims=True) / width).astype(BF)

    for copy in out_loads:
        copy.wait()
    for k in range(GROUP):
        pltpu.make_async_copy(heads_ref.at[k], context_ref.at[k], c_recv.at[GROUP + k]).wait()
    pltpu.make_async_copy(stat_ref, stat_ref, r_recv.at[0]).wait()
    for k in range(GROUP):
        pltpu.make_async_copy(x_more.at[k], x_more.at[k], r_recv.at[1 + k]).wait()
    projected = dot_tn(w_out[0], context_ref[0])
    for s in range(1, GROUP):
        projected += dot_tn(w_out[s], context_ref[s])
    attn[...] = projected + out_bias

    def norm(at):
        values = attn[:, at]
        values = values - jnp.sum(values, axis=0, keepdims=True) / width
        values = jnp.where(final, 0.0, values)
        attn[:, at] = values
        mine = (normed_ref[quarter, :, at].astype(F32) * back_gain[...]) * stat_ref[2:3, at]
        mine = mine + x_more[:, :, at].reshape(width, 128).astype(F32)
        mine = jnp.where(final, 0.0, mine)
        mine_ref[:, at] = mine
        values = values + mine
        middle[:, at] = values
        row_sum = jnp.sum(values, axis=0, keepdims=True)
        square_sum = jnp.sum(values * values, axis=0, keepdims=True)
        inverse = lax.rsqrt((square_sum + row_sum * row_sum) / width + EPS)
        recovered = jnp.where(final, -row_sum, values)
        n2t[:, at] = (recovered * inverse * wide_gain[...]).astype(BF)

    for args in x_rest_args:
        sent_block(*args)
    lane_chunks(lanes_count, norm)
    n2[...] = n2t[...].T
    for k in range(GROUP):
        pltpu.make_async_copy(grad_ref.at[k], grad_ref.at[k], c_recv.at[k]).wait()

    lane_chunks(lanes_count, centre_grad)
    gy[...] = gyt[...].T
    sums_ref[2] = jnp.sum(gy[...].astype(F32), axis=0, keepdims=True)
    arrived_mp(GROUP - 1)
    start(both(GROUP - 1, 1))
    grads = (
        (d_up, core_up, mine_up, one_up, 1, 2),
        (d_down, core_down, mine_down, one_down, 2, 1),
    )

    def to_sibling(r, slot):
        return [
            remote(g[0].at[slot, :, 1 - di], g[1].at[r], k_send.at[i, slot], k_recv.at[i, r], sibling)
            for i, g in enumerate(grads)
        ]

    def to_column(r):
        copies = []
        for i, g in enumerate(grads):
            first, second = g[4], g[5]
            for n, piece in enumerate((flip(do, first), flip(flip(do, first), second))):
                copies.append(
                    remote(
                        g[2].at[piece, r], g[3].at[n, r], o_send.at[i, n, r], o_recv.at[i, n, r],
                        column(first),
                    )
                )
        return copies

    def combine(r, slot):
        for copy in to_sibling(r, slot):
            copy.wait()
        for g in grads:
            add_pairs(
                GROUP, lambda k: g[2].at[k, r], lambda k: g[0].at[slot, k, di], lambda k: g[1].at[r, k]
            )
        start(to_column(r))

    chunk = 64
    root = 0.7978845608028654

    def shard_step(r, carry):
        slot = lax.rem(r, 2)
        for copy in fetch(r, slot):
            copy.wait()

        @pl.when(r < GROUP - 1)
        def _():
            arrived(both(r + 1, 3))
            start(fetch(r + 1, 1 - slot))

        up = w_up[slot].reshape(width, width)
        down = w_down[slot].reshape(width, width)
        bias = smalls_ref[lax.rem(mp + r, GROUP), 4:5]
        pre[...] = jnp.dot(n2[...], up, preferred_element_type=F32) + bias
        ghid[...] = dot_nt(gy[...], down)

        for step in (0, 1):

            @pl.when(r == step)
            def _():
                arrived(both(GROUP - 1, 1 + step))
                start(both(GROUP - 1, 2 + step))

        def gelu(i, carry):
            at = pl.ds(pl.multiple_of(i * chunk, chunk), chunk)
            p = pre[at]
            square = p * p
            t = jnp.tanh(root * (p + 0.044715 * (p * square)))
            half = 0.5 * (1.0 + t)
            hidden[at] = (p * half).astype(BF)
            slope = half + 0.5 * p * (1.0 - t * t) * (root * (1.0 + 3 * 0.044715 * square))
            gpre[at] = (ghid[at] * slope).astype(BF)
            return carry

        lax.fori_loop(0, tokens // chunk, gelu, 0)

        @pl.when(r >= 1)
        def _():
            combine(r - 1, 1 - slot)

        d_down[slot] = dot_tn(hidden[...], gy[...]).astype(BF).reshape(d_down.shape[1:])
        d_up[slot] = (
            jnp.dot(n2t[...], gpre[...], preferred_element_type=F32)
            .astype(BF)
            .reshape(d_up.shape[1:])
        )
        start(to_sibling(r, slot))
        sums_ref[3 + r] = jnp.sum(gpre[...].astype(F32), axis=0, keepdims=True)
        more_mlp = jnp.dot(hidden[...], down, preferred_element_type=F32)
        more_grad = dot_nt(gpre[...], up)

        @pl.when(r == 0)
        def _():
            mlp[...] = more_mlp
            gn2[...] = more_grad

        @pl.when(r > 0)
        def _():
            mlp[...] += more_mlp
            gn2[...] += more_grad

        return carry

    lax.fori_loop(0, GROUP, shard_step, 0)
    combine(GROUP - 1, (GROUP - 1) % 2)
    for args in x_args:
        sent_block(*args)
    mlp_y = mlp[...] + downb_ref[...]
    pre[...] = mlp_y - jnp.sum(mlp_y, axis=1, keepdims=True) / width

    def mixed_delta(at):
        delta = attn[:, at] + jnp.where(final, 0.0, pre[at].T)
        for j in range(GROUP):
            delta_ref[j, :, at] = delta[j * columns : (j + 1) * columns].astype(BF)

    lane_chunks(lanes_count, mixed_delta)
    acc_gain[...] = jnp.zeros_like(acc_gain)
    gat = gyt
    for args in cot_args + g_rest_args:
        sent_block(*args)
    for k in range(GROUP):
        pltpu.make_async_copy(g_more.at[k], g_more.at[k], r_recv.at[1 + GROUP + k]).wait()

    def back(at):
        grad = gn2[at].T
        values = middle[:, at]
        row_sum = jnp.sum(values, axis=0, keepdims=True)
        square_sum = jnp.sum(values * values, axis=0, keepdims=True)
        inverse = lax.rsqrt((square_sum + row_sum * row_sum) / width + EPS)
        recovered = jnp.where(final, -row_sum, values)
        acc_gain[...] += grad * recovered * inverse
        scaled = grad * wide_gain[...]
        dot_sum = jnp.sum(scaled * recovered, axis=0, keepdims=True)
        tail = scaled[width - 1 :]
        factor = dot_sum * (inverse * inverse * inverse) / width
        grad_in = inverse * (scaled - tail) - factor * (values + row_sum)
        grad_in = jnp.where(final, 0.0, grad_in)
        gnorm_ref[:, at] = grad_in.astype(BF)
        more = g_more[:, :, at].reshape(width, 128).astype(F32)
        grad_z = jnp.where(final, 0.0, (cotangent_at(at) + more) + grad_in)
        grad_z = grad_z.astype(BF).astype(F32)
        gat[:, at] = (grad_z - jnp.sum(grad_z, axis=0, keepdims=True) / width).astype(BF)

    lane_chunks(lanes_count, back)
    sums_ref[0] = jnp.sum(acc_gain[...].T, axis=0, keepdims=True)
    sums_ref[1] = dot_nt(jnp.ones((8, tokens), BF), gat[...])[:1]
    sums_ref[7] = jnp.zeros_like(sums_ref[7])
    for s in range(GROUP):
        gctx_ref[s] = jnp.dot(w_out[s], gat[...], preferred_element_type=F32).astype(BF)
        terms = dot_nt(context_ref[s], gat[...]).astype(BF)
        for side in range(2):
            dout_ref[:, side, lax.rem(s + GROUP - mp, GROUP)] = terms[
                :, side * lanes : (side + 1) * lanes
            ].reshape(GROUP, rows, lanes)
    sent_block(*head_args)
    for args in context_args:
        sent_block(*args)

    @pl.when(mp == 0)
    def _():
        for args in stat_args:
            sent_block(*args)

    sent = gathers + smalls + heads + sums_over
    for r in range(1, GROUP):
        sent += [over_mp(i, r) for i in range(3)]
        for stage in (1, 2, 3):
            sent += both(r, stage)
    for stage in (1, 2, 3):
        sent += out_hop(stage)
    for copy in sent:
        copy.wait_send()
    for r in range(GROUP):
        for copy in to_column(r):
            copy.wait()


def first_part(stream, cotangent, segment_ids, smalls, qkv_weight, up, down, out):
    columns, token_count = stream.shape
    width, tokens = columns * GROUP, token_count // GROUP
    heads = columns // HD
    shape = jax.ShapeDtypeStruct
    vmem, anywhere = pl.BlockSpec(memory_space=pltpu.VMEM), pl.BlockSpec(memory_space=pl.ANY)
    dma = pltpu.SemaphoreType.DMA
    up, down = pieces_of(up), pieces_of(down)
    head_pieces = qkv_weight.reshape(GROUP, 3 * columns // GROUP, width)
    slabs = (GROUP, columns, tokens)
    rows = up.shape[2:]
    out_rows = (columns // GROUP, width // 2)
    part, half = (2,) + up.shape, (GROUP, GROUP) + rows
    bf = lambda *dims: pltpu.VMEM(dims, BF)
    fl = lambda *dims: pltpu.VMEM(dims, F32)
    return pl.pallas_call(
        first_kernel,
        out_shape=[
            shape((width, tokens), F32),
            shape(slabs, BF),
            shape(slabs, BF),
            shape((GROUP, 3 * columns, tokens), BF),
            shape((heads, GROUP, 8, tokens), F32),
            shape((GROUP, width, tokens), BF),
            shape((GROUP, 8, width), F32),
            shape(head_pieces.shape, BF),
            shape((2, 1, token_count), jnp.int32),
            shape((8, tokens), F32),
            shape(slabs, BF),
            shape(slabs, BF),
            shape((width, tokens), BF),
            shape((8, 1, width), F32),
        ]
        + [shape(half, BF), shape((2,) + half[1:], BF)] * 2
        + [shape((GROUP, 2, GROUP) + out_rows, BF)]
        + [shape((GROUP, 2, GROUP) + p, BF) for p in (rows, rows, out_rows)],
        in_specs=[anywhere] * 2 + [vmem] * 7 + [anywhere] * 4,
        out_specs=[vmem] * 19 + [anywhere] * 3,
        scratch_shapes=[
            bf(*slabs), bf(*slabs), bf(heads, GROUP, tokens, HD),
            fl(token_count, tokens), fl(tokens, tokens), fl(width, 128), fl(width, 128),
            bf(width, tokens), bf(width, tokens), fl(GROUP + 1, GROUP, 8, tokens),
            bf(*slabs), bf(*slabs),
            bf(*part), bf(*part), bf(GROUP, columns, width), bf(*part), bf(*part),
            bf(tokens, width), bf(tokens, width), fl(tokens, width), fl(tokens, width),
            bf(tokens, width), bf(tokens, width), fl(tokens, width), fl(tokens, width),
            fl(width, 128), bf(*half), bf(*half),
            dma((10,)), dma((2, 2)), dma((2 * GROUP * GROUP,)),
            dma((GROUP,)), dma((GROUP,)), dma((3, GROUP)), dma((3, GROUP)),
            dma((2 * GROUP,)), dma((2 * GROUP,)), dma((GROUP,)), dma((GROUP,)),
            dma((GROUP,)), dma((GROUP,)), dma((4 * GROUP,)), dma((1 + 3 * GROUP,)),
            dma((7,)), dma((7,)), dma((3, GROUP)), dma((3, GROUP)),
            dma((2, GROUP, GROUP)), dma((2, GROUP, GROUP)), dma((2, 2)), dma((2, GROUP)),
            dma((2, 2, GROUP)), dma((2, 2, GROUP)),
        ],
        compiler_params=pltpu.CompilerParams(
            collective_id=6, has_side_effects=True, vmem_limit_bytes=62 * 2**20
        ),
    )(stream, cotangent, segment_ids, *smalls, head_pieces, up, down, out)


def local(
    stream, segment_ids, cotangent, ln1_gain, qkv_weight, qv_bias, out_weight, out_bias,
    ln2_gain, up_weight, up_bias, down_weight, down_bias,
):
    columns = stream.shape[0]
    mp = lax.axis_index("mp")
    smalls_in = [
        ln1_gain[None], ln2_gain[None], qv_bias, up_bias[None], out_bias[None], down_bias[None]
    ]
    (
        mine, heads_out, heads_rest, qkv, lse, normed_one, smalls, head_weight, segs, stat,
        delta, grad_context, grad_norm_two, sums, *rest,
    ) = first_part(
        stream, cotangent, segment_ids, smalls_in, qkv_weight, up_weight, down_weight, out_weight
    )
    weight_grads = rest[:5]
    small, mixed, stream_grad, qkv_grad, up_grad, down_grad, out_grad = backward_part(
        (
            grad_context, delta, mine, grad_norm_two, heads_out, heads_rest, qkv, lse, normed_one,
            smalls, head_weight, segs, stat, sums, *weight_grads, stream, cotangent,
        )
    )
    width = small.shape[-1]
    qkv_grad = qkv_grad.reshape(3, columns, width)
    up_grad, down_grad = [g.reshape(-1, width) for g in (up_grad, down_grad)]
    if lax.axis_size("blk") > 1:
        small, qkv_grad, up_grad, down_grad, out_grad = lax.psum(
            (small, qkv_grad, up_grad, down_grad, out_grad), "blk"
        )
    small = small[:, 0]
    shard = lambda values: lax.dynamic_slice_in_dim(values, mp * columns, columns, 0)
    at = lambda start, count: lax.dynamic_slice_in_dim(small, start, count, 0)
    return (
        mixed,
        stream_grad,
        shard(small[0]),
        qkv_grad,
        at(8 + 2 * mp, 2)[:, :columns],
        out_grad,
        small[2],
        shard(small[1]),
        up_grad,
        at(4 + mp, 1)[0],
        down_grad,
        small[3],
    )


def solution(mesh):
    rows, mp_count = mesh.shape["dp"], mesh.shape["mp"]
    pairs = Mesh(mesh.devices.reshape(rows // 8, 4, 2, mp_count), ALL)
    return jax.shard_map(
        local,
        mesh=pairs,
        in_specs=(
            P("mp", ROWS),
            P(ROWS, None),
            P("mp", ROWS),
            P("mp"),
            P(None, "mp", None),
            P(None, "mp"),
            P("mp", None),
            P(),
            P("mp"),
            P(None, "mp"),
            P("mp"),
            P("mp", None),
            P(),
        ),
        out_specs=(
            P("mp", ROWS),
            P("mp", ROWS),
            P("mp"),
            P(None, "mp", None),
            P(None, "mp"),
            P("mp", None),
            P(),
            P("mp"),
            P(None, "mp"),
            P("mp"),
            P("mp", None),
            P(),
        ),
        check_vma=False,
    )
```

```python
import functools

import jax
import jax.numpy as jnp
from jax import lax
from jax.experimental import pallas as pl
from jax.experimental.pallas import tpu as pltpu
from jax.sharding import Mesh, PartitionSpec as P

HD = 64
QB = 512
GROUP = 4
EPS = 1e-05
NEG = -1e30
MESH = pl.DeviceIdType.MESH
BF = jnp.bfloat16
F32 = jnp.float32
ALL = ("blk", "do", "di", "mp")
ROWS = ("blk", "do", "di")


def places():
    return lax.axis_index("do"), lax.axis_index("di"), lax.axis_index("mp")


def holder(row, quarter):
    return quarter // 2, 2 * row + lax.rem(quarter, 2)


def dev(do, di, mp):
    return (lax.axis_index("blk"), do, di, mp)


def flip(index, bit):
    return index + bit * (1 - 2 * lax.rem(index // bit, 2))


def remote(source, target, send, recv, device):
    return pltpu.make_async_remote_copy(
        source, target, send, recv, device_id=device, device_id_type=MESH
    )


def greet(others):
    barrier = pltpu.get_barrier_semaphore()
    for other in others:
        pl.semaphore_signal(barrier, inc=1, device_id=other, device_id_type=MESH)
    pl.semaphore_wait(barrier, len(others))


def neighbours(do, di, mp):
    column = [
        dev(do, lax.rem(di + a, 2), lax.rem(mp + b, GROUP))
        for a in range(2)
        for b in range(GROUP)
        if a or b
    ]
    return column + [dev(flip(do, 1), di, mp), dev(flip(do, 2), di, mp)]


def send_block(source, target, send, recv, place, target_place, do):
    (di, mp), (tdi, tmp) = place, target_place
    other = jnp.logical_or(tdi != di, tmp != mp)

    @pl.when(other)
    def _():
        remote(source, target, send, recv, dev(do, tdi, tmp)).start()

    @pl.when(jnp.logical_not(other))
    def _():
        pltpu.make_async_copy(source, target, recv).start()


def sent_block(source, target, send, recv, place, target_place, do):
    (di, mp), (tdi, tmp) = place, target_place
    other = jnp.logical_or(tdi != di, tmp != mp)

    @pl.when(other)
    def _():
        remote(source, target, send, recv, dev(do, tdi, tmp)).wait_send()


def piece_of(ref, do, di):
    rows, lanes = ref.shape[0] // GROUP, ref.shape[1] // 2
    return ref.at[
        pl.ds(pl.multiple_of(do * rows, rows), rows), pl.ds(pl.multiple_of(di * lanes, lanes), lanes)
    ]


def pieces_of(weight):
    return weight.reshape(GROUP, 2, weight.shape[0] // (2 * GROUP), weight.shape[1])


def dot_nt(left, right):
    return lax.dot_general(left, right, (((1,), (1,)), ((), ())), preferred_element_type=F32)


def dot_tn(left, right):
    return lax.dot_general(left, right, (((0,), (0,)), ((), ())), preferred_element_type=F32)


def add_pairs(count, target, first, second):
    def step(i, carry):
        ref = target(i)
        ref[...] = (first(i)[...].astype(F32) + second(i)[...].astype(F32)).astype(ref.dtype)
        return carry

    lax.fori_loop(0, count, step, 0)


def backward_kernel(
    gctx_ref, delta_ref, x_ref, gn2_ref, heads_ref, rest_ref, qkv_ref, lse_ref, normed_ref,
    smalls_ref, headw_ref, segs_ref, stat_ref, sums_ref, dup_ref, oup_ref, ddown_ref, odown_ref,
    dout_ref, stream_ref, cot_ref,
    small_out, mixed_ref, back_ref, qkvg_ref, up_out, down_out, out_out,
    s_ref, local_in, m_in, gall, k_tok, v_tok, causal, acc_k, acc_v, gj, acc_w, acc_b, gain_wide, acc_gain,
    part, near, total, far_buf, s_blocks,
    core_out, mine_up, mine_down, mine_out,
    one_up, one_down, one_out, two_up, two_down, two_out, z_up, z_down, z_out,
    fin_up, fin_down, fin_out, gq, q_one, q_two, q_z, q_fin, small_a, small_b, small_z,
    own_sem, b_send, b_recv, r_send, r_recv, send, recv,
):
    do, di, mp = places()
    width, tokens = x_ref.shape
    columns = heads_ref.shape[1]
    heads = columns // HD
    row, quarter, half = mp // 2, own_quarter(di, mp), lax.rem(mp, 2)
    place = (di, mp)
    sibling, across = dev(do, 1 - di, mp), dev(do, di, flip(mp, 1))
    posted, pending = [], []

    def prepare(source, target, device):
        n = len(posted)
        copy = remote(source, target, send.at[n], recv.at[n], device)
        posted.append(copy)
        pending.append(copy)
        return copy

    def post(source, target, device):
        copy = prepare(source, target, device)
        copy.start()
        return copy

    def finish(copy):
        copy.wait()
        pending[:] = [other for other in pending if other is not copy]

    def arrived(copies):
        for copy in copies:
            copy.wait_recv()

    def column(bit):
        return dev(flip(do, bit), di, mp)

    grads = (
        (dup_ref, mine_up, oup_ref, one_up, two_up, z_up, fin_up, up_out, 1, 2),
        (ddown_ref, mine_down, odown_ref, one_down, two_down, z_down, fin_down, down_out, 2, 1),
        (dout_ref, mine_out, core_out, one_out, two_out, z_out, fin_out, out_out, 1, 2),
    )
    own = []
    for i, g in enumerate(grads[:2]):
        for n, piece in enumerate((do, flip(do, g[9]))):
            own.append(pltpu.make_async_copy(g[0].at[piece], g[1].at[piece], own_sem.at[4 + 2 * i + n]))
        own.append(pltpu.make_async_copy(g[2], g[3], own_sem.at[8 + i]))
    own.append(pltpu.make_async_copy(dout_ref.at[:, di], mine_out, own_sem.at[2]))
    mixed_load = pltpu.make_async_copy(stream_ref, local_in, own_sem.at[10])
    mixed_load.start()
    for copy in own:
        copy.start()
    greet(neighbours(do, di, mp))

    swaps = []
    for k in range(GROUP):
        swaps.append(
            (
                gctx_ref.at[k], gall.at[quarter], b_send.at[k], b_recv.at[quarter], place,
                holder(row, k), do,
            )
        )
        send_block(*swaps[k])
    stage_core = [post(dout_ref.at[:, 1 - di], core_out, sibling)]

    def turn(step, carry):
        h, kb = step // GROUP, lax.rem(step, GROUP)
        rows = pl.ds(pl.multiple_of(columns + h * HD, HD), HD)
        k_tok[h, kb] = qkv_ref[kb, rows].T
        rows = pl.ds(pl.multiple_of(2 * columns + h * HD, HD), HD)
        v_tok[h, kb] = qkv_ref[kb, rows].T
        return carry

    lax.fori_loop(0, heads * GROUP, turn, 0)
    causal[...] = jnp.where(
        lax.broadcasted_iota(jnp.int32, causal.shape, 0)
        <= lax.broadcasted_iota(jnp.int32, causal.shape, 1),
        0.0, NEG,
    )
    for j in range(GROUP):
        turned = smalls_ref[j].T[:columns, 0:1]
        gain_wide[j * columns : (j + 1) * columns] = jnp.broadcast_to(turned, (columns, 128))
    acc_b[...] = jnp.zeros_like(acc_b)
    acc_w[...] = jnp.zeros_like(acc_w)
    segments = segs_ref[row]
    head_weight = headw_ref[...].reshape(3 * columns, width)
    def back_block(block):
        seg_q = segments[:, block * tokens : (block + 1) * tokens]
        masks = [
            jnp.where(segments[:, kb * tokens : kb * tokens + 1] == seg_q, 0.0, NEG)
            for kb in range(block)
        ]

        def one_head(h, carry):
            rows = pl.ds(pl.multiple_of(h * HD, HD), HD)
            k_rows = pl.ds(pl.multiple_of(columns + h * HD, HD), HD)
            query = qkv_ref[block, rows] * HD ** (-0.5)
            grad = gall[block, rows]
            mixed = heads_ref[block, rows].astype(F32) + rest_ref[block, rows].astype(F32)
            weighted = jnp.sum(grad.astype(F32) * mixed, axis=0, keepdims=True)
            lse = lse_ref[h, block, 0:1]
            grad_query = jnp.zeros((HD, tokens), F32)
            for kb in range(block + 1):
                raw = jnp.dot(k_tok[h, kb], query, preferred_element_type=F32)
                raw = raw + (causal[...] if kb == block else masks[kb])
                probs = jnp.exp(raw - lse)
                grad_probs = jnp.dot(v_tok[h, kb], grad, preferred_element_type=F32)
                grad_scores = (probs * (grad_probs - weighted)).astype(BF)
                grad_query += jnp.dot(qkv_ref[kb, k_rows], grad_scores, preferred_element_type=F32)
                key_term = dot_nt(query, grad_scores)
                value_term = dot_nt(grad, probs.astype(BF))
                if block == GROUP - 1:
                    acc_k[kb, rows] = key_term
                    acc_v[kb, rows] = value_term
                else:
                    acc_k[kb, rows] += key_term
                    acc_v[kb, rows] += value_term
            gj[rows] = (grad_query * HD ** (-0.5)).astype(BF)
            return carry

        lax.fori_loop(0, heads, one_head, 0)
        gj[columns : 2 * columns] = acc_k[block].astype(BF)
        gj[2 * columns :] = acc_v[block].astype(BF)
        part[block] = dot_tn(head_weight, gj[...])

    def near_args(i):
        return part.at[i], near.at[i % 2], r_send.at[i], r_recv.at[i], sibling

    def far_args(i):
        return total, far_buf, r_send.at[GROUP + i], r_recv.at[GROUP + i], across

    def to_sibling(i):
        @pl.when(di != i // 2)
        def _():
            remote(*near_args(i)).start()

    def across_row(i):
        @pl.when(di == i // 2)
        def _():
            remote(*near_args(i)).wait_recv()
            at = lambda k: pl.ds(pl.multiple_of(k * columns, columns), columns)
            add_pairs(
                GROUP,
                lambda k: near.at[i % 2, at(k)],
                lambda k: near.at[i % 2, at(k)],
                lambda k: part.at[i, at(k)],
            )

            @pl.when(half != i % 2)
            def _():
                total[...] = near[i % 2].astype(BF)
                remote(*far_args(i)).start()

    def weight_terms(block):
        acc_w[...] += dot_nt(gj[...], normed_ref[block])
        terms = gj[...].astype(F32)
        for k in range(tokens // 128):
            acc_b[: 3 * columns] += terms[:, k * 128 : (k + 1) * 128]

    def stage_one():
        arrived(stage_core)
        own[-1].wait()
        g = grads[2]
        add_pairs(
            GROUP * GROUP,
            lambda n: mine_out.at[n // GROUP, lax.rem(n, GROUP)],
            lambda n: mine_out.at[n // GROUP, lax.rem(n, GROUP)],
            lambda n: core_out.at[n // GROUP, lax.rem(n, GROUP)],
        )
        pieces = (flip(do, g[8]), flip(flip(do, g[8]), g[9]))
        return [post(mine_out.at[p], one_out.at[n], column(g[8])) for n, p in enumerate(pieces)]

    def stage_two(chosen):
        later = []
        for g in chosen:
            mine, one, first, second = g[1], g[3], g[8], g[9]
            for n, piece in ((1, flip(do, second)), (0, do)):
                add_pairs(
                    mine.shape[1], lambda k: mine.at[piece, k], lambda k: mine.at[piece, k],
                    lambda k: one.at[n, k],
                )
                if n == 1:
                    later.append(post(mine.at[piece], g[4], column(second)))
        return later

    def stage_three(copies, chosen):
        arrived(copies)
        later = []
        for g in chosen:
            mine, two, z_buf = g[1], g[4], g[5]
            add_pairs(
                mine.shape[1], lambda k: mine.at[do, k], lambda k: mine.at[do, k],
                lambda k: two.at[k],
            )
            for r in range(1, GROUP):
                later.append(
                    post(mine.at[do, r], z_buf.at[r - 1], dev(do, di, lax.rem(mp + r, GROUP)))
                )
        return later

    def result_of(i, piece):
        return grads[i][7].at[piece, di] if i < 2 else piece_of(out_out, piece, di)

    def stage_four(copies):
        arrived(copies)
        later = []
        for i, g in enumerate(grads):
            mine, z_buf, fin = g[1], g[5], g[6]
            fin[...] = (
                mine[do, 0].astype(F32) + z_buf[0].astype(F32)
                + z_buf[1].astype(F32) + z_buf[2].astype(F32)
            )
            target = result_of(i, do)
            pltpu.make_async_copy(fin, target, own_sem.at[i]).start()
            later.append(post(fin, target, column(g[8])))
        return later

    def stage_five(copies):
        arrived(copies)
        later = []
        for i, g in enumerate(grads):
            pltpu.make_async_copy(g[6], result_of(i, do), own_sem.at[i]).wait()
            for piece in (do, flip(do, g[8])):
                later.append(post(result_of(i, piece), result_of(i, piece), column(g[9])))
        return later

    def stage_six(copies):
        arrived(copies)
        halves = [g[7].at[:, di] for g in grads[:2]]
        lanes = out_out.shape[1] // 2
        halves.append(out_out.at[:, pl.ds(pl.multiple_of(di * lanes, lanes), lanes)])
        return [post(h, h, sibling) for h in halves]

    for copy in own[:-1]:
        copy.wait()
    copies = stage_two(grads[:2])
    for k in range(GROUP):
        swaps.append(
            (
                delta_ref.at[k], m_in.at[quarter], b_send.at[GROUP + k],
                b_recv.at[GROUP + quarter], place, (row, k), do,
            )
        )
        send_block(*swaps[GROUP + k])
    not_last = jnp.logical_or(
        mp < GROUP - 1, lax.broadcasted_iota(jnp.int32, (columns, 128), 0) < columns - 1
    )

    def add_local(blocks):
        def step(n, carry):
            k, lane = n // (tokens // 128), lax.rem(n, tokens // 128)
            at = pl.ds(pl.multiple_of(n * 128, 128), 128)
            inner = pl.ds(pl.multiple_of(lane * 128, 128), 128)
            value = local_in[:, at] + blocks[k, :, inner].astype(F32)
            local_in[:, at] = jnp.where(not_last, value, 0.0)
            return carry

        lax.fori_loop(0, GROUP * (tokens // 128), step, 0)

    for k in range(GROUP):
        pltpu.make_async_copy(gctx_ref.at[k], gall.at[k], b_recv.at[k]).wait()
    back_block(3)
    to_sibling(3)
    weight_terms(3)
    out_copies = stage_one()
    copies = stage_three(copies, grads[:2])
    back_block(2)
    to_sibling(2)
    across_row(3)
    weight_terms(2)
    arrived(out_copies)
    out_copies = stage_two(grads[2:])
    back_block(1)
    to_sibling(1)
    across_row(2)
    weight_terms(1)
    copies += stage_three(out_copies, grads[2:])
    for k in range(GROUP):
        pltpu.make_async_copy(delta_ref.at[k], m_in.at[k], b_recv.at[GROUP + k]).wait()
    mixed_load.wait()
    add_local(m_in)
    mixed_out = pltpu.make_async_copy(local_in, mixed_ref, own_sem.at[10])
    mixed_out.start()
    back_block(0)
    to_sibling(0)
    across_row(1)
    weight_terms(0)
    across_row(0)

    wide = width // 2
    sides = (pl.ds(0, wide), pl.ds(wide, wide))
    bits = ((1, 2), (2, 1))
    gq[...] = acc_w[...].astype(BF).reshape(gq.shape)
    q_copies = []
    for side, (first, second) in enumerate(bits):
        for n, piece in enumerate((flip(do, first), flip(flip(do, first), second))):
            q_copies.append(post(gq.at[piece, :, sides[side]], q_one.at[side, n], column(first)))

    copies = stage_four(copies)

    @pl.when(half == 0)
    def _():
        for i in (0, 2):
            @pl.when(di == i // 2)
            def _():
                remote(*far_args(i)).wait_recv()

    @pl.when(half == 1)
    def _():
        for i in (1, 3):
            @pl.when(di == i // 2)
            def _():
                remote(*far_args(i)).wait_recv()

    acc_gain[...] = jnp.zeros_like(acc_gain)

    def norm_step(lane, carry):
        lanes = pl.ds(pl.multiple_of(lane * 128, 128), 128)
        values = x_ref[:, lanes]
        grad = near[half, :, lanes] + far_buf[:, lanes].astype(F32)
        row_sum, inverse = stat_ref[0:1, lanes], stat_ref[1:2, lanes]
        final = lax.broadcasted_iota(jnp.int32, (width, 128), 0) == width - 1
        recovered = jnp.where(final, -row_sum, values)
        scaled = grad * gain_wide[...]
        acc_gain[...] += grad * recovered * inverse
        dot_sum = jnp.sum(scaled * recovered, axis=0, keepdims=True)
        tail = scaled[width - 1 :]
        factor = dot_sum * (inverse * inverse * inverse) / width
        grad_in = inverse * (scaled - tail) - factor * (values + row_sum)
        grad_in = jnp.where(final, 0.0, grad_in) + gn2_ref[:, lanes].astype(F32)
        for j in range(GROUP):
            s_blocks[j, :, lanes] = grad_in[j * columns : (j + 1) * columns].astype(BF)
        return carry

    lax.fori_loop(0, tokens // 128, norm_step, 0)
    for k in range(GROUP):
        swaps.append(
            (
                s_blocks.at[k], s_ref.at[quarter], b_send.at[2 * GROUP + k],
                b_recv.at[2 * GROUP + quarter], place, (row, k), do,
            )
        )
        send_block(*swaps[2 * GROUP + k])
    mixed_out.wait()
    cot_load = pltpu.make_async_copy(cot_ref, local_in, own_sem.at[11])
    cot_load.start()

    small_a[...] = jnp.zeros_like(small_a)
    small_a[0] = jnp.sum(acc_gain[...].T, axis=0, keepdims=True)
    bias_row = jnp.sum(acc_b[...].T, axis=0, keepdims=True)
    for r in range(3):
        small_a[1 + r] = sums_ref[r]
    for r in range(GROUP):
        small_a[4 + lax.rem(mp + r, GROUP)] = sums_ref[3 + r]
    small_a[8 + 2 * quarter, :, :columns] = bias_row[:, :columns]
    small_a[9 + 2 * quarter, :, :columns] = bias_row[:, 2 * columns : 3 * columns]
    small_one = post(small_a, small_b.at[0], sibling)

    arrived(q_copies)
    q_copies = []
    for side, (first, second) in enumerate(bits):
        for n, piece in ((1, flip(do, second)), (0, do)):
            gq[piece, :, sides[side]] = (
                gq[piece, :, sides[side]].astype(F32) + q_one[side, n].astype(F32)
            ).astype(BF)
            if n == 1:
                q_copies.append(post(gq.at[piece, :, sides[side]], q_two.at[side], column(second)))
    finish(small_one)
    small_a[...] += small_b[0]
    small_one = post(small_a, small_b.at[1], column(1))
    copies = stage_five(copies)
    arrived(q_copies)
    z_args = []
    for side in range(2):
        gq[do, :, sides[side]] = (
            gq[do, :, sides[side]].astype(F32) + q_two[side].astype(F32)
        ).astype(BF)
        z_args.append(
            (
                gq.at[do, :, sides[side]], q_z.at[row], b_send.at[3 * GROUP + side],
                b_recv.at[3 * GROUP + row], place, (side, quarter), do,
            )
        )
        send_block(*z_args[side])
    finish(small_one)
    small_a[...] += small_b[1]
    small_one = post(small_a, small_b.at[2], column(2))

    for r in range(2):
        pltpu.make_async_copy(q_z.at[r], q_z.at[r], b_recv.at[3 * GROUP + r]).wait()
    q_fin[...] = q_z[0].astype(F32) + q_z[1].astype(F32)

    def q_ref(piece, core):
        count = gq.shape[1]
        return qkvg_ref.at[
            pl.ds(pl.multiple_of(piece * count, count), count),
            pl.ds(pl.multiple_of(core * wide, wide), wide),
        ]

    q_own = pltpu.make_async_copy(q_fin, q_ref(do, di), own_sem.at[3])
    q_own.start()
    q_copies = [post(q_fin, q_ref(do, di), column(bit)) for bit in (1, 2)]
    finish(small_one)
    small_z[mp] = small_a[...] + small_b[2]
    small_copies = [
        post(small_z.at[mp], small_z.at[mp], dev(do, di, lax.rem(mp + r, GROUP)))
        for r in range(1, GROUP)
    ]
    copies = stage_six(copies)
    arrived(q_copies)

    q_last = prepare(q_ref(do, di), q_ref(do, di), sibling)
    n = len(posted) - 1

    @pl.when(di == 0)
    def _():
        piece = q_ref(flip(do, 1), di)
        remote(piece, piece, send.at[n], recv.at[n], column(2)).start()

    @pl.when(di == 1)
    def _():
        piece = q_ref(flip(do, 2), di)
        remote(piece, piece, send.at[n], recv.at[n], column(1)).start()

    q_own.wait()
    q_last.wait_recv()
    q_half = qkvg_ref.at[:, pl.ds(pl.multiple_of(di * wide, wide), wide)]
    q_copies = [post(q_half, q_half, sibling)]
    arrived(small_copies)
    small_out[...] = small_z[0] + small_z[1] + small_z[2] + small_z[3]
    arrived(q_copies)

    for k in range(GROUP):
        pltpu.make_async_copy(s_blocks.at[k], s_ref.at[k], b_recv.at[2 * GROUP + k]).wait()
    cot_load.wait()
    add_local(s_ref)
    back_out = pltpu.make_async_copy(local_in, back_ref, own_sem.at[11])
    back_out.start()
    for args in swaps + z_args:
        sent_block(*args)
    for i in range(GROUP):
        @pl.when(di != i // 2)
        def _():
            remote(*near_args(i)).wait_send()

        @pl.when(jnp.logical_and(di == i // 2, half != i % 2))
        def _():
            remote(*far_args(i)).wait_send()

    arrived(copies)
    for copy in pending:
        copy.wait_send()
    back_out.wait()


def backward_part(values):
    (
        grad_context, _, x_mine, grad_norm, heads_out, _, qkv, lse, normed, smalls,
        head_weight, segs, _, sums, up_grad, _, down_grad, _, out_grad, stream, _,
    ) = values
    columns, tokens = heads_out.shape[1:]
    width = x_mine.shape[0]
    heads = columns // HD
    shape = jax.ShapeDtypeStruct
    vmem, anywhere = pl.BlockSpec(memory_space=pltpu.VMEM), pl.BlockSpec(memory_space=pl.ANY)
    dma = pltpu.SemaphoreType.DMA
    slabs = (GROUP, columns, tokens)
    pieces = head_weight.shape[1]
    weight_grads = (up_grad, down_grad, out_grad)
    rows = [w.shape[-2:] for w in weight_grads]
    halves = [(GROUP, GROUP) + r for r in rows]
    buffers = (
        halves[2:]
        + halves
        + [(2, GROUP) + r for r in rows]
        + [(GROUP,) + r for r in rows]
        + [(GROUP - 1,) + r for r in rows]
    )
    return pl.pallas_call(
        backward_kernel,
        out_shape=[
            shape((16, 1, width), F32),
            shape(stream.shape, F32),
            shape(stream.shape, F32),
            shape((GROUP * pieces, width), F32),
        ]
        + [shape((GROUP, 2) + r, F32) for r in rows[:2]]
        + [shape((columns, width), F32)],
        in_specs=[vmem] * 14 + [anywhere] * 7,
        out_specs=[vmem] + [anywhere] * 6,
        scratch_shapes=[
            pltpu.VMEM(slabs, BF),
            pltpu.VMEM(stream.shape, F32),
            pltpu.VMEM(slabs, BF),
            pltpu.VMEM(slabs, BF),
            pltpu.VMEM((heads, GROUP, tokens, HD), BF),
            pltpu.VMEM((heads, GROUP, tokens, HD), BF),
            pltpu.VMEM((tokens, tokens), F32),
            pltpu.VMEM(slabs, F32),
            pltpu.VMEM(slabs, F32),
            pltpu.VMEM((3 * columns, tokens), BF),
            pltpu.VMEM((3 * columns, width), F32),
            pltpu.VMEM((640, 128), F32),
            pltpu.VMEM((width, 128), F32),
            pltpu.VMEM((width, 128), F32),
            pltpu.VMEM((GROUP, width, tokens), F32),
            pltpu.VMEM((2, width, tokens), F32),
            pltpu.VMEM((width, tokens), BF),
            pltpu.VMEM((width, tokens), BF),
            pltpu.VMEM(slabs, BF),
        ]
        + [pltpu.VMEM(b, BF) for b in buffers]
        + [pltpu.VMEM(r, F32) for r in rows]
        + [
            pltpu.VMEM((GROUP, pieces, width), BF),
            pltpu.VMEM((2, 2, pieces, width // 2), BF),
            pltpu.VMEM((2, pieces, width // 2), BF),
            pltpu.VMEM((2, pieces, width // 2), BF),
            pltpu.VMEM((pieces, width // 2), F32),
            pltpu.VMEM((16, 1, width), F32),
            pltpu.VMEM((3, 16, 1, width), F32),
            pltpu.VMEM((GROUP, 16, 1, width), F32),
            dma((12,)),
            dma((14,)),
            dma((14,)),
            dma((2 * GROUP,)),
            dma((2 * GROUP,)),
            dma((56,)),
            dma((56,)),
        ],
        compiler_params=pltpu.CompilerParams(
            collective_id=7, has_side_effects=True, vmem_limit_bytes=60 * 2**20
        ),
    )(*values)


def own_quarter(di, mp):
    return 2 * di + lax.rem(mp, 2)


def lane_chunks(count, step):
    lax.fori_loop(
        0, count, lambda i, c: (step(pl.ds(pl.multiple_of(i * 128, 128), 128)), c)[1], 0
    )


def xor(index, mask):
    for bit in (1, 2):
        if mask & bit:
            index = flip(index, bit)
    return index


def first_kernel(
    stream_ref, cot_ref, seg_ref, gain1_ref, gain2_ref, qv_ref, bias_ref,
    qkvw_ref, up_own, down_own, out_own,
    mine_ref, heads_ref, rest_ref, qkv_ref, lse_ref, normed_ref, smalls_ref, headw_ref, segs_ref,
    stat_ref, delta_ref, gctx_ref, gnorm_ref, sums_ref, mine_up, one_up, mine_down, one_down, dout_ref,
    up_all, down_all, out_all,
    grad_ref, context_ref, k_tokens, big, causal, wide_gain, back_gain, n2t, gyt,
    stats, x_more, g_more,
    w_up, w_down, w_out, d_up, d_down, n2, gy, pre, ghid, hidden, gpre, mlp, gn2, acc_gain,
    core_up, core_down,
    own_sem, in_sem, w_sem, x_send, x_recv, g_send, g_recv, c_send, c_recv, s_send, s_recv,
    st_send, st_recv, r_send, r_recv, h_send, h_recv, a_send, a_recv, t_send, t_recv, k_send, k_recv, o_send, o_recv,
):
    do, di, mp = places()
    width, tokens = normed_ref.shape[1], normed_ref.shape[2]
    columns = stream_ref.shape[0]
    heads_here = columns // HD
    lanes_count = tokens // 128
    row, quarter = mp // 2, own_quarter(di, mp)
    place = (di, mp)
    sibling, across = dev(do, 1 - di, mp), dev(do, di, flip(mp, 1))
    far = 2 * di + 1 - lax.rem(mp, 2)
    weights = ((up_own, up_all), (down_own, down_all), (out_own, out_all))
    final = lax.broadcasted_iota(jnp.int32, (width, 128), 0) == width - 1

    def column(bit):
        return dev(flip(do, bit), di, mp)

    loads = []
    for i, ref in enumerate((stream_ref, cot_ref)):
        for k in range(GROUP):
            loads.append(
                pltpu.make_async_copy(
                    ref.at[:, pl.ds(k * tokens, tokens)],
                    big.at[pl.ds(i * width + k * columns, columns)],
                    own_sem.at[2 + GROUP * i + k],
                )
            )
    own = [pltpu.make_async_copy(seg_ref, segs_ref.at[di], own_sem.at[1])]
    for copy in loads + own:
        copy.start()
    smalls_ref[mp] = jnp.zeros(smalls_ref.shape[1:], F32)
    smalls_ref[mp, 0:1, :columns] = gain1_ref[...]
    smalls_ref[mp, 1:2, :columns] = gain2_ref[...]
    smalls_ref[mp, 2:4, :columns] = qv_ref[...]
    smalls_ref[mp, 4:5] = bias_ref[0:1]
    greet(neighbours(do, di, mp))
    is_last = jnp.logical_and(
        mp == GROUP - 1, lax.broadcasted_iota(jnp.int32, (columns, tokens), 0) == columns - 1
    )

    def target_of(k):
        return k // 2, 2 * di + k % 2

    def rows_at(j):
        return pl.ds(pl.multiple_of(j * columns, 64), columns)

    def others():
        return [dev(do, di, lax.rem(mp + r, GROUP)) for r in range(1, GROUP)]

    def over_mp(i, r):
        ref, all_ref = weights[i]
        return remote(
            ref.at[do, di] if i < 2 else piece_of(ref, do, di), all_ref.at[do, di, r],
            a_send.at[i, r], a_recv.at[i, r], dev(do, di, lax.rem(mp + GROUP - r, GROUP)),
        )

    orders = ((1, 2), (2, 1))

    def hop(i, r, stage):
        all_ref = weights[i][1]
        first, second = orders[i]
        if stage == 3:
            ref = all_ref.at[:, di, r]
            return [remote(ref, ref, t_send.at[i, r, 3], t_recv.at[i, r, 3], sibling)]
        pieces = (do,) if stage == 1 else (do, flip(do, first))
        bit = first if stage == 1 else second
        copies = []
        for n, piece in enumerate(pieces):
            ref = all_ref.at[piece, di, r]
            at = stage - 1 + n
            copies.append(remote(ref, ref, t_send.at[i, r, at], t_recv.at[i, r, at], column(bit)))
        return copies

    def out_hop(stage):
        if stage == 3:
            ref = out_all.at[:, di, pl.ds(1, GROUP - 1)]
            return [remote(ref, ref, t_send.at[0, 0, 3], t_recv.at[0, 0, 3], sibling)]
        pieces = (do,) if stage == 1 else (do, flip(do, 1))
        copies = []
        for n, piece in enumerate(pieces):
            ref = out_all.at[piece, di, pl.ds(1, GROUP - 1)]
            at = stage - 1 + n
            copies.append(
                remote(ref, ref, t_send.at[0, 0, at], t_recv.at[0, 0, at], column(stage))
            )
        return copies

    def start(copies):
        for copy in copies:
            copy.start()

    def arrived(copies):
        for copy in copies:
            copy.wait_recv()

    def arrived_mp(r):
        arrived([over_mp(0, r), over_mp(1, r)])

    def both(r, stage):
        return hop(0, r, stage) + hop(1, r, stage)

    x_rest = [n2t.at[pl.ds(k * columns, columns)] for k in range(GROUP)]
    g_rest = [gnorm_ref.at[pl.ds(k * columns, columns)] for k in range(GROUP)]

    for k in range(GROUP):
        loads[k].wait()
        rows_k = pl.ds(k * columns, columns)
        part = jnp.where(is_last, 0.0, big[rows_k])
        big[rows_k] = part
        stats[mp, k, 0:1] = jnp.sum(part, axis=0, keepdims=True)
        stats[mp, k, 1:2] = jnp.sum(part * part, axis=0, keepdims=True)
    sums_over = [
        remote(stats.at[mp], stats.at[mp], st_send.at[r], st_recv.at[GROUP - r - 1], other)
        for r, other in zip(range(GROUP - 1), others())
    ]
    for copy in sums_over:
        copy.start()
    smalls = []
    for r in range(1, GROUP):
        target = dev(do, di, lax.rem(mp + r, GROUP))
        smalls.append(
            remote(smalls_ref.at[mp], smalls_ref.at[mp], s_send.at[r], s_recv.at[GROUP - r], target)
        )
    smalls.append(remote(seg_ref, segs_ref.at[di], s_send.at[0], s_recv.at[0], sibling))
    for copy in smalls:
        copy.start()
    own_gain = smalls_ref[mp].T[:columns, 0:1]
    for copy in sums_over:
        copy.wait_recv()
    x_args, stat_args, x_rest_args = [], [], []
    for k in range(GROUP):
        row_sum = stats[0, k, 0:1] + stats[1, k, 0:1] + stats[2, k, 0:1] + stats[3, k, 0:1]
        squares = stats[0, k, 1:2] + stats[1, k, 1:2] + stats[2, k, 1:2] + stats[3, k, 1:2]
        mean = (squares + row_sum * row_sum) / width + EPS
        inverse = lax.rsqrt(mean)
        stats[GROUP, k, 0:1] = row_sum
        stats[GROUP, k, 1:2] = inverse
        stats[GROUP, k, 2:3] = 1.0 / inverse
        values = big[k * columns : (k + 1) * columns]
        recovered = jnp.where(is_last, -row_sum, values)
        normed = (recovered * inverse * own_gain).astype(BF)
        delta_ref[k] = normed
        x_args.append(
            (
                delta_ref.at[k], normed_ref.at[k, rows_at(mp)], x_send.at[k], x_recv.at[mp],
                place, target_of(k), do,
            )
        )
        send_block(*x_args[k])
        near = (normed.astype(F32) * (1.0 / own_gain)) * stats[GROUP, k, 2:3]
        x_rest[k][...] = jnp.where(is_last, 0.0, values - near).astype(BF)
        stat_args.append(
            (stats.at[GROUP, k], stat_ref, r_send.at[k], r_recv.at[0], place, target_of(k), do)
        )
        x_rest_args.append(
            (
                x_rest[k], x_more.at[mp], r_send.at[GROUP + k], r_recv.at[1 + mp],
                place, target_of(k), do,
            )
        )

    @pl.when(mp == 0)
    def _():
        for args in stat_args:
            send_block(*args)

    head_target = (mp // 2, lax.rem(mp, 2) + 2 * di)
    head_args = (
        qkvw_ref.at[do], headw_ref.at[do], h_send.at[0], h_recv.at[0], place, head_target, do,
    )
    send_block(*head_args)

    gathers = []
    for k in range(GROUP):
        j = xor(mp, k)
        part = normed_ref.at[quarter, rows_at(j)]
        pltpu.make_async_copy(part, part, x_recv.at[j]).wait()
        for lane, other in enumerate((across, sibling)):
            copy = remote(part, part, g_send.at[lane, k], g_recv.at[lane, k], other)
            copy.start()
            gathers.append(copy)

    start([over_mp(2, r) for r in range(1, GROUP)])
    start([over_mp(i, r) for r in (1, 2) for i in range(2)])

    pltpu.make_async_copy(qkvw_ref.at[do], headw_ref.at[do], h_recv.at[0]).wait()
    cut = 80
    part_a, part_b = pl.ds(0, cut), pl.ds(cut, headw_ref.shape[1] - cut)
    heads = []

    def head_copy(piece, part, bit):
        ref = headw_ref.at[piece, part]
        n = len(heads) + 1
        copy = remote(ref, ref, h_send.at[n], h_recv.at[n], column(bit))
        copy.start()
        heads.append(copy)

    head_copy(do, part_a, 1)
    head_copy(do, part_b, 2)

    arrived(smalls)
    for copy in own:
        copy.wait()
    for j in range(GROUP):
        turned = smalls_ref[j].T
        at = slice(j * columns, (j + 1) * columns)
        back_gain[at] = jnp.broadcast_to(1.0 / turned[:columns, 0:1], (columns, 128))
        wide_gain[at] = jnp.broadcast_to(turned[:columns, 1:2], (columns, 128))
    biases = smalls_ref[quarter].T
    query_bias, value_bias = biases[:columns, 2:3], biases[:columns, 3:4]
    causal[...] = jnp.where(
        lax.broadcasted_iota(jnp.int32, causal.shape, 0)
        <= lax.broadcasted_iota(jnp.int32, causal.shape, 1),
        0.0, NEG,
    )
    for k in range(GROUP):
        loads[GROUP + k].wait()
        part = jnp.where(is_last, 0.0, big[width + k * columns : width + (k + 1) * columns])
        gctx_ref[k] = part.astype(BF)
        g_rest[k][...] = (part - gctx_ref[k].astype(F32)).astype(BF)
    arrived(heads[:2])
    head_copy(do, part_a, 2)
    head_copy(flip(do, 1), part_a, 2)
    head_copy(do, part_b, 1)
    head_copy(flip(do, 2), part_b, 1)
    for k in range(GROUP):
        gathers[2 * k].wait_recv()
        part = normed_ref.at[far, rows_at(xor(mp, 1 ^ k))]
        copy = remote(part, part, g_send.at[2, k], g_recv.at[2, k], sibling)
        copy.start()
        gathers.append(copy)
    for k in range(GROUP):
        gathers[2 * k + 1].wait_recv()
        gathers[2 * GROUP + k].wait_recv()
    arrived(heads[2:])
    cot_args = [
        (gctx_ref.at[k], grad_ref.at[mp], c_send.at[k], c_recv.at[mp], place, target_of(k), do)
        for k in range(GROUP)
    ]
    for args in x_rest_args:
        send_block(*args)
    arrived([over_mp(2, r) for r in range(1, GROUP)])
    start(out_hop(1))
    arrived_mp(1)
    start(both(1, 1))
    g_rest_args = [
        (
            g_rest[k], g_more.at[mp], r_send.at[2 * GROUP + k], r_recv.at[1 + GROUP + mp],
            place, target_of(k), do,
        )
        for k in range(GROUP)
    ]
    head_weight = headw_ref[...].reshape(3 * columns, width)

    def project(block, carry):
        joined = jnp.dot(head_weight, normed_ref[block], preferred_element_type=F32)
        qkv_ref[block, :columns] = (joined[:columns] + query_bias).astype(BF)
        keys = joined[columns : 2 * columns].astype(BF)
        qkv_ref[block, columns : 2 * columns] = keys
        qkv_ref[block, 2 * columns :] = (joined[2 * columns :] + value_bias).astype(BF)
        for h in range(heads_here):
            k_tokens[h, block] = keys[h * HD : (h + 1) * HD].T
        return carry

    lax.fori_loop(0, GROUP, project, 0)
    segments = segs_ref[row]

    def attend(block):
        seg_q = segments[:, block * tokens : (block + 1) * tokens]
        masks = [
            jnp.where(segments[:, kb * tokens : kb * tokens + 1] == seg_q, 0.0, NEG)
            for kb in range(block)
        ]

        def one_head(h, carry):
            rows = pl.ds(pl.multiple_of(h * HD, HD), HD)
            v_rows = pl.ds(pl.multiple_of(2 * columns + h * HD, HD), HD)
            query = qkv_ref[block, rows] * HD ** (-0.5)
            top = None
            for kb in range(block + 1):
                raw = jnp.dot(k_tokens[h, kb], query, preferred_element_type=F32)
                raw = raw + (causal[...] if kb == block else masks[kb])
                big[kb * tokens : (kb + 1) * tokens] = raw
                high = jnp.max(raw, axis=0, keepdims=True)
                top = high if top is None else jnp.maximum(top, high)
            total = jnp.zeros((1, tokens), F32)
            for kb in range(block + 1):
                expo = jnp.exp(big[kb * tokens : (kb + 1) * tokens] - top)
                big[kb * tokens : (kb + 1) * tokens] = expo
                total += jnp.sum(expo, axis=0, keepdims=True)
            portion = 1.0 / total
            mixed = jnp.zeros((HD, tokens), F32)
            for kb in range(block + 1):
                probs = (big[kb * tokens : (kb + 1) * tokens] * portion).astype(BF)
                mixed += jnp.dot(qkv_ref[kb, v_rows], probs, preferred_element_type=F32)
            rounded = mixed.astype(BF)
            heads_ref[block, rows] = rounded
            rest_ref[block, rows] = (mixed - rounded.astype(F32)).astype(BF)
            lse_ref[h, block] = jnp.broadcast_to(top + jnp.log(total), (8, tokens))
            return carry

        lax.fori_loop(0, heads_here, one_head, 0)

    context_args = [
        (
            heads_ref.at[block], context_ref.at[quarter], c_send.at[GROUP + block],
            c_recv.at[GROUP + quarter], place, holder(row, block), do,
        )
        for block in range(GROUP)
    ]

    attend(0)
    send_block(*context_args[0])
    for args in cot_args:
        send_block(*args)
    arrived(out_hop(1))
    start(out_hop(2))
    arrived_mp(2)
    start(both(2, 1))
    arrived(both(1, 1))
    start(both(1, 2))
    attend(1)
    send_block(*context_args[1])
    start([over_mp(i, 3) for i in range(2)])
    attend(2)
    send_block(*context_args[2])
    arrived(out_hop(2))
    start(out_hop(3))
    arrived(both(1, 2))
    start(both(1, 3))
    arrived(both(2, 1))
    start(both(2, 2))
    attend(3)
    send_block(*context_args[3])
    arrived(both(2, 2))
    start(both(2, 3))
    for args in g_rest_args:
        send_block(*args)

    attn, middle = big.at[pl.ds(0, width)], big.at[pl.ds(width, width)]
    own_weights = [
        pltpu.make_async_copy(ref, buf.at[0], in_sem.at[i, 0])
        for i, (ref, buf) in enumerate(((up_own, w_up), (down_own, w_down)))
    ]

    def fetch(r, slot):
        return [
            pltpu.make_async_copy(ref.at[:, :, r], buf.at[slot], in_sem.at[i, slot])
            for i, (ref, buf) in enumerate(((up_all, w_up), (down_all, w_down)))
        ]

    start(own_weights)
    rows, lanes = columns // GROUP, width // 2
    arrived(out_hop(3))
    out_loads = [pltpu.make_async_copy(out_own, w_out.at[mp], w_sem.at[0])]
    for r in range(1, GROUP):
        shard = lax.rem(mp + r, GROUP)
        for piece in range(GROUP):
            for side in range(2):
                out_loads.append(
                    pltpu.make_async_copy(
                        out_all.at[piece, side, r],
                        w_out.at[shard, pl.ds(piece * rows, rows), pl.ds(side * lanes, lanes)],
                        w_sem.at[(r * GROUP + piece) * 2 + side],
                    )
                )
    start(out_loads)
    out_bias = bias_ref[...].T[:, 1:2]
    def cotangent_at(at):
        return grad_ref[:, :, at].reshape(width, 128).astype(F32)

    def centre_grad(at):
        grad = cotangent_at(at)
        gyt[:, at] = (grad - jnp.sum(grad, axis=0, keepdims=True) / width).astype(BF)

    for copy in out_loads:
        copy.wait()
    for k in range(GROUP):
        pltpu.make_async_copy(heads_ref.at[k], context_ref.at[k], c_recv.at[GROUP + k]).wait()
    pltpu.make_async_copy(stat_ref, stat_ref, r_recv.at[0]).wait()
    for k in range(GROUP):
        pltpu.make_async_copy(x_more.at[k], x_more.at[k], r_recv.at[1 + k]).wait()
    projected = dot_tn(w_out[0], context_ref[0])
    for s in range(1, GROUP):
        projected += dot_tn(w_out[s], context_ref[s])
    attn[...] = projected + out_bias

    def norm(at):
        values = attn[:, at]
        values = values - jnp.sum(values, axis=0, keepdims=True) / width
        values = jnp.where(final, 0.0, values)
        attn[:, at] = values
        mine = (normed_ref[quarter, :, at].astype(F32) * back_gain[...]) * stat_ref[2:3, at]
        mine = mine + x_more[:, :, at].reshape(width, 128).astype(F32)
        mine = jnp.where(final, 0.0, mine)
        mine_ref[:, at] = mine
        values = values + mine
        middle[:, at] = values
        row_sum = jnp.sum(values, axis=0, keepdims=True)
        square_sum = jnp.sum(values * values, axis=0, keepdims=True)
        inverse = lax.rsqrt((square_sum + row_sum * row_sum) / width + EPS)
        recovered = jnp.where(final, -row_sum, values)
        n2t[:, at] = (recovered * inverse * wide_gain[...]).astype(BF)

    for args in x_rest_args:
        sent_block(*args)
    lane_chunks(lanes_count, norm)
    n2[...] = n2t[...].T
    for k in range(GROUP):
        pltpu.make_async_copy(grad_ref.at[k], grad_ref.at[k], c_recv.at[k]).wait()

    lane_chunks(lanes_count, centre_grad)
    gy[...] = gyt[...].T
    sums_ref[2] = jnp.sum(gy[...].astype(F32), axis=0, keepdims=True)
    arrived_mp(GROUP - 1)
    start(both(GROUP - 1, 1))
    grads = (
        (d_up, core_up, mine_up, one_up, 1, 2),
        (d_down, core_down, mine_down, one_down, 2, 1),
    )

    def to_sibling(r, slot):
        return [
            remote(g[0].at[slot, :, 1 - di], g[1].at[r], k_send.at[i, slot], k_recv.at[i, r], sibling)
            for i, g in enumerate(grads)
        ]

    def to_column(r):
        copies = []
        for i, g in enumerate(grads):
            first, second = g[4], g[5]
            for n, piece in enumerate((flip(do, first), flip(flip(do, first), second))):
                copies.append(
                    remote(
                        g[2].at[piece, r], g[3].at[n, r], o_send.at[i, n, r], o_recv.at[i, n, r],
                        column(first),
                    )
                )
        return copies

    def combine(r, slot):
        for copy in to_sibling(r, slot):
            copy.wait()
        for g in grads:
            add_pairs(
                GROUP, lambda k: g[2].at[k, r], lambda k: g[0].at[slot, k, di], lambda k: g[1].at[r, k]
            )
        start(to_column(r))

    chunk = 64
    root = 0.7978845608028654

    def shard_step(r, carry):
        slot = lax.rem(r, 2)
        for copy in fetch(r, slot):
            copy.wait()

        @pl.when(r < GROUP - 1)
        def _():
            arrived(both(r + 1, 3))
            start(fetch(r + 1, 1 - slot))

        up = w_up[slot].reshape(width, width)
        down = w_down[slot].reshape(width, width)
        bias = smalls_ref[lax.rem(mp + r, GROUP), 4:5]
        pre[...] = jnp.dot(n2[...], up, preferred_element_type=F32) + bias
        ghid[...] = dot_nt(gy[...], down)

        for step in (0, 1):

            @pl.when(r == step)
            def _():
                arrived(both(GROUP - 1, 1 + step))
                start(both(GROUP - 1, 2 + step))

        def gelu(i, carry):
            at = pl.ds(pl.multiple_of(i * chunk, chunk), chunk)
            p = pre[at]
            square = p * p
            t = jnp.tanh(root * (p + 0.044715 * (p * square)))
            half = 0.5 * (1.0 + t)
            hidden[at] = (p * half).astype(BF)
            slope = half + 0.5 * p * (1.0 - t * t) * (root * (1.0 + 3 * 0.044715 * square))
            gpre[at] = (ghid[at] * slope).astype(BF)
            return carry

        lax.fori_loop(0, tokens // chunk, gelu, 0)

        @pl.when(r >= 1)
        def _():
            combine(r - 1, 1 - slot)

        d_down[slot] = dot_tn(hidden[...], gy[...]).astype(BF).reshape(d_down.shape[1:])
        d_up[slot] = (
            jnp.dot(n2t[...], gpre[...], preferred_element_type=F32)
            .astype(BF)
            .reshape(d_up.shape[1:])
        )
        start(to_sibling(r, slot))
        sums_ref[3 + r] = jnp.sum(gpre[...].astype(F32), axis=0, keepdims=True)
        more_mlp = jnp.dot(hidden[...], down, preferred_element_type=F32)
        more_grad = dot_nt(gpre[...], up)

        @pl.when(r == 0)
        def _():
            mlp[...] = more_mlp
            gn2[...] = more_grad

        @pl.when(r > 0)
        def _():
            mlp[...] += more_mlp
            gn2[...] += more_grad

        return carry

    lax.fori_loop(0, GROUP, shard_step, 0)
    combine(GROUP - 1, (GROUP - 1) % 2)
    for args in x_args:
        sent_block(*args)
    mlp_y = mlp[...] + bias_ref[2:3]
    pre[...] = mlp_y - jnp.sum(mlp_y, axis=1, keepdims=True) / width

    def mixed_delta(at):
        delta = attn[:, at] + jnp.where(final, 0.0, pre[at].T)
        for j in range(GROUP):
            delta_ref[j, :, at] = delta[j * columns : (j + 1) * columns].astype(BF)

    lane_chunks(lanes_count, mixed_delta)
    acc_gain[...] = jnp.zeros_like(acc_gain)
    gat = gyt
    for args in cot_args + g_rest_args:
        sent_block(*args)
    for k in range(GROUP):
        pltpu.make_async_copy(g_more.at[k], g_more.at[k], r_recv.at[1 + GROUP + k]).wait()

    def back(at):
        grad = gn2[at].T
        values = middle[:, at]
        row_sum = jnp.sum(values, axis=0, keepdims=True)
        square_sum = jnp.sum(values * values, axis=0, keepdims=True)
        inverse = lax.rsqrt((square_sum + row_sum * row_sum) / width + EPS)
        recovered = jnp.where(final, -row_sum, values)
        acc_gain[...] += grad * recovered * inverse
        scaled = grad * wide_gain[...]
        dot_sum = jnp.sum(scaled * recovered, axis=0, keepdims=True)
        tail = scaled[width - 1 :]
        factor = dot_sum * (inverse * inverse * inverse) / width
        grad_in = inverse * (scaled - tail) - factor * (values + row_sum)
        grad_in = jnp.where(final, 0.0, grad_in)
        gnorm_ref[:, at] = grad_in.astype(BF)
        more = g_more[:, :, at].reshape(width, 128).astype(F32)
        grad_z = jnp.where(final, 0.0, (cotangent_at(at) + more) + grad_in)
        grad_z = grad_z.astype(BF).astype(F32)
        gat[:, at] = (grad_z - jnp.sum(grad_z, axis=0, keepdims=True) / width).astype(BF)

    lane_chunks(lanes_count, back)
    sums_ref[0] = jnp.sum(acc_gain[...].T, axis=0, keepdims=True)
    sums_ref[1] = dot_nt(jnp.ones((8, tokens), BF), gat[...])[:1]
    sums_ref[7] = jnp.zeros_like(sums_ref[7])
    for s in range(GROUP):
        gctx_ref[s] = jnp.dot(w_out[s], gat[...], preferred_element_type=F32).astype(BF)
        terms = dot_nt(context_ref[s], gat[...]).astype(BF)
        for side in range(2):
            dout_ref[:, side, lax.rem(s + GROUP - mp, GROUP)] = terms[
                :, side * lanes : (side + 1) * lanes
            ].reshape(GROUP, rows, lanes)
    sent_block(*head_args)
    for args in context_args:
        sent_block(*args)

    @pl.when(mp == 0)
    def _():
        for args in stat_args:
            sent_block(*args)

    sent = gathers + smalls + heads + sums_over
    for r in range(1, GROUP):
        sent += [over_mp(i, r) for i in range(3)]
        for stage in (1, 2, 3):
            sent += both(r, stage)
    for stage in (1, 2, 3):
        sent += out_hop(stage)
    for copy in sent:
        copy.wait_send()
    for r in range(GROUP):
        for copy in to_column(r):
            copy.wait()


def first_part(stream, cotangent, segment_ids, smalls, qkv_weight, up, down, out):
    columns, token_count = stream.shape
    width, tokens = columns * GROUP, token_count // GROUP
    heads = columns // HD
    shape = jax.ShapeDtypeStruct
    vmem, anywhere = pl.BlockSpec(memory_space=pltpu.VMEM), pl.BlockSpec(memory_space=pl.ANY)
    dma = pltpu.SemaphoreType.DMA
    up, down = pieces_of(up), pieces_of(down)
    head_pieces = qkv_weight.reshape(GROUP, 3 * columns // GROUP, width)
    slabs = (GROUP, columns, tokens)
    rows = up.shape[2:]
    out_rows = (columns // GROUP, width // 2)
    part, half = (2,) + up.shape, (GROUP, GROUP) + rows
    bf = lambda *dims: pltpu.VMEM(dims, BF)
    fl = lambda *dims: pltpu.VMEM(dims, F32)
    return pl.pallas_call(
        first_kernel,
        out_shape=[
            shape((width, tokens), F32),
            shape(slabs, BF),
            shape(slabs, BF),
            shape((GROUP, 3 * columns, tokens), BF),
            shape((heads, GROUP, 8, tokens), F32),
            shape((GROUP, width, tokens), BF),
            shape((GROUP, 8, width), F32),
            shape(head_pieces.shape, BF),
            shape((2, 1, token_count), jnp.int32),
            shape((8, tokens), F32),
            shape(slabs, BF),
            shape(slabs, BF),
            shape((width, tokens), BF),
            shape((8, 1, width), F32),
        ]
        + [shape(half, BF), shape((2,) + half[1:], BF)] * 2
        + [shape((GROUP, 2, GROUP) + out_rows, BF)]
        + [shape((GROUP, 2, GROUP) + p, BF) for p in (rows, rows, out_rows)],
        in_specs=[anywhere] * 2 + [vmem] * 5 + [anywhere] * 4,
        out_specs=[vmem] * 19 + [anywhere] * 3,
        scratch_shapes=[
            bf(*slabs), bf(*slabs), bf(heads, GROUP, tokens, HD),
            fl(token_count, tokens), fl(tokens, tokens), fl(width, 128), fl(width, 128),
            bf(width, tokens), bf(width, tokens), fl(GROUP + 1, GROUP, 8, tokens),
            bf(*slabs), bf(*slabs),
            bf(*part), bf(*part), bf(GROUP, columns, width), bf(*part), bf(*part),
            bf(tokens, width), bf(tokens, width), fl(tokens, width), fl(tokens, width),
            bf(tokens, width), bf(tokens, width), fl(tokens, width), fl(tokens, width),
            fl(width, 128), bf(*half), bf(*half),
            dma((10,)), dma((2, 2)), dma((2 * GROUP * GROUP,)),
            dma((GROUP,)), dma((GROUP,)), dma((3, GROUP)), dma((3, GROUP)),
            dma((2 * GROUP,)), dma((2 * GROUP,)), dma((GROUP,)), dma((GROUP,)),
            dma((GROUP,)), dma((GROUP,)), dma((4 * GROUP,)), dma((1 + 3 * GROUP,)),
            dma((7,)), dma((7,)), dma((3, GROUP)), dma((3, GROUP)),
            dma((2, GROUP, GROUP)), dma((2, GROUP, GROUP)), dma((2, 2)), dma((2, GROUP)),
            dma((2, 2, GROUP)), dma((2, 2, GROUP)),
        ],
        compiler_params=pltpu.CompilerParams(
            collective_id=6, has_side_effects=True, vmem_limit_bytes=62 * 2**20
        ),
    )(stream, cotangent, segment_ids, *smalls, head_pieces, up, down, out)


def local(
    stream, segment_ids, cotangent, ln1_gain, qkv_weight, qv_bias, out_weight, out_bias,
    ln2_gain, up_weight, up_bias, down_weight, down_bias,
):
    columns = stream.shape[0]
    mp = lax.axis_index("mp")
    kind = lax.broadcasted_iota(jnp.int32, (8, up_bias.shape[0]), 0)
    biases = jnp.where(
        kind == 0, up_bias[None], jnp.where(kind == 1, out_bias[None], down_bias[None])
    )
    smalls_in = [ln1_gain[None], ln2_gain[None], qv_bias, biases]
    (
        mine, heads_out, heads_rest, qkv, lse, normed_one, smalls, head_weight, segs, stat,
        delta, grad_context, grad_norm_two, sums, *rest,
    ) = first_part(
        stream, cotangent, segment_ids, smalls_in, qkv_weight, up_weight, down_weight, out_weight
    )
    weight_grads = rest[:5]
    small, mixed, stream_grad, qkv_grad, up_grad, down_grad, out_grad = backward_part(
        (
            grad_context, delta, mine, grad_norm_two, heads_out, heads_rest, qkv, lse, normed_one,
            smalls, head_weight, segs, stat, sums, *weight_grads, stream, cotangent,
        )
    )
    width = small.shape[-1]
    qkv_grad = qkv_grad.reshape(3, columns, width)
    up_grad, down_grad = [g.reshape(-1, width) for g in (up_grad, down_grad)]
    if lax.axis_size("blk") > 1:
        small, qkv_grad, up_grad, down_grad, out_grad = lax.psum(
            (small, qkv_grad, up_grad, down_grad, out_grad), "blk"
        )
    small = small[:, 0]
    shard = lambda values: lax.dynamic_slice_in_dim(values, mp * columns, columns, 0)
    at = lambda start, count: lax.dynamic_slice_in_dim(small, start, count, 0)
    return (
        mixed,
        stream_grad,
        shard(small[0]),
        qkv_grad,
        at(8 + 2 * mp, 2)[:, :columns],
        out_grad,
        small[2],
        shard(small[1]),
        up_grad,
        at(4 + mp, 1)[0],
        down_grad,
        small[3],
    )


def solution(mesh):
    rows, mp_count = mesh.shape["dp"], mesh.shape["mp"]
    pairs = Mesh(mesh.devices.reshape(rows // 8, 4, 2, mp_count), ALL)
    return jax.shard_map(
        local,
        mesh=pairs,
        in_specs=(
            P("mp", ROWS),
            P(ROWS, None),
            P("mp", ROWS),
            P("mp"),
            P(None, "mp", None),
            P(None, "mp"),
            P("mp", None),
            P(),
            P("mp"),
            P(None, "mp"),
            P("mp"),
            P("mp", None),
            P(),
        ),
        out_specs=(
            P("mp", ROWS),
            P("mp", ROWS),
            P("mp"),
            P(None, "mp", None),
            P(None, "mp"),
            P("mp", None),
            P(),
            P("mp"),
            P(None, "mp"),
            P("mp"),
            P("mp", None),
            P(),
        ),
        check_vma=False,
    )
```

```python
import functools

import jax
import jax.numpy as jnp
from jax import lax
from jax.experimental import pallas as pl
from jax.experimental.pallas import tpu as pltpu
from jax.sharding import Mesh, PartitionSpec as P

HD = 64
QB = 512
GROUP = 4
EPS = 1e-05
NEG = -1e30
MESH = pl.DeviceIdType.MESH
BF = jnp.bfloat16
F32 = jnp.float32
ALL = ("blk", "do", "di", "mp")
ROWS = ("blk", "do", "di")


def places():
    return lax.axis_index("do"), lax.axis_index("di"), lax.axis_index("mp")


def holder(row, quarter):
    return quarter // 2, 2 * row + lax.rem(quarter, 2)


def dev(do, di, mp):
    return (lax.axis_index("blk"), do, di, mp)


def flip(index, bit):
    return index + bit * (1 - 2 * lax.rem(index // bit, 2))


def remote(source, target, send, recv, device):
    return pltpu.make_async_remote_copy(
        source, target, send, recv, device_id=device, device_id_type=MESH
    )


def greet(others):
    barrier = pltpu.get_barrier_semaphore()
    for other in others:
        pl.semaphore_signal(barrier, inc=1, device_id=other, device_id_type=MESH)
    pl.semaphore_wait(barrier, len(others))


def neighbours(do, di, mp):
    column = [
        dev(do, lax.rem(di + a, 2), lax.rem(mp + b, GROUP))
        for a in range(2)
        for b in range(GROUP)
        if a or b
    ]
    return column + [dev(flip(do, 1), di, mp), dev(flip(do, 2), di, mp)]


def send_block(source, target, send, recv, place, target_place, do):
    (di, mp), (tdi, tmp) = place, target_place
    other = jnp.logical_or(tdi != di, tmp != mp)

    @pl.when(other)
    def _():
        remote(source, target, send, recv, dev(do, tdi, tmp)).start()

    @pl.when(jnp.logical_not(other))
    def _():
        pltpu.make_async_copy(source, target, recv).start()


def sent_block(source, target, send, recv, place, target_place, do):
    (di, mp), (tdi, tmp) = place, target_place
    other = jnp.logical_or(tdi != di, tmp != mp)

    @pl.when(other)
    def _():
        remote(source, target, send, recv, dev(do, tdi, tmp)).wait_send()


def piece_of(ref, do, di):
    rows, lanes = ref.shape[0] // GROUP, ref.shape[1] // 2
    return ref.at[
        pl.ds(pl.multiple_of(do * rows, rows), rows), pl.ds(pl.multiple_of(di * lanes, lanes), lanes)
    ]


def pieces_of(weight):
    return weight.reshape(GROUP, 2, weight.shape[0] // (2 * GROUP), weight.shape[1])


def dot_nt(left, right):
    return lax.dot_general(left, right, (((1,), (1,)), ((), ())), preferred_element_type=F32)


def dot_tn(left, right):
    return lax.dot_general(left, right, (((0,), (0,)), ((), ())), preferred_element_type=F32)


def add_pairs(count, target, first, second):
    def step(i, carry):
        ref = target(i)
        ref[...] = (first(i)[...].astype(F32) + second(i)[...].astype(F32)).astype(ref.dtype)
        return carry

    lax.fori_loop(0, count, step, 0)


def backward_kernel(
    gctx_ref, delta_ref, x_ref, gn2_ref, heads_ref, rest_ref, qkv_ref, lse_ref, normed_ref,
    smalls_ref, headw_ref, segs_ref, stat_ref, sums_ref, dup_ref, oup_ref, ddown_ref, odown_ref,
    dout_ref, stream_ref, cot_ref,
    small_out, mixed_ref, back_ref, qkvg_ref, up_out, down_out, out_out,
    s_ref, local_in, m_in, gall, k_tok, v_tok, causal, acc_k, acc_v, gj, acc_w, acc_b, gain_wide, acc_gain,
    part, near, total, far_buf, s_blocks,
    core_out, mine_up, mine_down, mine_out,
    one_up, one_down, one_out, two_up, two_down, two_out, z_up, z_down, z_out,
    fin_up, fin_down, fin_out, gq, q_one, q_two, q_z, q_fin, small_a, small_b, small_z,
    own_sem, b_send, b_recv, r_send, r_recv, send, recv,
):
    do, di, mp = places()
    width, tokens = x_ref.shape
    columns = heads_ref.shape[1]
    heads = columns // HD
    row, quarter, half = mp // 2, own_quarter(di, mp), lax.rem(mp, 2)
    place = (di, mp)
    sibling, across = dev(do, 1 - di, mp), dev(do, di, flip(mp, 1))
    posted, pending = [], []

    def prepare(source, target, device):
        n = len(posted)
        copy = remote(source, target, send.at[n], recv.at[n], device)
        posted.append(copy)
        pending.append(copy)
        return copy

    def post(source, target, device):
        copy = prepare(source, target, device)
        copy.start()
        return copy

    def finish(copy):
        copy.wait()
        pending[:] = [other for other in pending if other is not copy]

    def arrived(copies):
        for copy in copies:
            copy.wait_recv()

    def column(bit):
        return dev(flip(do, bit), di, mp)

    grads = (
        (dup_ref, mine_up, oup_ref, one_up, two_up, z_up, fin_up, up_out, 1, 2),
        (ddown_ref, mine_down, odown_ref, one_down, two_down, z_down, fin_down, down_out, 2, 1),
        (dout_ref, mine_out, core_out, one_out, two_out, z_out, fin_out, out_out, 1, 2),
    )
    own = []
    for i, g in enumerate(grads[:2]):
        for n, piece in enumerate((do, flip(do, g[9]))):
            own.append(pltpu.make_async_copy(g[0].at[piece], g[1].at[piece], own_sem.at[4 + 2 * i + n]))
        own.append(pltpu.make_async_copy(g[2], g[3], own_sem.at[8 + i]))
    own.append(pltpu.make_async_copy(dout_ref.at[:, di], mine_out, own_sem.at[2]))
    mixed_load = pltpu.make_async_copy(stream_ref, local_in, own_sem.at[10])
    mixed_load.start()
    for copy in own:
        copy.start()
    greet(neighbours(do, di, mp))

    swaps = []
    for k in range(GROUP):
        swaps.append(
            (
                gctx_ref.at[k], gall.at[quarter], b_send.at[k], b_recv.at[quarter], place,
                holder(row, k), do,
            )
        )
        send_block(*swaps[k])
    stage_core = [post(dout_ref.at[:, 1 - di], core_out, sibling)]

    def turn(step, carry):
        h, kb = step // GROUP, lax.rem(step, GROUP)
        rows = pl.ds(pl.multiple_of(columns + h * HD, HD), HD)
        k_tok[h, kb] = qkv_ref[kb, rows].T
        rows = pl.ds(pl.multiple_of(2 * columns + h * HD, HD), HD)
        v_tok[h, kb] = qkv_ref[kb, rows].T
        return carry

    lax.fori_loop(0, heads * GROUP, turn, 0)
    causal[...] = jnp.where(
        lax.broadcasted_iota(jnp.int32, causal.shape, 0)
        <= lax.broadcasted_iota(jnp.int32, causal.shape, 1),
        0.0, NEG,
    )
    for j in range(GROUP):
        turned = smalls_ref[j].T[:columns, 0:1]
        gain_wide[j * columns : (j + 1) * columns] = jnp.broadcast_to(turned, (columns, 128))
    acc_b[...] = jnp.zeros_like(acc_b)
    acc_w[...] = jnp.zeros_like(acc_w)
    segments = segs_ref[row]
    head_weight = headw_ref[...].reshape(3 * columns, width)
    def back_block(block):
        seg_q = segments[:, block * tokens : (block + 1) * tokens]
        masks = [
            jnp.where(segments[:, kb * tokens : kb * tokens + 1] == seg_q, 0.0, NEG)
            for kb in range(block)
        ]

        def one_head(h, carry):
            rows = pl.ds(pl.multiple_of(h * HD, HD), HD)
            k_rows = pl.ds(pl.multiple_of(columns + h * HD, HD), HD)
            query = qkv_ref[block, rows] * HD ** (-0.5)
            grad = gall[block, rows]
            mixed = heads_ref[block, rows].astype(F32) + rest_ref[block, rows].astype(F32)
            weighted = jnp.sum(grad.astype(F32) * mixed, axis=0, keepdims=True)
            lse = lse_ref[h, block, 0:1]
            grad_query = jnp.zeros((HD, tokens), F32)
            for kb in range(block + 1):
                raw = jnp.dot(k_tok[h, kb], query, preferred_element_type=F32)
                raw = raw + (causal[...] if kb == block else masks[kb])
                probs = jnp.exp(raw - lse)
                grad_probs = jnp.dot(v_tok[h, kb], grad, preferred_element_type=F32)
                grad_scores = (probs * (grad_probs - weighted)).astype(BF)
                grad_query += jnp.dot(qkv_ref[kb, k_rows], grad_scores, preferred_element_type=F32)
                key_term = dot_nt(query, grad_scores)
                value_term = dot_nt(grad, probs.astype(BF))
                if block == GROUP - 1:
                    acc_k[kb, rows] = key_term
                    acc_v[kb, rows] = value_term
                else:
                    acc_k[kb, rows] += key_term
                    acc_v[kb, rows] += value_term
            gj[rows] = (grad_query * HD ** (-0.5)).astype(BF)
            return carry

        lax.fori_loop(0, heads, one_head, 0)
        gj[columns : 2 * columns] = acc_k[block].astype(BF)
        gj[2 * columns :] = acc_v[block].astype(BF)
        part[block] = dot_tn(head_weight, gj[...])

    def near_args(i):
        return part.at[i], near.at[i % 2], r_send.at[i], r_recv.at[i], sibling

    def far_args(i):
        return total, far_buf, r_send.at[GROUP + i], r_recv.at[GROUP + i], across

    def to_sibling(i):
        @pl.when(di != i // 2)
        def _():
            remote(*near_args(i)).start()

    def across_row(i):
        @pl.when(di == i // 2)
        def _():
            remote(*near_args(i)).wait_recv()
            at = lambda k: pl.ds(pl.multiple_of(k * columns, columns), columns)
            add_pairs(
                GROUP,
                lambda k: near.at[i % 2, at(k)],
                lambda k: near.at[i % 2, at(k)],
                lambda k: part.at[i, at(k)],
            )

            @pl.when(half != i % 2)
            def _():
                total[...] = near[i % 2].astype(BF)
                remote(*far_args(i)).start()

    def weight_terms(block):
        acc_w[...] += dot_nt(gj[...], normed_ref[block])
        terms = gj[...].astype(F32)
        for k in range(tokens // 128):
            acc_b[: 3 * columns] += terms[:, k * 128 : (k + 1) * 128]

    def stage_one():
        arrived(stage_core)
        own[-1].wait()
        g = grads[2]
        add_pairs(
            GROUP * GROUP,
            lambda n: mine_out.at[n // GROUP, lax.rem(n, GROUP)],
            lambda n: mine_out.at[n // GROUP, lax.rem(n, GROUP)],
            lambda n: core_out.at[n // GROUP, lax.rem(n, GROUP)],
        )
        pieces = (flip(do, g[8]), flip(flip(do, g[8]), g[9]))
        return [post(mine_out.at[p], one_out.at[n], column(g[8])) for n, p in enumerate(pieces)]

    def stage_two(chosen):
        later = []
        for g in chosen:
            mine, one, first, second = g[1], g[3], g[8], g[9]
            for n, piece in ((1, flip(do, second)), (0, do)):
                add_pairs(
                    mine.shape[1], lambda k: mine.at[piece, k], lambda k: mine.at[piece, k],
                    lambda k: one.at[n, k],
                )
                if n == 1:
                    later.append(post(mine.at[piece], g[4], column(second)))
        return later

    def stage_three(copies, chosen):
        arrived(copies)
        later = []
        for g in chosen:
            mine, two, z_buf = g[1], g[4], g[5]
            add_pairs(
                mine.shape[1], lambda k: mine.at[do, k], lambda k: mine.at[do, k],
                lambda k: two.at[k],
            )
            for r in range(1, GROUP):
                later.append(
                    post(mine.at[do, r], z_buf.at[r - 1], dev(do, di, lax.rem(mp + r, GROUP)))
                )
        return later

    def result_of(i, piece):
        return grads[i][7].at[piece, di] if i < 2 else piece_of(out_out, piece, di)

    def stage_four(copies):
        arrived(copies)
        later = []
        for i, g in enumerate(grads):
            mine, z_buf, fin = g[1], g[5], g[6]
            fin[...] = (
                mine[do, 0].astype(F32) + z_buf[0].astype(F32)
                + z_buf[1].astype(F32) + z_buf[2].astype(F32)
            )
            target = result_of(i, do)
            pltpu.make_async_copy(fin, target, own_sem.at[i]).start()
            later.append(post(fin, target, column(g[8])))
        return later

    def stage_five(copies):
        arrived(copies)
        later = []
        for i, g in enumerate(grads):
            pltpu.make_async_copy(g[6], result_of(i, do), own_sem.at[i]).wait()
            for piece in (do, flip(do, g[8])):
                later.append(post(result_of(i, piece), result_of(i, piece), column(g[9])))
        return later

    def stage_six(copies):
        arrived(copies)
        halves = [g[7].at[:, di] for g in grads[:2]]
        lanes = out_out.shape[1] // 2
        halves.append(out_out.at[:, pl.ds(pl.multiple_of(di * lanes, lanes), lanes)])
        return [post(h, h, sibling) for h in halves]

    for copy in own[:-1]:
        copy.wait()
    copies = stage_two(grads[:2])
    for k in range(GROUP):
        swaps.append(
            (
                delta_ref.at[k], m_in.at[quarter], b_send.at[GROUP + k],
                b_recv.at[GROUP + quarter], place, (row, k), do,
            )
        )
        send_block(*swaps[GROUP + k])
    not_last = jnp.logical_or(
        mp < GROUP - 1, lax.broadcasted_iota(jnp.int32, (columns, 128), 0) < columns - 1
    )

    def add_local(blocks):
        def step(n, carry):
            k, lane = n // (tokens // 128), lax.rem(n, tokens // 128)
            at = pl.ds(pl.multiple_of(n * 128, 128), 128)
            inner = pl.ds(pl.multiple_of(lane * 128, 128), 128)
            value = local_in[:, at] + blocks[k, :, inner].astype(F32)
            local_in[:, at] = jnp.where(not_last, value, 0.0)
            return carry

        lax.fori_loop(0, GROUP * (tokens // 128), step, 0)

    for k in range(GROUP):
        pltpu.make_async_copy(gctx_ref.at[k], gall.at[k], b_recv.at[k]).wait()
    back_block(3)
    to_sibling(3)
    weight_terms(3)
    out_copies = stage_one()
    copies = stage_three(copies, grads[:2])
    back_block(2)
    to_sibling(2)
    across_row(3)
    weight_terms(2)
    arrived(out_copies)
    out_copies = stage_two(grads[2:])
    back_block(1)
    to_sibling(1)
    across_row(2)
    weight_terms(1)
    copies += stage_three(out_copies, grads[2:])
    back_block(0)
    to_sibling(0)
    across_row(1)
    weight_terms(0)
    across_row(0)

    wide = width // 2
    sides = (pl.ds(0, wide), pl.ds(wide, wide))
    bits = ((1, 2), (2, 1))
    gq[...] = acc_w[...].astype(BF).reshape(gq.shape)
    q_copies = []
    for side, (first, second) in enumerate(bits):
        for n, piece in enumerate((flip(do, first), flip(flip(do, first), second))):
            q_copies.append(post(gq.at[piece, :, sides[side]], q_one.at[side, n], column(first)))

    copies = stage_four(copies)

    for k in range(GROUP):
        pltpu.make_async_copy(delta_ref.at[k], m_in.at[k], b_recv.at[GROUP + k]).wait()
    mixed_load.wait()
    add_local(m_in)
    mixed_out = pltpu.make_async_copy(local_in, mixed_ref, own_sem.at[10])
    mixed_out.start()

    @pl.when(half == 0)
    def _():
        for i in (0, 2):
            @pl.when(di == i // 2)
            def _():
                remote(*far_args(i)).wait_recv()

    @pl.when(half == 1)
    def _():
        for i in (1, 3):
            @pl.when(di == i // 2)
            def _():
                remote(*far_args(i)).wait_recv()

    acc_gain[...] = jnp.zeros_like(acc_gain)

    def norm_step(lane, carry):
        lanes = pl.ds(pl.multiple_of(lane * 128, 128), 128)
        values = x_ref[:, lanes]
        grad = near[half, :, lanes] + far_buf[:, lanes].astype(F32)
        row_sum, inverse = stat_ref[0:1, lanes], stat_ref[1:2, lanes]
        final = lax.broadcasted_iota(jnp.int32, (width, 128), 0) == width - 1
        recovered = jnp.where(final, -row_sum, values)
        scaled = grad * gain_wide[...]
        acc_gain[...] += grad * recovered * inverse
        dot_sum = jnp.sum(scaled * recovered, axis=0, keepdims=True)
        tail = scaled[width - 1 :]
        factor = dot_sum * (inverse * inverse * inverse) / width
        grad_in = inverse * (scaled - tail) - factor * (values + row_sum)
        grad_in = jnp.where(final, 0.0, grad_in) + gn2_ref[:, lanes].astype(F32)
        for j in range(GROUP):
            s_blocks[j, :, lanes] = grad_in[j * columns : (j + 1) * columns].astype(BF)
        return carry

    lax.fori_loop(0, tokens // 128, norm_step, 0)
    for k in range(GROUP):
        swaps.append(
            (
                s_blocks.at[k], s_ref.at[quarter], b_send.at[2 * GROUP + k],
                b_recv.at[2 * GROUP + quarter], place, (row, k), do,
            )
        )
        send_block(*swaps[2 * GROUP + k])
    mixed_out.wait()
    cot_load = pltpu.make_async_copy(cot_ref, local_in, own_sem.at[11])
    cot_load.start()

    small_a[...] = jnp.zeros_like(small_a)
    small_a[0] = jnp.sum(acc_gain[...].T, axis=0, keepdims=True)
    bias_row = jnp.sum(acc_b[...].T, axis=0, keepdims=True)
    for r in range(3):
        small_a[1 + r] = sums_ref[r]
    for r in range(GROUP):
        small_a[4 + lax.rem(mp + r, GROUP)] = sums_ref[3 + r]
    small_a[8 + 2 * quarter, :, :columns] = bias_row[:, :columns]
    small_a[9 + 2 * quarter, :, :columns] = bias_row[:, 2 * columns : 3 * columns]
    small_one = post(small_a, small_b.at[0], sibling)

    arrived(q_copies)
    q_copies = []
    for side, (first, second) in enumerate(bits):
        for n, piece in ((1, flip(do, second)), (0, do)):
            gq[piece, :, sides[side]] = (
                gq[piece, :, sides[side]].astype(F32) + q_one[side, n].astype(F32)
            ).astype(BF)
            if n == 1:
                q_copies.append(post(gq.at[piece, :, sides[side]], q_two.at[side], column(second)))
    finish(small_one)
    small_a[...] += small_b[0]
    small_one = post(small_a, small_b.at[1], column(1))
    copies = stage_five(copies)
    arrived(q_copies)
    z_args = []
    for side in range(2):
        gq[do, :, sides[side]] = (
            gq[do, :, sides[side]].astype(F32) + q_two[side].astype(F32)
        ).astype(BF)
        z_args.append(
            (
                gq.at[do, :, sides[side]], q_z.at[row], b_send.at[3 * GROUP + side],
                b_recv.at[3 * GROUP + row], place, (side, quarter), do,
            )
        )
        send_block(*z_args[side])
    finish(small_one)
    small_a[...] += small_b[1]
    small_one = post(small_a, small_b.at[2], column(2))

    for r in range(2):
        pltpu.make_async_copy(q_z.at[r], q_z.at[r], b_recv.at[3 * GROUP + r]).wait()
    q_fin[...] = q_z[0].astype(F32) + q_z[1].astype(F32)

    def q_ref(piece, core):
        count = gq.shape[1]
        return qkvg_ref.at[
            pl.ds(pl.multiple_of(piece * count, count), count),
            pl.ds(pl.multiple_of(core * wide, wide), wide),
        ]

    q_own = pltpu.make_async_copy(q_fin, q_ref(do, di), own_sem.at[3])
    q_own.start()
    q_copies = [post(q_fin, q_ref(do, di), column(bit)) for bit in (1, 2)]
    finish(small_one)
    small_z[mp] = small_a[...] + small_b[2]
    small_copies = [
        post(small_z.at[mp], small_z.at[mp], dev(do, di, lax.rem(mp + r, GROUP)))
        for r in range(1, GROUP)
    ]
    copies = stage_six(copies)
    arrived(q_copies)

    q_last = prepare(q_ref(do, di), q_ref(do, di), sibling)
    n = len(posted) - 1

    @pl.when(di == 0)
    def _():
        piece = q_ref(flip(do, 1), di)
        remote(piece, piece, send.at[n], recv.at[n], column(2)).start()

    @pl.when(di == 1)
    def _():
        piece = q_ref(flip(do, 2), di)
        remote(piece, piece, send.at[n], recv.at[n], column(1)).start()

    q_own.wait()
    q_last.wait_recv()
    q_half = qkvg_ref.at[:, pl.ds(pl.multiple_of(di * wide, wide), wide)]
    q_copies = [post(q_half, q_half, sibling)]
    arrived(small_copies)
    small_out[...] = small_z[0] + small_z[1] + small_z[2] + small_z[3]
    arrived(q_copies)

    for k in range(GROUP):
        pltpu.make_async_copy(s_blocks.at[k], s_ref.at[k], b_recv.at[2 * GROUP + k]).wait()
    cot_load.wait()
    add_local(s_ref)
    back_out = pltpu.make_async_copy(local_in, back_ref, own_sem.at[11])
    back_out.start()
    for args in swaps + z_args:
        sent_block(*args)
    for i in range(GROUP):
        @pl.when(di != i // 2)
        def _():
            remote(*near_args(i)).wait_send()

        @pl.when(jnp.logical_and(di == i // 2, half != i % 2))
        def _():
            remote(*far_args(i)).wait_send()

    arrived(copies)
    for copy in pending:
        copy.wait_send()
    back_out.wait()


def backward_part(values):
    (
        grad_context, _, x_mine, grad_norm, heads_out, _, qkv, lse, normed, smalls,
        head_weight, segs, _, sums, up_grad, _, down_grad, _, out_grad, stream, _,
    ) = values
    columns, tokens = heads_out.shape[1:]
    width = x_mine.shape[0]
    heads = columns // HD
    shape = jax.ShapeDtypeStruct
    vmem, anywhere = pl.BlockSpec(memory_space=pltpu.VMEM), pl.BlockSpec(memory_space=pl.ANY)
    dma = pltpu.SemaphoreType.DMA
    slabs = (GROUP, columns, tokens)
    pieces = head_weight.shape[1]
    weight_grads = (up_grad, down_grad, out_grad)
    rows = [w.shape[-2:] for w in weight_grads]
    halves = [(GROUP, GROUP) + r for r in rows]
    buffers = (
        halves[2:]
        + halves
        + [(2, GROUP) + r for r in rows]
        + [(GROUP,) + r for r in rows]
        + [(GROUP - 1,) + r for r in rows]
    )
    return pl.pallas_call(
        backward_kernel,
        out_shape=[
            shape((16, 1, width), F32),
            shape(stream.shape, F32),
            shape(stream.shape, F32),
            shape((GROUP * pieces, width), F32),
        ]
        + [shape((GROUP, 2) + r, F32) for r in rows[:2]]
        + [shape((columns, width), F32)],
        in_specs=[vmem] * 14 + [anywhere] * 7,
        out_specs=[vmem] + [anywhere] * 6,
        scratch_shapes=[
            pltpu.VMEM(slabs, BF),
            pltpu.VMEM(stream.shape, F32),
            pltpu.VMEM(slabs, BF),
            pltpu.VMEM(slabs, BF),
            pltpu.VMEM((heads, GROUP, tokens, HD), BF),
            pltpu.VMEM((heads, GROUP, tokens, HD), BF),
            pltpu.VMEM((tokens, tokens), F32),
            pltpu.VMEM(slabs, F32),
            pltpu.VMEM(slabs, F32),
            pltpu.VMEM((3 * columns, tokens), BF),
            pltpu.VMEM((3 * columns, width), F32),
            pltpu.VMEM((640, 128), F32),
            pltpu.VMEM((width, 128), F32),
            pltpu.VMEM((width, 128), F32),
            pltpu.VMEM((GROUP, width, tokens), F32),
            pltpu.VMEM((2, width, tokens), F32),
            pltpu.VMEM((width, tokens), BF),
            pltpu.VMEM((width, tokens), BF),
            pltpu.VMEM(slabs, BF),
        ]
        + [pltpu.VMEM(b, BF) for b in buffers]
        + [pltpu.VMEM(r, F32) for r in rows]
        + [
            pltpu.VMEM((GROUP, pieces, width), BF),
            pltpu.VMEM((2, 2, pieces, width // 2), BF),
            pltpu.VMEM((2, pieces, width // 2), BF),
            pltpu.VMEM((2, pieces, width // 2), BF),
            pltpu.VMEM((pieces, width // 2), F32),
            pltpu.VMEM((16, 1, width), F32),
            pltpu.VMEM((3, 16, 1, width), F32),
            pltpu.VMEM((GROUP, 16, 1, width), F32),
            dma((12,)),
            dma((14,)),
            dma((14,)),
            dma((2 * GROUP,)),
            dma((2 * GROUP,)),
            dma((56,)),
            dma((56,)),
        ],
        compiler_params=pltpu.CompilerParams(
            collective_id=7, has_side_effects=True, vmem_limit_bytes=60 * 2**20
        ),
    )(*values)


def own_quarter(di, mp):
    return 2 * di + lax.rem(mp, 2)


def lane_chunks(count, step):
    lax.fori_loop(
        0, count, lambda i, c: (step(pl.ds(pl.multiple_of(i * 128, 128), 128)), c)[1], 0
    )


def xor(index, mask):
    for bit in (1, 2):
        if mask & bit:
            index = flip(index, bit)
    return index


def first_kernel(
    stream_ref, cot_ref, seg_ref, gain1_ref, gain2_ref, qv_ref, bias_ref,
    qkvw_ref, up_own, down_own, out_own,
    mine_ref, heads_ref, rest_ref, qkv_ref, lse_ref, normed_ref, smalls_ref, headw_ref, segs_ref,
    stat_ref, delta_ref, gctx_ref, gnorm_ref, sums_ref, mine_up, one_up, mine_down, one_down, dout_ref,
    up_all, down_all, out_all,
    grad_ref, context_ref, k_tokens, big, causal, wide_gain, back_gain, n2t, gyt,
    stats, x_more, g_more,
    w_up, w_down, w_out, d_up, d_down, n2, gy, pre, ghid, hidden, gpre, mlp, gn2, acc_gain,
    core_up, core_down,
    own_sem, in_sem, w_sem, x_send, x_recv, g_send, g_recv, c_send, c_recv, s_send, s_recv,
    st_send, st_recv, r_send, r_recv, h_send, h_recv, a_send, a_recv, t_send, t_recv, k_send, k_recv, o_send, o_recv,
):
    do, di, mp = places()
    width, tokens = normed_ref.shape[1], normed_ref.shape[2]
    columns = stream_ref.shape[0]
    heads_here = columns // HD
    lanes_count = tokens // 128
    row, quarter = mp // 2, own_quarter(di, mp)
    place = (di, mp)
    sibling, across = dev(do, 1 - di, mp), dev(do, di, flip(mp, 1))
    far = 2 * di + 1 - lax.rem(mp, 2)
    weights = ((up_own, up_all), (down_own, down_all), (out_own, out_all))
    final = lax.broadcasted_iota(jnp.int32, (width, 128), 0) == width - 1

    def column(bit):
        return dev(flip(do, bit), di, mp)

    loads = []
    for i, ref in enumerate((stream_ref, cot_ref)):
        for k in range(GROUP):
            loads.append(
                pltpu.make_async_copy(
                    ref.at[:, pl.ds(k * tokens, tokens)],
                    big.at[pl.ds(i * width + k * columns, columns)],
                    own_sem.at[2 + GROUP * i + k],
                )
            )
    own = [pltpu.make_async_copy(seg_ref, segs_ref.at[di], own_sem.at[1])]
    for copy in loads + own:
        copy.start()
    smalls_ref[mp] = jnp.zeros(smalls_ref.shape[1:], F32)
    smalls_ref[mp, 0:1, :columns] = gain1_ref[...]
    smalls_ref[mp, 1:2, :columns] = gain2_ref[...]
    smalls_ref[mp, 2:4, :columns] = qv_ref[...]
    smalls_ref[mp, 4:5] = bias_ref[0:1]
    greet(neighbours(do, di, mp))
    is_last = jnp.logical_and(
        mp == GROUP - 1, lax.broadcasted_iota(jnp.int32, (columns, tokens), 0) == columns - 1
    )

    def target_of(k):
        return k // 2, 2 * di + k % 2

    def rows_at(j):
        return pl.ds(pl.multiple_of(j * columns, 64), columns)

    def others():
        return [dev(do, di, lax.rem(mp + r, GROUP)) for r in range(1, GROUP)]

    def over_mp(i, r):
        ref, all_ref = weights[i]
        return remote(
            ref.at[do, di] if i < 2 else piece_of(ref, do, di), all_ref.at[do, di, r],
            a_send.at[i, r], a_recv.at[i, r], dev(do, di, lax.rem(mp + GROUP - r, GROUP)),
        )

    orders = ((1, 2), (2, 1))

    def hop(i, r, stage):
        all_ref = weights[i][1]
        first, second = orders[i]
        if stage == 3:
            ref = all_ref.at[:, di, r]
            return [remote(ref, ref, t_send.at[i, r, 3], t_recv.at[i, r, 3], sibling)]
        pieces = (do,) if stage == 1 else (do, flip(do, first))
        bit = first if stage == 1 else second
        copies = []
        for n, piece in enumerate(pieces):
            ref = all_ref.at[piece, di, r]
            at = stage - 1 + n
            copies.append(remote(ref, ref, t_send.at[i, r, at], t_recv.at[i, r, at], column(bit)))
        return copies

    def out_hop(stage):
        if stage == 3:
            ref = out_all.at[:, di, pl.ds(1, GROUP - 1)]
            return [remote(ref, ref, t_send.at[0, 0, 3], t_recv.at[0, 0, 3], sibling)]
        pieces = (do,) if stage == 1 else (do, flip(do, 1))
        copies = []
        for n, piece in enumerate(pieces):
            ref = out_all.at[piece, di, pl.ds(1, GROUP - 1)]
            at = stage - 1 + n
            copies.append(
                remote(ref, ref, t_send.at[0, 0, at], t_recv.at[0, 0, at], column(stage))
            )
        return copies

    def start(copies):
        for copy in copies:
            copy.start()

    def arrived(copies):
        for copy in copies:
            copy.wait_recv()

    def arrived_mp(r):
        arrived([over_mp(0, r), over_mp(1, r)])

    def both(r, stage):
        return hop(0, r, stage) + hop(1, r, stage)

    x_rest = [n2t.at[pl.ds(k * columns, columns)] for k in range(GROUP)]
    g_rest = [gnorm_ref.at[pl.ds(k * columns, columns)] for k in range(GROUP)]

    for k in range(GROUP):
        loads[k].wait()
        rows_k = pl.ds(k * columns, columns)
        part = jnp.where(is_last, 0.0, big[rows_k])
        big[rows_k] = part
        stats[mp, k, 0:1] = jnp.sum(part, axis=0, keepdims=True)
        stats[mp, k, 1:2] = jnp.sum(part * part, axis=0, keepdims=True)
    sums_over = [
        remote(stats.at[mp], stats.at[mp], st_send.at[r], st_recv.at[GROUP - r - 1], other)
        for r, other in zip(range(GROUP - 1), others())
    ]
    for copy in sums_over:
        copy.start()
    smalls = []
    for r in range(1, GROUP):
        target = dev(do, di, lax.rem(mp + r, GROUP))
        smalls.append(
            remote(smalls_ref.at[mp], smalls_ref.at[mp], s_send.at[r], s_recv.at[GROUP - r], target)
        )
    smalls.append(remote(seg_ref, segs_ref.at[di], s_send.at[0], s_recv.at[0], sibling))
    for copy in smalls:
        copy.start()
    own_gain = smalls_ref[mp].T[:columns, 0:1]
    for copy in sums_over:
        copy.wait_recv()
    x_args, stat_args, x_rest_args = [], [], []
    for k in range(GROUP):
        row_sum = stats[0, k, 0:1] + stats[1, k, 0:1] + stats[2, k, 0:1] + stats[3, k, 0:1]
        squares = stats[0, k, 1:2] + stats[1, k, 1:2] + stats[2, k, 1:2] + stats[3, k, 1:2]
        mean = (squares + row_sum * row_sum) / width + EPS
        inverse = lax.rsqrt(mean)
        stats[GROUP, k, 0:1] = row_sum
        stats[GROUP, k, 1:2] = inverse
        stats[GROUP, k, 2:3] = 1.0 / inverse
        values = big[k * columns : (k + 1) * columns]
        recovered = jnp.where(is_last, -row_sum, values)
        normed = (recovered * inverse * own_gain).astype(BF)
        delta_ref[k] = normed
        x_args.append(
            (
                delta_ref.at[k], normed_ref.at[k, rows_at(mp)], x_send.at[k], x_recv.at[mp],
                place, target_of(k), do,
            )
        )
        send_block(*x_args[k])
        near = (normed.astype(F32) * (1.0 / own_gain)) * stats[GROUP, k, 2:3]
        x_rest[k][...] = jnp.where(is_last, 0.0, values - near).astype(BF)
        stat_args.append(
            (stats.at[GROUP, k], stat_ref, r_send.at[k], r_recv.at[0], place, target_of(k), do)
        )
        x_rest_args.append(
            (
                x_rest[k], x_more.at[mp], r_send.at[GROUP + k], r_recv.at[1 + mp],
                place, target_of(k), do,
            )
        )

    @pl.when(mp == 0)
    def _():
        for args in stat_args:
            send_block(*args)

    head_target = (mp // 2, lax.rem(mp, 2) + 2 * di)
    head_args = (
        qkvw_ref.at[do], headw_ref.at[do], h_send.at[0], h_recv.at[0], place, head_target, do,
    )
    send_block(*head_args)

    gathers = []
    for k in range(GROUP):
        j = xor(mp, k)
        part = normed_ref.at[quarter, rows_at(j)]
        pltpu.make_async_copy(part, part, x_recv.at[j]).wait()
        for lane, other in enumerate((across, sibling)):
            copy = remote(part, part, g_send.at[lane, k], g_recv.at[lane, k], other)
            copy.start()
            gathers.append(copy)

    start([over_mp(2, r) for r in range(1, GROUP)])
    start([over_mp(i, r) for r in (1, 2) for i in range(2)])

    pltpu.make_async_copy(qkvw_ref.at[do], headw_ref.at[do], h_recv.at[0]).wait()
    cut = 80
    part_a, part_b = pl.ds(0, cut), pl.ds(cut, headw_ref.shape[1] - cut)
    heads = []

    def head_copy(piece, part, bit):
        ref = headw_ref.at[piece, part]
        n = len(heads) + 1
        copy = remote(ref, ref, h_send.at[n], h_recv.at[n], column(bit))
        copy.start()
        heads.append(copy)

    head_copy(do, part_a, 1)
    head_copy(do, part_b, 2)

    arrived(smalls)
    for copy in own:
        copy.wait()
    for j in range(GROUP):
        turned = smalls_ref[j].T
        at = slice(j * columns, (j + 1) * columns)
        back_gain[at] = jnp.broadcast_to(1.0 / turned[:columns, 0:1], (columns, 128))
        wide_gain[at] = jnp.broadcast_to(turned[:columns, 1:2], (columns, 128))
    biases = smalls_ref[quarter].T
    query_bias, value_bias = biases[:columns, 2:3], biases[:columns, 3:4]
    causal[...] = jnp.where(
        lax.broadcasted_iota(jnp.int32, causal.shape, 0)
        <= lax.broadcasted_iota(jnp.int32, causal.shape, 1),
        0.0, NEG,
    )
    for k in range(GROUP):
        loads[GROUP + k].wait()
        part = jnp.where(is_last, 0.0, big[width + k * columns : width + (k + 1) * columns])
        gctx_ref[k] = part.astype(BF)
        g_rest[k][...] = (part - gctx_ref[k].astype(F32)).astype(BF)
    arrived(heads[:2])
    head_copy(do, part_a, 2)
    head_copy(flip(do, 1), part_a, 2)
    head_copy(do, part_b, 1)
    head_copy(flip(do, 2), part_b, 1)
    for k in range(GROUP):
        gathers[2 * k].wait_recv()
        part = normed_ref.at[far, rows_at(xor(mp, 1 ^ k))]
        copy = remote(part, part, g_send.at[2, k], g_recv.at[2, k], sibling)
        copy.start()
        gathers.append(copy)
    for k in range(GROUP):
        gathers[2 * k + 1].wait_recv()
        gathers[2 * GROUP + k].wait_recv()
    arrived(heads[2:])
    cot_args = [
        (gctx_ref.at[k], grad_ref.at[mp], c_send.at[k], c_recv.at[mp], place, target_of(k), do)
        for k in range(GROUP)
    ]
    for args in x_rest_args:
        send_block(*args)
    arrived([over_mp(2, r) for r in range(1, GROUP)])
    start(out_hop(1))
    arrived_mp(1)
    start(both(1, 1))
    g_rest_args = [
        (
            g_rest[k], g_more.at[mp], r_send.at[2 * GROUP + k], r_recv.at[1 + GROUP + mp],
            place, target_of(k), do,
        )
        for k in range(GROUP)
    ]
    head_weight = headw_ref[...].reshape(3 * columns, width)

    def project(block, carry):
        joined = jnp.dot(head_weight, normed_ref[block], preferred_element_type=F32)
        qkv_ref[block, :columns] = (joined[:columns] + query_bias).astype(BF)
        keys = joined[columns : 2 * columns].astype(BF)
        qkv_ref[block, columns : 2 * columns] = keys
        qkv_ref[block, 2 * columns :] = (joined[2 * columns :] + value_bias).astype(BF)
        for h in range(heads_here):
            k_tokens[h, block] = keys[h * HD : (h + 1) * HD].T
        return carry

    lax.fori_loop(0, GROUP, project, 0)
    segments = segs_ref[row]

    def attend(block):
        seg_q = segments[:, block * tokens : (block + 1) * tokens]
        masks = [
            jnp.where(segments[:, kb * tokens : kb * tokens + 1] == seg_q, 0.0, NEG)
            for kb in range(block)
        ]

        def one_head(h, carry):
            rows = pl.ds(pl.multiple_of(h * HD, HD), HD)
            v_rows = pl.ds(pl.multiple_of(2 * columns + h * HD, HD), HD)
            query = qkv_ref[block, rows] * HD ** (-0.5)
            top = None
            for kb in range(block + 1):
                raw = jnp.dot(k_tokens[h, kb], query, preferred_element_type=F32)
                raw = raw + (causal[...] if kb == block else masks[kb])
                big[kb * tokens : (kb + 1) * tokens] = raw
                high = jnp.max(raw, axis=0, keepdims=True)
                top = high if top is None else jnp.maximum(top, high)
            total = jnp.zeros((1, tokens), F32)
            for kb in range(block + 1):
                expo = jnp.exp(big[kb * tokens : (kb + 1) * tokens] - top)
                big[kb * tokens : (kb + 1) * tokens] = expo
                total += jnp.sum(expo, axis=0, keepdims=True)
            portion = 1.0 / total
            mixed = jnp.zeros((HD, tokens), F32)
            for kb in range(block + 1):
                probs = (big[kb * tokens : (kb + 1) * tokens] * portion).astype(BF)
                mixed += jnp.dot(qkv_ref[kb, v_rows], probs, preferred_element_type=F32)
            rounded = mixed.astype(BF)
            heads_ref[block, rows] = rounded
            rest_ref[block, rows] = (mixed - rounded.astype(F32)).astype(BF)
            lse_ref[h, block] = jnp.broadcast_to(top + jnp.log(total), (8, tokens))
            return carry

        lax.fori_loop(0, heads_here, one_head, 0)

    context_args = [
        (
            heads_ref.at[block], context_ref.at[quarter], c_send.at[GROUP + block],
            c_recv.at[GROUP + quarter], place, holder(row, block), do,
        )
        for block in range(GROUP)
    ]

    attend(0)
    send_block(*context_args[0])
    for args in cot_args:
        send_block(*args)
    arrived(out_hop(1))
    start(out_hop(2))
    arrived_mp(2)
    start(both(2, 1))
    arrived(both(1, 1))
    start(both(1, 2))
    attend(1)
    send_block(*context_args[1])
    start([over_mp(i, 3) for i in range(2)])
    attend(2)
    send_block(*context_args[2])
    arrived(out_hop(2))
    start(out_hop(3))
    arrived(both(1, 2))
    start(both(1, 3))
    arrived(both(2, 1))
    start(both(2, 2))
    attend(3)
    send_block(*context_args[3])
    arrived(both(2, 2))
    start(both(2, 3))
    for args in g_rest_args:
        send_block(*args)

    attn, middle = big.at[pl.ds(0, width)], big.at[pl.ds(width, width)]
    own_weights = [
        pltpu.make_async_copy(ref, buf.at[0], in_sem.at[i, 0])
        for i, (ref, buf) in enumerate(((up_own, w_up), (down_own, w_down)))
    ]

    def fetch(r, slot):
        return [
            pltpu.make_async_copy(ref.at[:, :, r], buf.at[slot], in_sem.at[i, slot])
            for i, (ref, buf) in enumerate(((up_all, w_up), (down_all, w_down)))
        ]

    start(own_weights)
    rows, lanes = columns // GROUP, width // 2
    arrived(out_hop(3))
    out_loads = [pltpu.make_async_copy(out_own, w_out.at[mp], w_sem.at[0])]
    for r in range(1, GROUP):
        shard = lax.rem(mp + r, GROUP)
        for piece in range(GROUP):
            for side in range(2):
                out_loads.append(
                    pltpu.make_async_copy(
                        out_all.at[piece, side, r],
                        w_out.at[shard, pl.ds(piece * rows, rows), pl.ds(side * lanes, lanes)],
                        w_sem.at[(r * GROUP + piece) * 2 + side],
                    )
                )
    start(out_loads)
    out_bias = bias_ref[...].T[:, 1:2]
    def cotangent_at(at):
        return grad_ref[:, :, at].reshape(width, 128).astype(F32)

    def centre_grad(at):
        grad = cotangent_at(at)
        gyt[:, at] = (grad - jnp.sum(grad, axis=0, keepdims=True) / width).astype(BF)

    for copy in out_loads:
        copy.wait()
    for k in range(GROUP):
        pltpu.make_async_copy(heads_ref.at[k], context_ref.at[k], c_recv.at[GROUP + k]).wait()
    pltpu.make_async_copy(stat_ref, stat_ref, r_recv.at[0]).wait()
    for k in range(GROUP):
        pltpu.make_async_copy(x_more.at[k], x_more.at[k], r_recv.at[1 + k]).wait()
    projected = dot_tn(w_out[0], context_ref[0])
    for s in range(1, GROUP):
        projected += dot_tn(w_out[s], context_ref[s])
    attn[...] = projected + out_bias

    def norm(at):
        values = attn[:, at]
        values = values - jnp.sum(values, axis=0, keepdims=True) / width
        values = jnp.where(final, 0.0, values)
        attn[:, at] = values
        mine = (normed_ref[quarter, :, at].astype(F32) * back_gain[...]) * stat_ref[2:3, at]
        mine = mine + x_more[:, :, at].reshape(width, 128).astype(F32)
        mine = jnp.where(final, 0.0, mine)
        mine_ref[:, at] = mine
        values = values + mine
        middle[:, at] = values
        row_sum = jnp.sum(values, axis=0, keepdims=True)
        square_sum = jnp.sum(values * values, axis=0, keepdims=True)
        inverse = lax.rsqrt((square_sum + row_sum * row_sum) / width + EPS)
        recovered = jnp.where(final, -row_sum, values)
        n2t[:, at] = (recovered * inverse * wide_gain[...]).astype(BF)

    for args in x_rest_args:
        sent_block(*args)
    lane_chunks(lanes_count, norm)
    n2[...] = n2t[...].T
    for k in range(GROUP):
        pltpu.make_async_copy(grad_ref.at[k], grad_ref.at[k], c_recv.at[k]).wait()

    lane_chunks(lanes_count, centre_grad)
    gy[...] = gyt[...].T
    sums_ref[2] = jnp.sum(gy[...].astype(F32), axis=0, keepdims=True)
    arrived_mp(GROUP - 1)
    start(both(GROUP - 1, 1))
    grads = (
        (d_up, core_up, mine_up, one_up, 1, 2),
        (d_down, core_down, mine_down, one_down, 2, 1),
    )

    def to_sibling(r, slot):
        return [
            remote(g[0].at[slot, :, 1 - di], g[1].at[r], k_send.at[i, slot], k_recv.at[i, r], sibling)
            for i, g in enumerate(grads)
        ]

    def to_column(r):
        copies = []
        for i, g in enumerate(grads):
            first, second = g[4], g[5]
            for n, piece in enumerate((flip(do, first), flip(flip(do, first), second))):
                copies.append(
                    remote(
                        g[2].at[piece, r], g[3].at[n, r], o_send.at[i, n, r], o_recv.at[i, n, r],
                        column(first),
                    )
                )
        return copies

    def combine(r, slot):
        for copy in to_sibling(r, slot):
            copy.wait()
        for g in grads:
            add_pairs(
                GROUP, lambda k: g[2].at[k, r], lambda k: g[0].at[slot, k, di], lambda k: g[1].at[r, k]
            )
        start(to_column(r))

    chunk = 64
    root = 0.7978845608028654

    def shard_step(r, carry):
        slot = lax.rem(r, 2)
        for copy in fetch(r, slot):
            copy.wait()

        @pl.when(r < GROUP - 1)
        def _():
            arrived(both(r + 1, 3))
            start(fetch(r + 1, 1 - slot))

        up = w_up[slot].reshape(width, width)
        down = w_down[slot].reshape(width, width)
        bias = smalls_ref[lax.rem(mp + r, GROUP), 4:5]
        pre[...] = jnp.dot(n2[...], up, preferred_element_type=F32) + bias
        ghid[...] = dot_nt(gy[...], down)

        for step in (0, 1):

            @pl.when(r == step)
            def _():
                arrived(both(GROUP - 1, 1 + step))
                start(both(GROUP - 1, 2 + step))

        def gelu(i, carry):
            at = pl.ds(pl.multiple_of(i * chunk, chunk), chunk)
            p = pre[at]
            square = p * p
            t = jnp.tanh(root * (p + 0.044715 * (p * square)))
            half = 0.5 * (1.0 + t)
            hidden[at] = (p * half).astype(BF)
            slope = half + 0.5 * p * (1.0 - t * t) * (root * (1.0 + 3 * 0.044715 * square))
            gpre[at] = (ghid[at] * slope).astype(BF)
            return carry

        lax.fori_loop(0, tokens // chunk, gelu, 0)

        @pl.when(r >= 1)
        def _():
            combine(r - 1, 1 - slot)

        d_down[slot] = dot_tn(hidden[...], gy[...]).astype(BF).reshape(d_down.shape[1:])
        d_up[slot] = (
            jnp.dot(n2t[...], gpre[...], preferred_element_type=F32)
            .astype(BF)
            .reshape(d_up.shape[1:])
        )
        start(to_sibling(r, slot))
        sums_ref[3 + r] = jnp.sum(gpre[...].astype(F32), axis=0, keepdims=True)
        more_mlp = jnp.dot(hidden[...], down, preferred_element_type=F32)
        more_grad = dot_nt(gpre[...], up)

        @pl.when(r == 0)
        def _():
            mlp[...] = more_mlp
            gn2[...] = more_grad

        @pl.when(r > 0)
        def _():
            mlp[...] += more_mlp
            gn2[...] += more_grad

        return carry

    lax.fori_loop(0, GROUP, shard_step, 0)
    combine(GROUP - 1, (GROUP - 1) % 2)
    for args in x_args:
        sent_block(*args)
    mlp_y = mlp[...] + bias_ref[2:3]
    pre[...] = mlp_y - jnp.sum(mlp_y, axis=1, keepdims=True) / width

    def mixed_delta(at):
        delta = attn[:, at] + jnp.where(final, 0.0, pre[at].T)
        for j in range(GROUP):
            delta_ref[j, :, at] = delta[j * columns : (j + 1) * columns].astype(BF)

    lane_chunks(lanes_count, mixed_delta)
    acc_gain[...] = jnp.zeros_like(acc_gain)
    gat = gyt
    for args in cot_args + g_rest_args:
        sent_block(*args)
    for k in range(GROUP):
        pltpu.make_async_copy(g_more.at[k], g_more.at[k], r_recv.at[1 + GROUP + k]).wait()

    def back(at):
        grad = gn2[at].T
        values = middle[:, at]
        row_sum = jnp.sum(values, axis=0, keepdims=True)
        square_sum = jnp.sum(values * values, axis=0, keepdims=True)
        inverse = lax.rsqrt((square_sum + row_sum * row_sum) / width + EPS)
        recovered = jnp.where(final, -row_sum, values)
        acc_gain[...] += grad * recovered * inverse
        scaled = grad * wide_gain[...]
        dot_sum = jnp.sum(scaled * recovered, axis=0, keepdims=True)
        tail = scaled[width - 1 :]
        factor = dot_sum * (inverse * inverse * inverse) / width
        grad_in = inverse * (scaled - tail) - factor * (values + row_sum)
        grad_in = jnp.where(final, 0.0, grad_in)
        gnorm_ref[:, at] = grad_in.astype(BF)
        more = g_more[:, :, at].reshape(width, 128).astype(F32)
        grad_z = jnp.where(final, 0.0, (cotangent_at(at) + more) + grad_in)
        grad_z = grad_z.astype(BF).astype(F32)
        gat[:, at] = (grad_z - jnp.sum(grad_z, axis=0, keepdims=True) / width).astype(BF)

    lane_chunks(lanes_count, back)
    sums_ref[0] = jnp.sum(acc_gain[...].T, axis=0, keepdims=True)
    sums_ref[1] = dot_nt(jnp.ones((8, tokens), BF), gat[...])[:1]
    sums_ref[7] = jnp.zeros_like(sums_ref[7])
    for s in range(GROUP):
        gctx_ref[s] = jnp.dot(w_out[s], gat[...], preferred_element_type=F32).astype(BF)
        terms = dot_nt(context_ref[s], gat[...]).astype(BF)
        for side in range(2):
            dout_ref[:, side, lax.rem(s + GROUP - mp, GROUP)] = terms[
                :, side * lanes : (side + 1) * lanes
            ].reshape(GROUP, rows, lanes)
    sent_block(*head_args)
    for args in context_args:
        sent_block(*args)

    @pl.when(mp == 0)
    def _():
        for args in stat_args:
            sent_block(*args)

    sent = gathers + smalls + heads + sums_over
    for r in range(1, GROUP):
        sent += [over_mp(i, r) for i in range(3)]
        for stage in (1, 2, 3):
            sent += both(r, stage)
    for stage in (1, 2, 3):
        sent += out_hop(stage)
    for copy in sent:
        copy.wait_send()
    for r in range(GROUP):
        for copy in to_column(r):
            copy.wait()


def first_part(stream, cotangent, segment_ids, smalls, qkv_weight, up, down, out):
    columns, token_count = stream.shape
    width, tokens = columns * GROUP, token_count // GROUP
    heads = columns // HD
    shape = jax.ShapeDtypeStruct
    vmem, anywhere = pl.BlockSpec(memory_space=pltpu.VMEM), pl.BlockSpec(memory_space=pl.ANY)
    dma = pltpu.SemaphoreType.DMA
    up, down = pieces_of(up), pieces_of(down)
    head_pieces = qkv_weight.reshape(GROUP, 3 * columns // GROUP, width)
    slabs = (GROUP, columns, tokens)
    rows = up.shape[2:]
    out_rows = (columns // GROUP, width // 2)
    part, half = (2,) + up.shape, (GROUP, GROUP) + rows
    bf = lambda *dims: pltpu.VMEM(dims, BF)
    fl = lambda *dims: pltpu.VMEM(dims, F32)
    return pl.pallas_call(
        first_kernel,
        out_shape=[
            shape((width, tokens), F32),
            shape(slabs, BF),
            shape(slabs, BF),
            shape((GROUP, 3 * columns, tokens), BF),
            shape((heads, GROUP, 8, tokens), F32),
            shape((GROUP, width, tokens), BF),
            shape((GROUP, 8, width), F32),
            shape(head_pieces.shape, BF),
            shape((2, 1, token_count), jnp.int32),
            shape((8, tokens), F32),
            shape(slabs, BF),
            shape(slabs, BF),
            shape((width, tokens), BF),
            shape((8, 1, width), F32),
        ]
        + [shape(half, BF), shape((2,) + half[1:], BF)] * 2
        + [shape((GROUP, 2, GROUP) + out_rows, BF)]
        + [shape((GROUP, 2, GROUP) + p, BF) for p in (rows, rows, out_rows)],
        in_specs=[anywhere] * 2 + [vmem] * 5 + [anywhere] * 4,
        out_specs=[vmem] * 19 + [anywhere] * 3,
        scratch_shapes=[
            bf(*slabs), bf(*slabs), bf(heads, GROUP, tokens, HD),
            fl(token_count, tokens), fl(tokens, tokens), fl(width, 128), fl(width, 128),
            bf(width, tokens), bf(width, tokens), fl(GROUP + 1, GROUP, 8, tokens),
            bf(*slabs), bf(*slabs),
            bf(*part), bf(*part), bf(GROUP, columns, width), bf(*part), bf(*part),
            bf(tokens, width), bf(tokens, width), fl(tokens, width), fl(tokens, width),
            bf(tokens, width), bf(tokens, width), fl(tokens, width), fl(tokens, width),
            fl(width, 128), bf(*half), bf(*half),
            dma((10,)), dma((2, 2)), dma((2 * GROUP * GROUP,)),
            dma((GROUP,)), dma((GROUP,)), dma((3, GROUP)), dma((3, GROUP)),
            dma((2 * GROUP,)), dma((2 * GROUP,)), dma((GROUP,)), dma((GROUP,)),
            dma((GROUP,)), dma((GROUP,)), dma((4 * GROUP,)), dma((1 + 3 * GROUP,)),
            dma((7,)), dma((7,)), dma((3, GROUP)), dma((3, GROUP)),
            dma((2, GROUP, GROUP)), dma((2, GROUP, GROUP)), dma((2, 2)), dma((2, GROUP)),
            dma((2, 2, GROUP)), dma((2, 2, GROUP)),
        ],
        compiler_params=pltpu.CompilerParams(
            collective_id=6, has_side_effects=True, vmem_limit_bytes=62 * 2**20
        ),
    )(stream, cotangent, segment_ids, *smalls, head_pieces, up, down, out)


def local(
    stream, segment_ids, cotangent, ln1_gain, qkv_weight, qv_bias, out_weight, out_bias,
    ln2_gain, up_weight, up_bias, down_weight, down_bias,
):
    columns = stream.shape[0]
    mp = lax.axis_index("mp")
    kind = lax.broadcasted_iota(jnp.int32, (8, up_bias.shape[0]), 0)
    biases = jnp.where(
        kind == 0, up_bias[None], jnp.where(kind == 1, out_bias[None], down_bias[None])
    )
    smalls_in = [ln1_gain[None], ln2_gain[None], qv_bias, biases]
    (
        mine, heads_out, heads_rest, qkv, lse, normed_one, smalls, head_weight, segs, stat,
        delta, grad_context, grad_norm_two, sums, *rest,
    ) = first_part(
        stream, cotangent, segment_ids, smalls_in, qkv_weight, up_weight, down_weight, out_weight
    )
    weight_grads = rest[:5]
    small, mixed, stream_grad, qkv_grad, up_grad, down_grad, out_grad = backward_part(
        (
            grad_context, delta, mine, grad_norm_two, heads_out, heads_rest, qkv, lse, normed_one,
            smalls, head_weight, segs, stat, sums, *weight_grads, stream, cotangent,
        )
    )
    width = small.shape[-1]
    qkv_grad = qkv_grad.reshape(3, columns, width)
    up_grad, down_grad = [g.reshape(-1, width) for g in (up_grad, down_grad)]
    if lax.axis_size("blk") > 1:
        small, qkv_grad, up_grad, down_grad, out_grad = lax.psum(
            (small, qkv_grad, up_grad, down_grad, out_grad), "blk"
        )
    small = small[:, 0]
    shard = lambda values: lax.dynamic_slice_in_dim(values, mp * columns, columns, 0)
    at = lambda start, count: lax.dynamic_slice_in_dim(small, start, count, 0)
    return (
        mixed,
        stream_grad,
        shard(small[0]),
        qkv_grad,
        at(8 + 2 * mp, 2)[:, :columns],
        out_grad,
        small[2],
        shard(small[1]),
        up_grad,
        at(4 + mp, 1)[0],
        down_grad,
        small[3],
    )


def solution(mesh):
    rows, mp_count = mesh.shape["dp"], mesh.shape["mp"]
    pairs = Mesh(mesh.devices.reshape(rows // 8, 4, 2, mp_count), ALL)
    return jax.shard_map(
        local,
        mesh=pairs,
        in_specs=(
            P("mp", ROWS),
            P(ROWS, None),
            P("mp", ROWS),
            P("mp"),
            P(None, "mp", None),
            P(None, "mp"),
            P("mp", None),
            P(),
            P("mp"),
            P(None, "mp"),
            P("mp"),
            P("mp", None),
            P(),
        ),
        out_specs=(
            P("mp", ROWS),
            P("mp", ROWS),
            P("mp"),
            P(None, "mp", None),
            P(None, "mp"),
            P("mp", None),
            P(),
            P("mp"),
            P(None, "mp"),
            P("mp"),
            P("mp", None),
            P(),
        ),
        check_vma=False,
    )
```
